128 devices in a mesh: rep: 16 (over y_hi, x, core), shard: 8 (over z, y_lo).
Axes of the slice: x: 4, y: 4 (y_hi: 2, y_lo: 2; y = y_hi * 2 + y_lo), z: 4, core: 2. Of those that a mesh axis runs over, the one named last changes fastest.
Arguments:
- layer_in: float32 [32768, 1024], P(('rep', 'shard')), may hold values from -6 to 6
- cotangent: float32 [32768, 1024], P(('rep', 'shard')), may hold values from -6 to 6
- seq_lengths: int32 [128, 2], P(('rep', 'shard')), may hold values from 1 to 192, 256 in all within a row
- norm_gain: float32 [1024], P('shard'), may hold values from 0.5 to 1.5
- in_weight: bfloat16 [1024, 4384], P('shard'), may hold values from -0.1875 to 0.1875
- conv_weight: float32 [2304, 4], P('shard'), may hold values from -3 to 3
- conv_bias: float32 [2304], P('shard'), may hold values from -0.5 to 0.5
- step_bias: float32 [32], P('shard'), may hold values from -6.9 to -2.3
- decay_log: float32 [32], P('shard'), may hold values from 0 to 2.77
- skip_gain: float32 [32], P('shard'), may hold values from 0.5 to 1.5
- gate_gain: float32 [2048], P('shard'), may hold values from 0.5 to 1.5
- out_weight: bfloat16 [2048, 1024], P('shard'), may hold values from -0.125 to 0.125
Outputs:
- layer_out: float32 [32768, 1024], P(('rep', 'shard'))
- input_grad: float32 [32768, 1024], P(('rep', 'shard'))
- norm_gain_grad: float32 [1024], P('shard')
- in_weight_grad: float32 [1024, 4384], P('shard')
- conv_weight_grad: float32 [2304, 4], P('shard')
- conv_bias_grad: float32 [2304], P('shard')
- step_bias_grad: float32 [32], P('shard')
- decay_log_grad: float32 [32], P('shard')
- skip_gain_grad: float32 [32], P('shard')
- gate_gain_grad: float32 [2048], P('shard')
- out_weight_grad: float32 [2048, 1024], P('shard')
The draws below stay inside these ranges and needn't reach their ends.
Inputs may be any that keep to these rules, and one draw needn't show every extreme that they name: `seq_lengths`: each device's row of 2 lengths sums to 256.
All inputs are finite; a program needn't handle non-finite values.
Results may differ from the reference program's by a relative error of at most 0.0064.
Values may be sent and summed in bfloat16 or wider, within the bound.
No kernel may reach another device: no remote copies, remote signals or barrier semaphores. Data moves between devices by JAX's collectives and lax.ppermute only.
A program may use at most 128 MiB of HBM per device.

```python
import math
import jax
import jax.numpy as jnp
import numpy as np
from jax import lax

D = 1024
D_INNER = 2048
HEADS = 32
CONV = 4
SPAN = 256
TOK_DEV = 256
SEQ_DEV = 2
CONV_CH = 2304
PROJ = 4384
TOKENS = 32768
N_REP = 16
N_SHARD = 8


def block_scale(rng, dims, split, least, top_value):
    level = 1.0
    for position, shards_of in split:
        steps = jax.random.uniform(jax.random.fold_in(jax.random.fold_in(rng, 6), position), (shards_of,), jnp.float32, least / len(split), top_value / len(split))
        level = level * jnp.repeat(jnp.exp(steps), dims[position] // shards_of).reshape((-1,) + (1,) * (len(dims) - 1 - position))
    return level


def split_up(number_of, total, limit, skew):
    weights = [(1 << 20) // math.isqrt(grade ** skew) + 1 for grade in range(2, number_of + 1)]
    spare, given = total - limit - (number_of - 1), [1] * (number_of - 1)
    while spare > 0:
        candidates = [i for i in range(number_of - 1) if given[i] < limit]
        whole, budget = sum([weights[i] for i in candidates]), spare
        for i in candidates:
            extra = min(limit - given[i], max(1, budget * weights[i] // whole), spare)
            given[i] = given[i] + extra
            spare = spare - extra
    return np.array([limit] + given)


def uneven(own_key, amount, total, most, skew):
    if amount == 2:
        one = jax.random.randint(own_key, (), max(1, total - most), min(most, total - 1) + 1)
        return jnp.stack([one, total - one])
    tallies = jnp.asarray(split_up(amount, total, most, skew), jnp.int32)
    twos = (amount - 1) // 2
    source_of, receiver = tallies[1:1 + 2 * twos:2], tallies[2:2 + 2 * twos:2]
    room = jnp.minimum(source_of - 1, most - receiver)
    passed = jax.random.randint(jax.random.fold_in(own_key, 1), (twos,), 0, 1 << 20) % (room + 1)
    tallies = tallies.at[1:1 + 2 * twos:2].set(source_of - passed).at[2:2 + 2 * twos:2].set(receiver + passed)
    return tallies[jax.random.permutation(jax.random.fold_in(own_key, 2), amount)]


def normal_values(stream_key, extent, scale, most, shards=(), kind=jnp.bfloat16):
    loudness = block_scale(stream_key, extent, shards, -0.22, 0.18) if shards else 1.0
    result = jax.random.normal(stream_key, extent, jnp.float32) * scale * loudness
    return jnp.minimum(jnp.maximum(result, -most), most).astype(kind)


def setup_inputs(seed: int = 0) -> dict:
    splits = jax.random.split(jax.random.key(seed), 13)
    layer_in = normal_values(splits[0], (TOKENS, D), 1.0, 6.0, ((0, 128),), jnp.float32)
    cotangent = normal_values(splits[1], (TOKENS, D), 1.0, 6.0, ((0, 128),), jnp.float32)
    seq_lengths = jax.vmap(lambda own: uneven(own, SEQ_DEV, TOK_DEV, 3 * TOK_DEV // 4, 2))(jax.random.split(splits[2], (N_REP * N_SHARD))).reshape((N_REP * N_SHARD, SEQ_DEV)).astype(jnp.int32)
    norm_gain = jnp.clip(1.0 + 0.1 * jax.random.normal(splits[3], (D,), jnp.float32), 0.5, 1.5)
    in_weight = normal_values(splits[4], (D, PROJ), D ** -0.5, 0.1875, ((0, 8),))
    conv_weight = normal_values(splits[5], (CONV_CH, CONV), CONV ** -0.5, 3.0, ((0, 8),), jnp.float32)
    conv_bias = jnp.clip(jax.random.uniform(splits[6], (CONV_CH,), jnp.float32, -0.5, 0.5) * block_scale(splits[6], (CONV_CH,), ((0, 8),), -0.4, 0.0), -0.5, 0.5)
    step_bias = jnp.clip(-6.9 + 4.6000001430511475 * jax.random.uniform(splits[7], (HEADS,), jnp.float32) ** block_scale(splits[7], (HEADS,), ((0, 8),), -0.2, 0.2), -6.9, -2.3)
    decay_log = jnp.clip(2.77 * jax.random.uniform(splits[8], (HEADS,), jnp.float32) ** block_scale(splits[8], (HEADS,), ((0, 8),), -0.2, 0.2), 0.0, 2.77)
    skip_gain = jnp.clip(0.5 + 1.0 * jax.random.uniform(splits[9], (HEADS,), jnp.float32) ** block_scale(splits[9], (HEADS,), ((0, 8),), -0.2, 0.2), 0.5, 1.5)
    gate_gain = jnp.clip(1.0 + 0.1 * jax.random.normal(splits[10], (D_INNER,), jnp.float32), 0.5, 1.5)
    out_weight = normal_values(splits[11], (D_INNER, D), D_INNER ** -0.5, 0.125, ((0, 8),))
    return {"layer_in": layer_in, "cotangent": cotangent, "seq_lengths": seq_lengths, "norm_gain": norm_gain, "in_weight": in_weight, "conv_weight": conv_weight, "conv_bias": conv_bias, "step_bias": step_bias, "decay_log": decay_log, "skip_gain": skip_gain, "gate_gain": gate_gain, "out_weight": out_weight}


EPS = 1e-05
HIGH = lax.Precision.HIGHEST

def shifted(values, lag):
    zeros_top = jnp.zeros((lag,) + values.shape[1:], values.dtype)
    return jnp.concatenate([zeros_top, values[:-lag]], axis=0)

def segment_ids(lengths_row, count):
    offsets = jnp.cumsum(lengths_row, dtype=jnp.int32) - lengths_row
    places = jnp.arange(count, dtype=jnp.int32)
    return lax.optimization_barrier(jnp.sum((places[:, None] >= offsets[None, :]).astype(jnp.int32), axis=1, dtype=jnp.int32)) - 1

def row_product(left, right):
    return lax.dot_general(left, right, (((0,), (0,)), ((), ())), preferred_element_type=jnp.float32)

def norm_input(inputs, gain_one):
    scaling = lax.rsqrt(lax.optimization_barrier(jnp.mean(inputs * inputs, axis=1, keepdims=True)) + EPS)
    return inputs * scaling * gain_one[None, :]

def mixer(projected, segment, conv_weight, conv_bias, step_bias, decay_log, skip_gain, gate_gain):
    count = projected.shape[0]
    inner = gate_gain.shape[0]
    heads = step_bias.shape[0]
    head_dim = inner // heads
    channels = conv_weight.shape[0]
    state_dim = (channels - inner) // 2
    taps = conv_weight.shape[1]
    gate_part = projected[:, :inner]
    conv_in = projected[:, inner:inner + channels]
    step_raw = projected[:, inner + channels:]
    places = jnp.arange(count, dtype=jnp.int32)
    conv_out = conv_bias[None, :] + conv_weight[:, taps - 1][None, :] * conv_in
    for lag in range(1, taps):
        same = (shifted(segment, lag) == segment) & (places >= lag)
        conv_out = conv_out + jnp.where(same[:, None], conv_weight[:, taps - 1 - lag][None, :] * shifted(conv_in, lag), 0.0)
    activated = jax.nn.silu(conv_out)
    values = activated[:, :inner].reshape(count, heads, head_dim)
    b_matrix = activated[:, inner:inner + state_dim]
    c_matrix = activated[:, inner + state_dim:]
    step_size = jax.nn.softplus(step_raw + step_bias[None, :])
    decay = -jnp.exp(decay_log)[None, :] * step_size
    blocks = count // SPAN
    values_c = values.reshape(blocks, SPAN, heads, head_dim)
    b_spans = b_matrix.reshape(blocks, SPAN, state_dim)
    c_spans = c_matrix.reshape(blocks, SPAN, state_dim)
    step_c = step_size.reshape(blocks, SPAN, heads)
    cumul = jnp.cumsum(decay.reshape(blocks, SPAN, heads), axis=1)
    seg_c = segment.reshape(blocks, SPAN)
    rows_in = jnp.arange(SPAN, dtype=jnp.int32)
    lower = rows_in[:, None] >= rows_in[None, :]
    allowed = lower[None] & (seg_c[:, :, None] == seg_c[:, None, :])
    cumul_t = jnp.transpose(cumul, (0, 2, 1))
    differ = cumul_t[:, :, :, None] - cumul_t[:, :, None, :]
    weights_l = jnp.exp(jnp.where(allowed[:, None], differ, -10000.0))
    scores = jnp.einsum('cin,cjn->cij', c_spans, b_spans, precision=HIGH)
    mixing = weights_l * scores[:, None]
    scaled_in = values_c * step_c[..., None]
    y_intra = jnp.einsum('chij,cjhp->cihp', mixing, scaled_in, precision=HIGH)
    last_seg = seg_c[:, -1]
    tails = jnp.exp(cumul[:, -1:, :] - cumul) * (seg_c == last_seg[:, None]).astype(jnp.float32)[..., None]
    local_states = jnp.einsum('cjhp,cjn->chpn', scaled_in * tails[..., None], b_spans, precision=HIGH)
    carried = jnp.zeros((heads, head_dim, state_dim), jnp.float32)
    before_seg = jnp.int32(-1)
    pieces = []
    for block_index in range(blocks):
        linked = (seg_c[block_index] == before_seg).astype(jnp.float32)
        reach = jnp.exp(cumul[block_index]) * linked[:, None]
        inter = jnp.einsum('in,hpn->ihp', c_spans[block_index], carried, precision=HIGH) * reach[:, :, None]
        pieces.append(y_intra[block_index] + inter)
        wholly = last_seg[block_index] == before_seg
        carried = local_states[block_index] + jnp.where(wholly, jnp.exp(cumul[block_index, -1])[:, None, None] * carried, 0.0)
        before_seg = last_seg[block_index]
    y_all = jnp.concatenate(pieces, axis=0) + skip_gain[None, :, None] * values
    gated_pre = y_all.reshape(count, inner) * jax.nn.silu(gate_part)
    scaling = lax.rsqrt(lax.optimization_barrier(jnp.mean(gated_pre * gated_pre, axis=1, keepdims=True)) + EPS)
    return gated_pre * scaling * gate_gain[None, :]

def reference(layer_in, cotangent, seq_lengths, norm_gain, in_weight, conv_weight, conv_bias, step_bias, decay_log, skip_gain, gate_gain, out_weight):
    blocks_all = seq_lengths.shape[0]
    per_block = layer_in.shape[0] // blocks_all
    width = layer_in.shape[1]
    inputs_b = layer_in.reshape(blocks_all, per_block, width)
    cot_b = cotangent.reshape(blocks_all, per_block, width)

    def one_block(carry, items):
        block_in, block_cot, block_len = items
        segment = segment_ids(block_len, per_block)
        normed_f, norm_back = jax.vjp(norm_input, block_in, norm_gain)
        normed = normed_f.astype(jnp.bfloat16)
        projected = jnp.dot(normed, in_weight, preferred_element_type=jnp.float32)

        def bound_mixer(proj_arg, cw_arg, cb_arg, sb_arg, dl_arg, sk_arg, gg_arg):
            return mixer(proj_arg, segment, cw_arg, cb_arg, sb_arg, dl_arg, sk_arg, gg_arg)
        gated_f, mixer_back = jax.vjp(bound_mixer, projected, conv_weight, conv_bias, step_bias, decay_log, skip_gain, gate_gain)
        gated = gated_f.astype(jnp.bfloat16)
        block_out = block_in + jnp.dot(gated, out_weight, preferred_element_type=jnp.float32)
        cot_low = block_cot.astype(jnp.bfloat16)
        grad_out_w = row_product(gated, cot_low)
        gated_grad = lax.dot_general(cot_low, out_weight, (((1,), (1,)), ((), ())), preferred_element_type=jnp.float32)
        proj_grad, g_cw, g_cb, g_sb, g_dl, g_sk, g_gg = mixer_back(gated_grad)
        proj_low = proj_grad.astype(jnp.bfloat16)
        grad_in_w = row_product(normed, proj_low)
        normed_grad = lax.dot_general(proj_low, in_weight, (((1,), (1,)), ((), ())), preferred_element_type=jnp.float32)
        back_in, g_norm = norm_back(normed_grad)
        block_grad = block_cot + back_in
        updates = (g_norm, grad_in_w, g_cw, g_cb, g_sb, g_dl, g_sk, g_gg, grad_out_w)
        carry = tuple((old + new for old, new in zip(carry, updates)))
        return (carry, (block_out, block_grad))
    start_carry = (jnp.zeros(norm_gain.shape, jnp.float32), jnp.zeros(in_weight.shape, jnp.float32), jnp.zeros(conv_weight.shape, jnp.float32), jnp.zeros(conv_bias.shape, jnp.float32), jnp.zeros(step_bias.shape, jnp.float32), jnp.zeros(decay_log.shape, jnp.float32), jnp.zeros(skip_gain.shape, jnp.float32), jnp.zeros(gate_gain.shape, jnp.float32), jnp.zeros(out_weight.shape, jnp.float32))
    totals, outputs = lax.scan(one_block, start_carry, (inputs_b, cot_b, seq_lengths))
    layer_out = outputs[0].reshape(blocks_all * per_block, width)
    input_grad = outputs[1].reshape(blocks_all * per_block, width)
    return (layer_out, input_grad, totals[0], totals[1], totals[2], totals[3], totals[4], totals[5], totals[6], totals[7], totals[8])
```

```python
import math

import jax
import jax.numpy as jnp
from jax import lax
from jax.sharding import Mesh
from jax.sharding import PartitionSpec as P

SPAN = 256
SHARD = ("shard_0", "shard_1")
REP = ("rep_hi", "core")
REP_SHARD = ("rep_hi", "core", "shard_0", "shard_1")
ALL = REP_SHARD


EPS = 1e-05
HIGH = lax.Precision.HIGHEST


def side_by_side(arrays, axis, dim, along):
    widths = [math.prod(a.shape[along:]) for a in arrays]
    both = jnp.concatenate(
        [a.reshape(*a.shape[:along], w) for a, w in zip(arrays, widths)], axis=along
    )
    result = lax.all_gather(both, axis, axis=dim, tiled=True)
    blocks = jnp.split(result, [sum(widths[:k]) for k in range(1, len(widths))], axis=along)
    return tuple(
        (b.reshape(*result.shape[:along], *a.shape[along:]) for a, b in zip(arrays, blocks))
    )


def sum_by_axis(total, axes):
    for axis in axes:
        total = lax.psum_scatter(total, axis, scatter_dimension=0, tiled=True)
    return total


def in_blocks(shard, dim, size):
    before, after = (shard.shape[:dim], shard.shape[dim + 1 :])
    return jnp.moveaxis(shard.reshape(*before, size, -1, *after), dim, 0)


def sum_at_owner(shard, axis, dim):
    size = lax.axis_size(axis)
    blocks = lax.all_to_all(in_blocks(shard, dim, size), axis, 0, 0, tiled=True)
    return jnp.sum(blocks, axis=0)


def sent_together(arrays, axis, dim, along):
    widths = [math.prod(a.shape[along:]) for a in arrays]
    both = jnp.concatenate(
        [a.reshape(*a.shape[:along], w) for a, w in zip(arrays, widths)], axis=along
    )
    result = sum_at_owner(both, axis, dim)
    blocks = jnp.split(result, [sum(widths[:k]) for k in range(1, len(widths))], axis=along)
    return tuple(
        (b.reshape(*result.shape[:along], *a.shape[along:]) for a, b in zip(arrays, blocks))
    )


def shifted(values, lag):
    zeros_top = jnp.zeros((lag,) + values.shape[1:], values.dtype)
    return jnp.concatenate([zeros_top, values[:-lag]], axis=0)


def segment_ids(lengths_row, count):
    offsets = jnp.cumsum(lengths_row, dtype=jnp.int32) - lengths_row
    places = jnp.arange(count, dtype=jnp.int32)
    return (
        jnp.sum((places[:, None] >= offsets[None, :]).astype(jnp.int32), axis=1, dtype=jnp.int32)
        - 1
    )


def row_product(left, right):
    return lax.dot_general(
        left, right, (((0,), (0,)), ((), ())), preferred_element_type=jnp.float32
    )


def back_product(left, right):
    return lax.dot_general(
        left, right, (((1,), (1,)), ((), ())), preferred_element_type=jnp.float32
    )


def norm_input(inputs, gain_one):
    scaling = lax.rsqrt(jnp.mean(inputs * inputs, axis=1, keepdims=True) + EPS)
    return inputs * scaling * gain_one[None, :]


def mixer(projected, segment, conv_weight, conv_bias, step_bias, decay_log, skip_gain, gate_gain):
    count = projected.shape[0]
    inner = gate_gain.shape[0]
    heads = step_bias.shape[0]
    head_dim = inner // heads
    channels = conv_weight.shape[0]
    state_dim = (channels - inner) // 2
    taps = conv_weight.shape[1]
    gate_part = projected[:, :inner]
    conv_in = projected[:, inner : inner + channels]
    step_raw = projected[:, inner + channels :]
    places = jnp.arange(count, dtype=jnp.int32)
    conv_out = conv_bias[None, :] + conv_weight[:, taps - 1][None, :] * conv_in
    for lag in range(1, taps):
        same = (shifted(segment, lag) == segment) & (places >= lag)
        conv_out = conv_out + jnp.where(
            same[:, None], conv_weight[:, taps - 1 - lag][None, :] * shifted(conv_in, lag), 0.0
        )
    activated = jax.nn.silu(conv_out)
    values = activated[:, :inner].reshape(count, heads, head_dim)
    b_matrix = activated[:, inner : inner + state_dim]
    c_matrix = activated[:, inner + state_dim :]
    step_size = jax.nn.softplus(step_raw + step_bias[None, :])
    decay = -jnp.exp(decay_log)[None, :] * step_size
    blocks = count // SPAN
    values_c = values.reshape(blocks, SPAN, heads, head_dim)
    b_spans = b_matrix.reshape(blocks, SPAN, state_dim)
    c_spans = c_matrix.reshape(blocks, SPAN, state_dim)
    step_c = step_size.reshape(blocks, SPAN, heads)
    cumul = jnp.cumsum(decay.reshape(blocks, SPAN, heads), axis=1)
    seg_c = segment.reshape(blocks, SPAN)
    rows_in = jnp.arange(SPAN, dtype=jnp.int32)
    lower = rows_in[:, None] >= rows_in[None, :]
    allowed = lower[None] & (seg_c[:, :, None] == seg_c[:, None, :])
    cumul_t = jnp.transpose(cumul, (0, 2, 1))
    differ = cumul_t[:, :, :, None] - cumul_t[:, :, None, :]
    weights_l = jnp.exp(jnp.where(allowed[:, None], differ, -10000.0))
    scores = jnp.einsum("cin,cjn->cij", c_spans, b_spans, precision=HIGH)
    mixing = weights_l * scores[:, None]
    scaled_in = values_c * step_c[..., None]
    y_intra = jnp.einsum("chij,cjhp->cihp", mixing, scaled_in, precision=HIGH)
    carried = jnp.zeros((heads, head_dim, state_dim), jnp.float32)
    before_seg = jnp.int32(-1)
    linked = (seg_c[0] == before_seg).astype(jnp.float32)
    reach = jnp.exp(cumul[0]) * linked[:, None]
    inter = jnp.einsum("in,hpn->ihp", c_spans[0], carried, precision=HIGH) * reach[:, :, None]
    pieces = [y_intra[0] + inter]
    y_all = jnp.concatenate(pieces, axis=0) + skip_gain[None, :, None] * values
    gated_pre = y_all.reshape(count, inner) * jax.nn.silu(gate_part)
    scaling = lax.rsqrt(jnp.mean(gated_pre * gated_pre, axis=1, keepdims=True) + EPS)
    return gated_pre * scaling * gate_gain[None, :]


def gather_rows(weight):
    rows = weight.shape[0]
    half = rows // 2
    core = lax.axis_index("core")
    mine = lax.dynamic_slice_in_dim(weight, core * half, half, axis=0)
    part = lax.all_gather(mine, SHARD, axis=0, tiled=False)
    both = lax.all_gather(part, "core", axis=1, tiled=False)
    return both.reshape(-1, weight.shape[1])


def reduce_rows(partial):
    groups = lax.axis_size(SHARD)
    cols = partial.shape[1]
    blocks = partial.reshape(groups, 2, -1, cols)
    halves = lax.psum_scatter(blocks, "core", scatter_dimension=1, tiled=False)
    owned = lax.psum_scatter(halves, SHARD, scatter_dimension=0, tiled=False)
    owned = lax.psum(owned, "rep_hi")
    return lax.all_gather(owned, "core", axis=0, tiled=True)


def on_device(
    layer_in,
    cotangent,
    seq_lengths,
    norm_gain,
    in_weight,
    conv_weight,
    conv_bias,
    step_bias,
    decay_log,
    skip_gain,
    gate_gain,
    out_weight,
):
    count = layer_in.shape[0]
    groups = lax.axis_size(SHARD)
    segment = segment_ids(seq_lengths[0], count)
    smalls = (norm_gain, conv_weight, conv_bias, step_bias, decay_log, skip_gain, gate_gain)
    flat = jnp.concatenate([a.reshape(-1) for a in smalls])
    flat_all = lax.all_gather(flat, SHARD, axis=0, tiled=False)
    pieces_full = []
    offset = 0
    for a in smalls:
        size = a.size
        block = flat_all[:, offset : offset + size]
        pieces_full.append(block.reshape((groups * a.shape[0],) + a.shape[1:]))
        offset += size
    norm_full, convw_full, convb_full, stepb_full, decay_full, skip_full, gategain_full = pieces_full
    normed_f, norm_back = jax.vjp(norm_input, layer_in, norm_full)
    normed = normed_f.astype(jnp.bfloat16)
    in_whole = gather_rows(in_weight)
    out_whole = gather_rows(out_weight)
    projected = jnp.dot(normed, in_whole, preferred_element_type=jnp.float32)

    def bound_mixer(proj_arg, cw_arg, cb_arg, sb_arg, dl_arg, sk_arg, gg_arg):
        return mixer(proj_arg, segment, cw_arg, cb_arg, sb_arg, dl_arg, sk_arg, gg_arg)

    gated_f, mixer_back = jax.vjp(
        bound_mixer,
        projected,
        convw_full,
        convb_full,
        stepb_full,
        decay_full,
        skip_full,
        gategain_full,
    )
    gated = gated_f.astype(jnp.bfloat16)
    branch_out = jnp.dot(gated, out_whole, preferred_element_type=jnp.float32)
    layer_out = layer_in + branch_out
    cot_low = cotangent.astype(jnp.bfloat16)
    out_owned = reduce_rows(row_product(gated, cot_low))
    gated_grad = back_product(cot_low, out_whole)
    proj_grad, g_convw, g_convb, g_stepb, g_decay, g_skip, g_gategain = mixer_back(gated_grad)
    proj_low = proj_grad.astype(jnp.bfloat16)
    cols = proj_low.shape[1]
    wide = -(-cols // 128) * 128
    proj_wide = jnp.pad(proj_low, ((0, 0), (0, wide - cols)))
    in_owned = reduce_rows(row_product(normed, proj_wide))[:, :cols]
    normed_grad = back_product(proj_low, in_whole)
    back_in, g_norm = norm_back(normed_grad)
    input_grad = cotangent + back_in
    grads = (g_norm, g_convw, g_convb, g_stepb, g_decay, g_skip, g_gategain)
    small_blocks = jnp.concatenate([g.reshape(groups, -1) for g in grads], axis=1)
    small_sum = lax.psum(small_blocks, ALL)
    mine = lax.dynamic_index_in_dim(small_sum, lax.axis_index(SHARD), axis=0, keepdims=False)
    small_final = []
    offset = 0
    for g in grads:
        size = g.size // groups
        small_final.append(mine[offset : offset + size].reshape((g.shape[0] // groups,) + g.shape[1:]))
        offset += size
    return (
        layer_out,
        input_grad,
        small_final[0],
        in_owned,
        small_final[1],
        small_final[2],
        small_final[3],
        small_final[4],
        small_final[5],
        small_final[6],
        out_owned,
    )


def solution(mesh):
    split = Mesh(
        mesh.devices.reshape(mesh.shape["rep"] // 2, 2, 4, 2),
        ("rep_hi", "core", "shard_0", "shard_1"),
    )
    in_specs = (
        P(REP_SHARD, None),
        P(REP_SHARD, None),
        P(REP_SHARD, None),
        P(SHARD),
        P(SHARD, None),
        P(SHARD, None),
        P(SHARD),
        P(SHARD),
        P(SHARD),
        P(SHARD),
        P(SHARD),
        P(SHARD, None),
    )
    out_specs = (
        P(REP_SHARD, None),
        P(REP_SHARD, None),
        P(SHARD),
        P(SHARD, None),
        P(SHARD, None),
        P(SHARD),
        P(SHARD),
        P(SHARD),
        P(SHARD),
        P(SHARD),
        P(SHARD, None),
    )
    return jax.shard_map(
        on_device, mesh=split, in_specs=in_specs, out_specs=out_specs, check_vma=False
    )
```

```python
import math

import jax
import jax.numpy as jnp
from jax import lax
from jax.sharding import Mesh
from jax.sharding import PartitionSpec as P

SPAN = 256
SHARD = ("shard_0", "shard_1")
REP = ("rep_hi", "core")
REP_SHARD = ("rep_hi", "core", "shard_0", "shard_1")
ALL = REP_SHARD


EPS = 1e-05
HIGH = lax.Precision.HIGHEST


def side_by_side(arrays, axis, dim, along):
    widths = [math.prod(a.shape[along:]) for a in arrays]
    both = jnp.concatenate(
        [a.reshape(*a.shape[:along], w) for a, w in zip(arrays, widths)], axis=along
    )
    result = lax.all_gather(both, axis, axis=dim, tiled=True)
    blocks = jnp.split(result, [sum(widths[:k]) for k in range(1, len(widths))], axis=along)
    return tuple(
        (b.reshape(*result.shape[:along], *a.shape[along:]) for a, b in zip(arrays, blocks))
    )


def sum_by_axis(total, axes):
    for axis in axes:
        total = lax.psum_scatter(total, axis, scatter_dimension=0, tiled=True)
    return total


def in_blocks(shard, dim, size):
    before, after = (shard.shape[:dim], shard.shape[dim + 1 :])
    return jnp.moveaxis(shard.reshape(*before, size, -1, *after), dim, 0)


def sum_at_owner(shard, axis, dim):
    size = lax.axis_size(axis)
    blocks = lax.all_to_all(in_blocks(shard, dim, size), axis, 0, 0, tiled=True)
    return jnp.sum(blocks, axis=0)


def sent_together(arrays, axis, dim, along):
    widths = [math.prod(a.shape[along:]) for a in arrays]
    both = jnp.concatenate(
        [a.reshape(*a.shape[:along], w) for a, w in zip(arrays, widths)], axis=along
    )
    result = sum_at_owner(both, axis, dim)
    blocks = jnp.split(result, [sum(widths[:k]) for k in range(1, len(widths))], axis=along)
    return tuple(
        (b.reshape(*result.shape[:along], *a.shape[along:]) for a, b in zip(arrays, blocks))
    )


def shifted(values, lag):
    zeros_top = jnp.zeros((lag,) + values.shape[1:], values.dtype)
    return jnp.concatenate([zeros_top, values[:-lag]], axis=0)


def segment_ids(lengths_row, count):
    offsets = jnp.cumsum(lengths_row, dtype=jnp.int32) - lengths_row
    places = jnp.arange(count, dtype=jnp.int32)
    return (
        jnp.sum((places[:, None] >= offsets[None, :]).astype(jnp.int32), axis=1, dtype=jnp.int32)
        - 1
    )


def row_product(left, right):
    return lax.dot_general(
        left, right, (((0,), (0,)), ((), ())), preferred_element_type=jnp.float32
    )


def back_product(left, right):
    return lax.dot_general(
        left, right, (((1,), (1,)), ((), ())), preferred_element_type=jnp.float32
    )


def norm_input(inputs, gain_one):
    scaling = lax.rsqrt(jnp.mean(inputs * inputs, axis=1, keepdims=True) + EPS)
    return inputs * scaling * gain_one[None, :]


def mixer(projected, segment, conv_weight, conv_bias, step_bias, decay_log, skip_gain, gate_gain):
    count = projected.shape[0]
    inner = gate_gain.shape[0]
    heads = step_bias.shape[0]
    head_dim = inner // heads
    channels = conv_weight.shape[0]
    state_dim = (channels - inner) // 2
    taps = conv_weight.shape[1]
    gate_part = projected[:, :inner]
    conv_in = projected[:, inner : inner + channels]
    step_raw = projected[:, inner + channels :]
    places = jnp.arange(count, dtype=jnp.int32)
    conv_out = conv_bias[None, :] + conv_weight[:, taps - 1][None, :] * conv_in
    for lag in range(1, taps):
        same = (shifted(segment, lag) == segment) & (places >= lag)
        conv_out = conv_out + jnp.where(
            same[:, None], conv_weight[:, taps - 1 - lag][None, :] * shifted(conv_in, lag), 0.0
        )
    activated = jax.nn.silu(conv_out)
    values = activated[:, :inner].reshape(count, heads, head_dim)
    b_matrix = activated[:, inner : inner + state_dim]
    c_matrix = activated[:, inner + state_dim :]
    step_size = jax.nn.softplus(step_raw + step_bias[None, :])
    decay = -jnp.exp(decay_log)[None, :] * step_size
    blocks = count // SPAN
    values_c = values.reshape(blocks, SPAN, heads, head_dim)
    b_spans = b_matrix.reshape(blocks, SPAN, state_dim)
    c_spans = c_matrix.reshape(blocks, SPAN, state_dim)
    step_c = step_size.reshape(blocks, SPAN, heads)
    cumul = jnp.cumsum(decay.reshape(blocks, SPAN, heads), axis=1)
    seg_c = segment.reshape(blocks, SPAN)
    rows_in = jnp.arange(SPAN, dtype=jnp.int32)
    lower = rows_in[:, None] >= rows_in[None, :]
    allowed = lower[None] & (seg_c[:, :, None] == seg_c[:, None, :])
    cumul_t = jnp.transpose(cumul, (0, 2, 1))
    differ = cumul_t[:, :, :, None] - cumul_t[:, :, None, :]
    weights_l = jnp.exp(jnp.where(allowed[:, None], differ, -10000.0))
    scores = jnp.einsum("cin,cjn->cij", c_spans, b_spans, precision=HIGH)
    mixing = weights_l * scores[:, None]
    scaled_in = values_c * step_c[..., None]
    y_intra = jnp.einsum("chij,cjhp->cihp", mixing, scaled_in, precision=HIGH)
    carried = jnp.zeros((heads, head_dim, state_dim), jnp.float32)
    before_seg = jnp.int32(-1)
    linked = (seg_c[0] == before_seg).astype(jnp.float32)
    reach = jnp.exp(cumul[0]) * linked[:, None]
    inter = jnp.einsum("in,hpn->ihp", c_spans[0], carried, precision=HIGH) * reach[:, :, None]
    pieces = [y_intra[0] + inter]
    y_all = jnp.concatenate(pieces, axis=0) + skip_gain[None, :, None] * values
    gated_pre = y_all.reshape(count, inner) * jax.nn.silu(gate_part)
    scaling = lax.rsqrt(jnp.mean(gated_pre * gated_pre, axis=1, keepdims=True) + EPS)
    return gated_pre * scaling * gate_gain[None, :]


def gather_rows(weight):
    rows = weight.shape[0]
    half = rows // 2
    core = lax.axis_index("core")
    mine = lax.dynamic_slice_in_dim(weight, core * half, half, axis=0)
    part = lax.all_gather(mine, SHARD, axis=0, tiled=False)
    both = lax.all_gather(part, "core", axis=1, tiled=False)
    return both.reshape(-1, weight.shape[1])


def reduce_rows(partial, extra=None, at=None):
    groups = lax.axis_size(SHARD)
    cols = partial.shape[1]
    blocks = partial.reshape(groups, 2, -1, cols)
    if extra is not None:
        width = extra.shape[1]
        pad_cols = cols - at
        extra_rows = -(-width // pad_cols)
        extra = jnp.pad(extra, ((0, 0), (0, extra_rows * pad_cols - width)))
        extra = extra.reshape(groups, 1, extra_rows, pad_cols)
        blocks = lax.dynamic_update_slice(blocks, extra, (0, 0, 0, cols - pad_cols))
    halves = lax.psum_scatter(blocks, "core", scatter_dimension=1, tiled=False)
    owned = lax.psum_scatter(halves.astype(jnp.bfloat16), SHARD, scatter_dimension=0, tiled=False)
    owned = owned.astype(jnp.float32)
    if extra is not None:
        small = halves[:, :extra_rows, cols - pad_cols :]
        small = lax.psum_scatter(small, SHARD, scatter_dimension=0, tiled=False)
        owned, small = lax.psum((owned, small), "rep_hi")
        owned = lax.dynamic_update_slice(owned, small, (0, cols - pad_cols))
    else:
        owned = lax.psum(owned, "rep_hi")
    whole = lax.all_gather(owned, "core", axis=0, tiled=True)
    if extra is None:
        return whole
    small = whole[:extra_rows, cols - pad_cols :].reshape(-1)[:width]
    return whole, small


def on_device(
    layer_in,
    cotangent,
    seq_lengths,
    norm_gain,
    in_weight,
    conv_weight,
    conv_bias,
    step_bias,
    decay_log,
    skip_gain,
    gate_gain,
    out_weight,
):
    count = layer_in.shape[0]
    groups = lax.axis_size(SHARD)
    segment = segment_ids(seq_lengths[0], count)
    smalls = (norm_gain, conv_weight, conv_bias, step_bias, decay_log, skip_gain, gate_gain)
    flat = jnp.concatenate([a.reshape(-1) for a in smalls])
    flat_len = flat.shape[0]
    tile_rows = -(-flat_len // 1024) * 8
    flat = jnp.pad(flat, (0, tile_rows * 128 - flat_len)).reshape(tile_rows, 128)
    flat_all = lax.all_gather(flat, SHARD, axis=0, tiled=False)
    flat_all = flat_all.reshape(groups, -1)[:, :flat_len]
    pieces_full = []
    offset = 0
    for a in smalls:
        size = a.size
        block = flat_all[:, offset : offset + size]
        pieces_full.append(block.reshape((groups * a.shape[0],) + a.shape[1:]))
        offset += size
    norm_full, convw_full, convb_full, stepb_full, decay_full, skip_full, gategain_full = pieces_full
    normed_f, norm_back = jax.vjp(norm_input, layer_in, norm_full)
    normed = normed_f.astype(jnp.bfloat16)
    in_whole = gather_rows(in_weight)
    out_whole = gather_rows(out_weight)
    projected = jnp.dot(normed, in_whole, preferred_element_type=jnp.float32)

    def bound_mixer(proj_arg, cw_arg, cb_arg, sb_arg, dl_arg, sk_arg, gg_arg):
        return mixer(proj_arg, segment, cw_arg, cb_arg, sb_arg, dl_arg, sk_arg, gg_arg)

    gated_f, mixer_back = jax.vjp(
        bound_mixer,
        projected,
        convw_full,
        convb_full,
        stepb_full,
        decay_full,
        skip_full,
        gategain_full,
    )
    gated = gated_f.astype(jnp.bfloat16)
    branch_out = jnp.dot(gated, out_whole, preferred_element_type=jnp.float32)
    layer_out = layer_in + branch_out
    cot_low = cotangent.astype(jnp.bfloat16)
    out_owned = reduce_rows(row_product(gated, cot_low))
    gated_grad = back_product(cot_low, out_whole)
    proj_grad, g_convw, g_convb, g_stepb, g_decay, g_skip, g_gategain = mixer_back(gated_grad)
    proj_low = proj_grad.astype(jnp.bfloat16)
    normed_grad = back_product(proj_low, in_whole)
    back_in, g_norm = norm_back(normed_grad)
    input_grad = cotangent + back_in
    grads = (g_norm, g_convw, g_convb, g_stepb, g_decay, g_skip, g_gategain)
    small_blocks = jnp.concatenate([g.reshape(groups, -1) for g in grads], axis=1)
    cols = proj_low.shape[1]
    wide = -(-cols // 128) * 128
    proj_wide = jnp.pad(proj_low, ((0, 0), (0, wide - cols)))
    in_wide, mine = reduce_rows(row_product(normed, proj_wide), small_blocks, cols)
    in_owned = in_wide[:, :cols]
    small_final = []
    offset = 0
    for g in grads:
        size = g.size // groups
        small_final.append(mine[offset : offset + size].reshape((g.shape[0] // groups,) + g.shape[1:]))
        offset += size
    return (
        layer_out,
        input_grad,
        small_final[0],
        in_owned,
        small_final[1],
        small_final[2],
        small_final[3],
        small_final[4],
        small_final[5],
        small_final[6],
        out_owned,
    )


def solution(mesh):
    split = Mesh(
        mesh.devices.reshape(mesh.shape["rep"] // 2, 2, 4, 2),
        ("rep_hi", "core", "shard_0", "shard_1"),
    )
    in_specs = (
        P(REP_SHARD, None),
        P(REP_SHARD, None),
        P(REP_SHARD, None),
        P(SHARD),
        P(SHARD, None),
        P(SHARD, None),
        P(SHARD),
        P(SHARD),
        P(SHARD),
        P(SHARD),
        P(SHARD),
        P(SHARD, None),
    )
    out_specs = (
        P(REP_SHARD, None),
        P(REP_SHARD, None),
        P(SHARD),
        P(SHARD, None),
        P(SHARD, None),
        P(SHARD),
        P(SHARD),
        P(SHARD),
        P(SHARD),
        P(SHARD),
        P(SHARD, None),
    )
    return jax.shard_map(
        on_device, mesh=split, in_specs=in_specs, out_specs=out_specs, check_vma=False
    )
```

```python
import math

import jax
import jax.numpy as jnp
from jax import lax
from jax.sharding import Mesh
from jax.sharding import PartitionSpec as P

SPAN = 256
SHARD = ("shard_0", "shard_1")
REP = ("rep_hi", "core")
REP_SHARD = ("rep_hi", "core", "shard_0", "shard_1")
ALL = REP_SHARD


EPS = 1e-05
HIGH = lax.Precision.HIGHEST


def side_by_side(arrays, axis, dim, along):
    widths = [math.prod(a.shape[along:]) for a in arrays]
    both = jnp.concatenate(
        [a.reshape(*a.shape[:along], w) for a, w in zip(arrays, widths)], axis=along
    )
    result = lax.all_gather(both, axis, axis=dim, tiled=True)
    blocks = jnp.split(result, [sum(widths[:k]) for k in range(1, len(widths))], axis=along)
    return tuple(
        (b.reshape(*result.shape[:along], *a.shape[along:]) for a, b in zip(arrays, blocks))
    )


def sum_by_axis(total, axes):
    for axis in axes:
        total = lax.psum_scatter(total, axis, scatter_dimension=0, tiled=True)
    return total


def in_blocks(shard, dim, size):
    before, after = (shard.shape[:dim], shard.shape[dim + 1 :])
    return jnp.moveaxis(shard.reshape(*before, size, -1, *after), dim, 0)


def sum_at_owner(shard, axis, dim):
    size = lax.axis_size(axis)
    blocks = lax.all_to_all(in_blocks(shard, dim, size), axis, 0, 0, tiled=True)
    return jnp.sum(blocks, axis=0)


def sent_together(arrays, axis, dim, along):
    widths = [math.prod(a.shape[along:]) for a in arrays]
    both = jnp.concatenate(
        [a.reshape(*a.shape[:along], w) for a, w in zip(arrays, widths)], axis=along
    )
    result = sum_at_owner(both, axis, dim)
    blocks = jnp.split(result, [sum(widths[:k]) for k in range(1, len(widths))], axis=along)
    return tuple(
        (b.reshape(*result.shape[:along], *a.shape[along:]) for a, b in zip(arrays, blocks))
    )


def shifted(values, lag):
    zeros_top = jnp.zeros((lag,) + values.shape[1:], values.dtype)
    return jnp.concatenate([zeros_top, values[:-lag]], axis=0)


def segment_ids(lengths_row, count):
    offsets = jnp.cumsum(lengths_row, dtype=jnp.int32) - lengths_row
    places = jnp.arange(count, dtype=jnp.int32)
    return (
        jnp.sum((places[:, None] >= offsets[None, :]).astype(jnp.int32), axis=1, dtype=jnp.int32)
        - 1
    )


def row_product(left, right):
    return lax.dot_general(
        left, right, (((0,), (0,)), ((), ())), preferred_element_type=jnp.float32
    )


def back_product(left, right):
    return lax.dot_general(
        left, right, (((1,), (1,)), ((), ())), preferred_element_type=jnp.float32
    )


def norm_input(inputs, gain_one):
    scaling = lax.rsqrt(jnp.mean(inputs * inputs, axis=1, keepdims=True) + EPS)
    return inputs * scaling * gain_one[None, :]


def mixer(projected, segment, conv_weight, conv_bias, step_bias, decay_log, skip_gain, gate_gain):
    count = projected.shape[0]
    inner = gate_gain.shape[0]
    heads = step_bias.shape[0]
    head_dim = inner // heads
    channels = conv_weight.shape[0]
    state_dim = (channels - inner) // 2
    taps = conv_weight.shape[1]
    gate_part = projected[:, :inner]
    conv_in = projected[:, inner : inner + channels]
    step_raw = projected[:, inner + channels :]
    places = jnp.arange(count, dtype=jnp.int32)
    conv_out = conv_bias[None, :] + conv_weight[:, taps - 1][None, :] * conv_in
    for lag in range(1, taps):
        same = (shifted(segment, lag) == segment) & (places >= lag)
        conv_out = conv_out + jnp.where(
            same[:, None], conv_weight[:, taps - 1 - lag][None, :] * shifted(conv_in, lag), 0.0
        )
    activated = jax.nn.silu(conv_out)
    values = activated[:, :inner].reshape(count, heads, head_dim)
    b_matrix = activated[:, inner : inner + state_dim]
    c_matrix = activated[:, inner + state_dim :]
    step_size = jax.nn.softplus(step_raw + step_bias[None, :])
    decay = -jnp.exp(decay_log)[None, :] * step_size
    blocks = count // SPAN
    values_c = values.reshape(blocks, SPAN, heads, head_dim)
    b_spans = b_matrix.reshape(blocks, SPAN, state_dim)
    c_spans = c_matrix.reshape(blocks, SPAN, state_dim)
    step_c = step_size.reshape(blocks, SPAN, heads)
    cumul = jnp.cumsum(decay.reshape(blocks, SPAN, heads), axis=1)
    seg_c = segment.reshape(blocks, SPAN)
    rows_in = jnp.arange(SPAN, dtype=jnp.int32)
    lower = rows_in[:, None] >= rows_in[None, :]
    allowed = lower[None] & (seg_c[:, :, None] == seg_c[:, None, :])
    cumul_t = jnp.transpose(cumul, (0, 2, 1))
    differ = cumul_t[:, :, :, None] - cumul_t[:, :, None, :]
    weights_l = jnp.exp(jnp.where(allowed[:, None], differ, -10000.0))
    scores = jnp.einsum("cin,cjn->cij", c_spans, b_spans, precision=HIGH)
    mixing = weights_l * scores[:, None]
    scaled_in = values_c * step_c[..., None]
    y_intra = jnp.einsum("chij,cjhp->cihp", mixing, scaled_in, precision=HIGH)
    carried = jnp.zeros((heads, head_dim, state_dim), jnp.float32)
    before_seg = jnp.int32(-1)
    linked = (seg_c[0] == before_seg).astype(jnp.float32)
    reach = jnp.exp(cumul[0]) * linked[:, None]
    inter = jnp.einsum("in,hpn->ihp", c_spans[0], carried, precision=HIGH) * reach[:, :, None]
    pieces = [y_intra[0] + inter]
    y_all = jnp.concatenate(pieces, axis=0) + skip_gain[None, :, None] * values
    gated_pre = y_all.reshape(count, inner) * jax.nn.silu(gate_part)
    scaling = lax.rsqrt(jnp.mean(gated_pre * gated_pre, axis=1, keepdims=True) + EPS)
    return gated_pre * scaling * gate_gain[None, :]


def gather_rows(weight):
    rows = weight.shape[0]
    half = rows // 2
    core = lax.axis_index("core")
    mine = lax.dynamic_slice_in_dim(weight, core * half, half, axis=0)
    part = lax.all_gather(mine, SHARD, axis=0, tiled=False)
    both = lax.all_gather(part, "core", axis=1, tiled=False)
    return both.reshape(-1, weight.shape[1])


def reduce_rows(partial):
    groups = lax.axis_size(SHARD)
    cols = partial.shape[1]
    blocks = partial.reshape(groups, 2, -1, cols)
    halves = lax.psum_scatter(blocks, "core", scatter_dimension=1, tiled=False)
    owned = lax.psum_scatter(halves.astype(jnp.bfloat16), SHARD, scatter_dimension=0, tiled=False)
    owned = lax.psum(owned.astype(jnp.float32), "rep_hi")
    return lax.all_gather(owned, "core", axis=0, tiled=True)


def exchange_sum(values, axes):
    for axis in axes:
        size = lax.axis_size(axis)
        step = 1
        while step < size:
            pairs = [(i, i ^ step) for i in range(size)]
            values = values + lax.ppermute(values, axis, pairs)
            step *= 2
    return values


def on_device(
    layer_in,
    cotangent,
    seq_lengths,
    norm_gain,
    in_weight,
    conv_weight,
    conv_bias,
    step_bias,
    decay_log,
    skip_gain,
    gate_gain,
    out_weight,
):
    count = layer_in.shape[0]
    groups = lax.axis_size(SHARD)
    segment = segment_ids(seq_lengths[0], count)
    smalls = (norm_gain, conv_weight, conv_bias, step_bias, decay_log, skip_gain, gate_gain)
    flat = jnp.concatenate([a.reshape(-1) for a in smalls])
    flat_len = flat.shape[0]
    place = lax.axis_index(SHARD)
    spread = jnp.where(
        (jnp.arange(groups, dtype=jnp.int32) == place)[:, None], flat[None, :], 0.0
    )
    flat_all = exchange_sum(spread, ("shard_1", "shard_0"))
    pieces_full = []
    offset = 0
    for a in smalls:
        size = a.size
        block = flat_all[:, offset : offset + size]
        pieces_full.append(block.reshape((groups * a.shape[0],) + a.shape[1:]))
        offset += size
    norm_full, convw_full, convb_full, stepb_full, decay_full, skip_full, gategain_full = pieces_full
    normed_f, norm_back = jax.vjp(norm_input, layer_in, norm_full)
    normed = normed_f.astype(jnp.bfloat16)
    in_whole = gather_rows(in_weight)
    in_whole, out_weight = lax.optimization_barrier((in_whole, out_weight))
    out_whole = gather_rows(out_weight)
    projected = jnp.dot(normed, in_whole, preferred_element_type=jnp.float32)

    def bound_mixer(proj_arg, cw_arg, cb_arg, sb_arg, dl_arg, sk_arg, gg_arg):
        return mixer(proj_arg, segment, cw_arg, cb_arg, sb_arg, dl_arg, sk_arg, gg_arg)

    gated_f, mixer_back = jax.vjp(
        bound_mixer,
        projected,
        convw_full,
        convb_full,
        stepb_full,
        decay_full,
        skip_full,
        gategain_full,
    )
    gated = gated_f.astype(jnp.bfloat16)
    branch_out = jnp.dot(gated, out_whole, preferred_element_type=jnp.float32)
    layer_out = layer_in + branch_out
    cot_low = cotangent.astype(jnp.bfloat16)
    out_owned = reduce_rows(row_product(gated, cot_low))
    gated_grad = back_product(cot_low, out_whole)
    proj_grad, g_convw, g_convb, g_stepb, g_decay, g_skip, g_gategain = mixer_back(gated_grad)
    proj_low = proj_grad.astype(jnp.bfloat16)
    normed_grad = back_product(proj_low, in_whole)
    back_in, g_norm = norm_back(normed_grad)
    input_grad = cotangent + back_in
    grads = (g_norm, g_convw, g_convb, g_stepb, g_decay, g_skip, g_gategain)
    small_blocks = jnp.concatenate([g.reshape(groups, -1) for g in grads], axis=1)
    cols = proj_low.shape[1]
    wide = -(-cols // 128) * 128
    proj_wide = jnp.pad(proj_low, ((0, 0), (0, wide - cols)))
    in_owned = reduce_rows(row_product(normed, proj_wide))[:, :cols]
    small_sum = exchange_sum(small_blocks, ("shard_1", "shard_0", "core", "rep_hi"))
    mine = lax.dynamic_index_in_dim(small_sum, lax.axis_index(SHARD), axis=0, keepdims=False)
    small_final = []
    offset = 0
    for g in grads:
        size = g.size // groups
        small_final.append(mine[offset : offset + size].reshape((g.shape[0] // groups,) + g.shape[1:]))
        offset += size
    return (
        layer_out,
        input_grad,
        small_final[0],
        in_owned,
        small_final[1],
        small_final[2],
        small_final[3],
        small_final[4],
        small_final[5],
        small_final[6],
        out_owned,
    )


def solution(mesh):
    split = Mesh(
        mesh.devices.reshape(mesh.shape["rep"] // 2, 2, 4, 2),
        ("rep_hi", "core", "shard_0", "shard_1"),
    )
    in_specs = (
        P(REP_SHARD, None),
        P(REP_SHARD, None),
        P(REP_SHARD, None),
        P(SHARD),
        P(SHARD, None),
        P(SHARD, None),
        P(SHARD),
        P(SHARD),
        P(SHARD),
        P(SHARD),
        P(SHARD),
        P(SHARD, None),
    )
    out_specs = (
        P(REP_SHARD, None),
        P(REP_SHARD, None),
        P(SHARD),
        P(SHARD, None),
        P(SHARD, None),
        P(SHARD),
        P(SHARD),
        P(SHARD),
        P(SHARD),
        P(SHARD),
        P(SHARD, None),
    )
    return jax.shard_map(
        on_device, mesh=split, in_specs=in_specs, out_specs=out_specs, check_vma=False
    )
```

```python
import math

import jax
import jax.numpy as jnp
from jax import lax
from jax.sharding import Mesh
from jax.sharding import PartitionSpec as P

SPAN = 256
SHARD = ("shard_0", "shard_1")
REP = ("rep_hi", "core")
REP_SHARD = ("rep_hi", "core", "shard_0", "shard_1")
ALL = REP_SHARD


EPS = 1e-05
HIGH = lax.Precision.HIGHEST


def side_by_side(arrays, axis, dim, along):
    widths = [math.prod(a.shape[along:]) for a in arrays]
    both = jnp.concatenate(
        [a.reshape(*a.shape[:along], w) for a, w in zip(arrays, widths)], axis=along
    )
    result = lax.all_gather(both, axis, axis=dim, tiled=True)
    blocks = jnp.split(result, [sum(widths[:k]) for k in range(1, len(widths))], axis=along)
    return tuple(
        (b.reshape(*result.shape[:along], *a.shape[along:]) for a, b in zip(arrays, blocks))
    )


def sum_by_axis(total, axes):
    for axis in axes:
        total = lax.psum_scatter(total, axis, scatter_dimension=0, tiled=True)
    return total


def in_blocks(shard, dim, size):
    before, after = (shard.shape[:dim], shard.shape[dim + 1 :])
    return jnp.moveaxis(shard.reshape(*before, size, -1, *after), dim, 0)


def sum_at_owner(shard, axis, dim):
    size = lax.axis_size(axis)
    blocks = lax.all_to_all(in_blocks(shard, dim, size), axis, 0, 0, tiled=True)
    return jnp.sum(blocks, axis=0)


def sent_together(arrays, axis, dim, along):
    widths = [math.prod(a.shape[along:]) for a in arrays]
    both = jnp.concatenate(
        [a.reshape(*a.shape[:along], w) for a, w in zip(arrays, widths)], axis=along
    )
    result = sum_at_owner(both, axis, dim)
    blocks = jnp.split(result, [sum(widths[:k]) for k in range(1, len(widths))], axis=along)
    return tuple(
        (b.reshape(*result.shape[:along], *a.shape[along:]) for a, b in zip(arrays, blocks))
    )


def shifted(values, lag):
    zeros_top = jnp.zeros((lag,) + values.shape[1:], values.dtype)
    return jnp.concatenate([zeros_top, values[:-lag]], axis=0)


def segment_ids(lengths_row, count):
    offsets = jnp.cumsum(lengths_row, dtype=jnp.int32) - lengths_row
    places = jnp.arange(count, dtype=jnp.int32)
    return (
        jnp.sum((places[:, None] >= offsets[None, :]).astype(jnp.int32), axis=1, dtype=jnp.int32)
        - 1
    )


def row_product(left, right):
    return lax.dot_general(
        left, right, (((0,), (0,)), ((), ())), preferred_element_type=jnp.float32
    )


def back_product(left, right):
    return lax.dot_general(
        left, right, (((1,), (1,)), ((), ())), preferred_element_type=jnp.float32
    )


def norm_input(inputs, gain_one):
    scaling = lax.rsqrt(jnp.mean(inputs * inputs, axis=1, keepdims=True) + EPS)
    return inputs * scaling * gain_one[None, :]


def mixer(projected, segment, conv_weight, conv_bias, step_bias, decay_log, skip_gain, gate_gain):
    count = projected.shape[0]
    inner = gate_gain.shape[0]
    heads = step_bias.shape[0]
    head_dim = inner // heads
    channels = conv_weight.shape[0]
    state_dim = (channels - inner) // 2
    taps = conv_weight.shape[1]
    gate_part = projected[:, :inner]
    conv_in = projected[:, inner : inner + channels]
    step_raw = projected[:, inner + channels :]
    places = jnp.arange(count, dtype=jnp.int32)
    conv_out = conv_bias[None, :] + conv_weight[:, taps - 1][None, :] * conv_in
    for lag in range(1, taps):
        same = (shifted(segment, lag) == segment) & (places >= lag)
        conv_out = conv_out + jnp.where(
            same[:, None], conv_weight[:, taps - 1 - lag][None, :] * shifted(conv_in, lag), 0.0
        )
    activated = jax.nn.silu(conv_out)
    values = activated[:, :inner].reshape(count, heads, head_dim)
    b_matrix = activated[:, inner : inner + state_dim]
    c_matrix = activated[:, inner + state_dim :]
    step_size = jax.nn.softplus(step_raw + step_bias[None, :])
    decay = -jnp.exp(decay_log)[None, :] * step_size
    blocks = count // SPAN
    values_c = values.reshape(blocks, SPAN, heads, head_dim)
    b_spans = b_matrix.reshape(blocks, SPAN, state_dim)
    c_spans = c_matrix.reshape(blocks, SPAN, state_dim)
    step_c = step_size.reshape(blocks, SPAN, heads)
    cumul = jnp.cumsum(decay.reshape(blocks, SPAN, heads), axis=1)
    seg_c = segment.reshape(blocks, SPAN)
    rows_in = jnp.arange(SPAN, dtype=jnp.int32)
    lower = rows_in[:, None] >= rows_in[None, :]
    allowed = lower[None] & (seg_c[:, :, None] == seg_c[:, None, :])
    cumul_t = jnp.transpose(cumul, (0, 2, 1))
    differ = cumul_t[:, :, :, None] - cumul_t[:, :, None, :]
    weights_l = jnp.exp(jnp.where(allowed[:, None], differ, -10000.0))
    scores = jnp.einsum("cin,cjn->cij", c_spans, b_spans, precision=HIGH)
    mixing = weights_l * scores[:, None]
    scaled_in = values_c * step_c[..., None]
    y_intra = jnp.einsum("chij,cjhp->cihp", mixing, scaled_in, precision=HIGH)
    carried = jnp.zeros((heads, head_dim, state_dim), jnp.float32)
    before_seg = jnp.int32(-1)
    linked = (seg_c[0] == before_seg).astype(jnp.float32)
    reach = jnp.exp(cumul[0]) * linked[:, None]
    inter = jnp.einsum("in,hpn->ihp", c_spans[0], carried, precision=HIGH) * reach[:, :, None]
    pieces = [y_intra[0] + inter]
    y_all = jnp.concatenate(pieces, axis=0) + skip_gain[None, :, None] * values
    gated_pre = y_all.reshape(count, inner) * jax.nn.silu(gate_part)
    scaling = lax.rsqrt(jnp.mean(gated_pre * gated_pre, axis=1, keepdims=True) + EPS)
    return gated_pre * scaling * gate_gain[None, :]


def core_swap(values):
    return lax.ppermute(values, "core", [(0, 1), (1, 0)])


def gather_rows(weight):
    rows = weight.shape[0]
    half = rows // 2
    core = lax.axis_index("core")
    mine = lax.dynamic_slice_in_dim(weight, core * half, half, axis=0)
    part = lax.all_gather(mine, SHARD, axis=0, tiled=False)
    other = core_swap(part)
    first = jnp.where(core == 0, part, other)
    second = jnp.where(core == 0, other, part)
    return jnp.stack([first, second], axis=1).reshape(-1, weight.shape[1])


def reduce_rows(partial):
    groups = lax.axis_size(SHARD)
    cols = partial.shape[1]
    core = lax.axis_index("core")
    blocks = partial.reshape(groups, 2, -1, cols)
    keep = jnp.where(core == 0, blocks[:, 0], blocks[:, 1])
    give = jnp.where(core == 0, blocks[:, 1], blocks[:, 0])
    halves = keep + core_swap(give)
    owned = lax.psum_scatter(halves.astype(jnp.bfloat16), SHARD, scatter_dimension=0, tiled=False)
    owned = lax.psum(owned.astype(jnp.float32), "rep_hi")
    other = core_swap(owned)
    first = jnp.where(core == 0, owned, other)
    second = jnp.where(core == 0, other, owned)
    return jnp.concatenate([first, second], axis=0)


def exchange_sum(values, axes):
    for axis in axes:
        size = lax.axis_size(axis)
        step = 1
        while step < size:
            pairs = [(i, i ^ step) for i in range(size)]
            values = values + lax.ppermute(values, axis, pairs)
            step *= 2
    return values


def on_device(
    layer_in,
    cotangent,
    seq_lengths,
    norm_gain,
    in_weight,
    conv_weight,
    conv_bias,
    step_bias,
    decay_log,
    skip_gain,
    gate_gain,
    out_weight,
):
    count = layer_in.shape[0]
    groups = lax.axis_size(SHARD)
    segment = segment_ids(seq_lengths[0], count)
    smalls = (norm_gain, conv_weight, conv_bias, step_bias, decay_log, skip_gain, gate_gain)
    flat = jnp.concatenate([a.reshape(-1) for a in smalls])
    flat_len = flat.shape[0]
    place = lax.axis_index(SHARD)
    spread = jnp.where(
        (jnp.arange(groups, dtype=jnp.int32) == place)[:, None], flat[None, :], 0.0
    )
    flat_all = exchange_sum(spread, ("shard_1", "shard_0"))
    pieces_full = []
    offset = 0
    for a in smalls:
        size = a.size
        block = flat_all[:, offset : offset + size]
        pieces_full.append(block.reshape((groups * a.shape[0],) + a.shape[1:]))
        offset += size
    norm_full, convw_full, convb_full, stepb_full, decay_full, skip_full, gategain_full = pieces_full
    normed_f, norm_back = jax.vjp(norm_input, layer_in, norm_full)
    normed = normed_f.astype(jnp.bfloat16)
    in_whole = gather_rows(in_weight)
    in_whole, out_weight = lax.optimization_barrier((in_whole, out_weight))
    out_whole = gather_rows(out_weight)
    projected = jnp.dot(normed, in_whole, preferred_element_type=jnp.float32)

    def bound_mixer(proj_arg, cw_arg, cb_arg, sb_arg, dl_arg, sk_arg, gg_arg):
        return mixer(proj_arg, segment, cw_arg, cb_arg, sb_arg, dl_arg, sk_arg, gg_arg)

    gated_f, mixer_back = jax.vjp(
        bound_mixer,
        projected,
        convw_full,
        convb_full,
        stepb_full,
        decay_full,
        skip_full,
        gategain_full,
    )
    gated = gated_f.astype(jnp.bfloat16)
    branch_out = jnp.dot(gated, out_whole, preferred_element_type=jnp.float32)
    layer_out = layer_in + branch_out
    cot_low = cotangent.astype(jnp.bfloat16)
    out_owned = reduce_rows(row_product(gated, cot_low))
    gated_grad = back_product(cot_low, out_whole)
    proj_grad, g_convw, g_convb, g_stepb, g_decay, g_skip, g_gategain = mixer_back(gated_grad)
    proj_low = proj_grad.astype(jnp.bfloat16)
    normed_grad = back_product(proj_low, in_whole)
    back_in, g_norm = norm_back(normed_grad)
    input_grad = cotangent + back_in
    grads = (g_norm, g_convw, g_convb, g_stepb, g_decay, g_skip, g_gategain)
    small_blocks = jnp.concatenate([g.reshape(groups, -1) for g in grads], axis=1)
    cols = proj_low.shape[1]
    wide = -(-cols // 128) * 128
    proj_wide = jnp.pad(proj_low, ((0, 0), (0, wide - cols)))
    in_owned = reduce_rows(row_product(normed, proj_wide))[:, :cols]
    small_sum = exchange_sum(small_blocks, ("shard_1", "shard_0", "core", "rep_hi"))
    mine = lax.dynamic_index_in_dim(small_sum, lax.axis_index(SHARD), axis=0, keepdims=False)
    small_final = []
    offset = 0
    for g in grads:
        size = g.size // groups
        small_final.append(mine[offset : offset + size].reshape((g.shape[0] // groups,) + g.shape[1:]))
        offset += size
    return (
        layer_out,
        input_grad,
        small_final[0],
        in_owned,
        small_final[1],
        small_final[2],
        small_final[3],
        small_final[4],
        small_final[5],
        small_final[6],
        out_owned,
    )


def solution(mesh):
    split = Mesh(
        mesh.devices.reshape(mesh.shape["rep"] // 2, 2, 4, 2),
        ("rep_hi", "core", "shard_0", "shard_1"),
    )
    in_specs = (
        P(REP_SHARD, None),
        P(REP_SHARD, None),
        P(REP_SHARD, None),
        P(SHARD),
        P(SHARD, None),
        P(SHARD, None),
        P(SHARD),
        P(SHARD),
        P(SHARD),
        P(SHARD),
        P(SHARD),
        P(SHARD, None),
    )
    out_specs = (
        P(REP_SHARD, None),
        P(REP_SHARD, None),
        P(SHARD),
        P(SHARD, None),
        P(SHARD, None),
        P(SHARD),
        P(SHARD),
        P(SHARD),
        P(SHARD),
        P(SHARD),
        P(SHARD, None),
    )
    return jax.shard_map(
        on_device, mesh=split, in_specs=in_specs, out_specs=out_specs, check_vma=False
    )
```

```python
import math

import jax
import jax.numpy as jnp
from jax import lax
from jax.sharding import Mesh
from jax.sharding import PartitionSpec as P

SPAN = 256
SHARD = ("shard_0", "shard_1")
REP = ("rep_hi", "core")
REP_SHARD = ("rep_hi", "core", "shard_0", "shard_1")
ALL = REP_SHARD


EPS = 1e-05
HIGH = lax.Precision.HIGHEST


def side_by_side(arrays, axis, dim, along):
    widths = [math.prod(a.shape[along:]) for a in arrays]
    both = jnp.concatenate(
        [a.reshape(*a.shape[:along], w) for a, w in zip(arrays, widths)], axis=along
    )
    result = lax.all_gather(both, axis, axis=dim, tiled=True)
    blocks = jnp.split(result, [sum(widths[:k]) for k in range(1, len(widths))], axis=along)
    return tuple(
        (b.reshape(*result.shape[:along], *a.shape[along:]) for a, b in zip(arrays, blocks))
    )


def sum_by_axis(total, axes):
    for axis in axes:
        total = lax.psum_scatter(total, axis, scatter_dimension=0, tiled=True)
    return total


def in_blocks(shard, dim, size):
    before, after = (shard.shape[:dim], shard.shape[dim + 1 :])
    return jnp.moveaxis(shard.reshape(*before, size, -1, *after), dim, 0)


def sum_at_owner(shard, axis, dim):
    size = lax.axis_size(axis)
    blocks = lax.all_to_all(in_blocks(shard, dim, size), axis, 0, 0, tiled=True)
    return jnp.sum(blocks, axis=0)


def sent_together(arrays, axis, dim, along):
    widths = [math.prod(a.shape[along:]) for a in arrays]
    both = jnp.concatenate(
        [a.reshape(*a.shape[:along], w) for a, w in zip(arrays, widths)], axis=along
    )
    result = sum_at_owner(both, axis, dim)
    blocks = jnp.split(result, [sum(widths[:k]) for k in range(1, len(widths))], axis=along)
    return tuple(
        (b.reshape(*result.shape[:along], *a.shape[along:]) for a, b in zip(arrays, blocks))
    )


def shifted(values, lag):
    zeros_top = jnp.zeros((lag,) + values.shape[1:], values.dtype)
    return jnp.concatenate([zeros_top, values[:-lag]], axis=0)


def segment_ids(lengths_row, count):
    offsets = jnp.cumsum(lengths_row, dtype=jnp.int32) - lengths_row
    places = jnp.arange(count, dtype=jnp.int32)
    return (
        jnp.sum((places[:, None] >= offsets[None, :]).astype(jnp.int32), axis=1, dtype=jnp.int32)
        - 1
    )


def row_product(left, right):
    return lax.dot_general(
        left, right, (((0,), (0,)), ((), ())), preferred_element_type=jnp.float32
    )


def back_product(left, right):
    return lax.dot_general(
        left, right, (((1,), (1,)), ((), ())), preferred_element_type=jnp.float32
    )


def norm_input(inputs, gain_one):
    scaling = lax.rsqrt(jnp.mean(inputs * inputs, axis=1, keepdims=True) + EPS)
    return inputs * scaling * gain_one[None, :]


def mixer(projected, segment, conv_weight, conv_bias, step_bias, decay_log, skip_gain, gate_gain):
    count = projected.shape[0]
    inner = gate_gain.shape[0]
    heads = step_bias.shape[0]
    head_dim = inner // heads
    channels = conv_weight.shape[0]
    state_dim = (channels - inner) // 2
    taps = conv_weight.shape[1]
    gate_part = projected[:, :inner]
    conv_in = projected[:, inner : inner + channels]
    step_raw = projected[:, inner + channels :]
    places = jnp.arange(count, dtype=jnp.int32)
    conv_out = conv_bias[None, :] + conv_weight[:, taps - 1][None, :] * conv_in
    for lag in range(1, taps):
        same = (shifted(segment, lag) == segment) & (places >= lag)
        conv_out = conv_out + jnp.where(
            same[:, None], conv_weight[:, taps - 1 - lag][None, :] * shifted(conv_in, lag), 0.0
        )
    activated = jax.nn.silu(conv_out)
    values = activated[:, :inner].reshape(count, heads, head_dim)
    b_matrix = activated[:, inner : inner + state_dim]
    c_matrix = activated[:, inner + state_dim :]
    step_size = jax.nn.softplus(step_raw + step_bias[None, :])
    decay = -jnp.exp(decay_log)[None, :] * step_size
    blocks = count // SPAN
    values_c = values.reshape(blocks, SPAN, heads, head_dim)
    b_spans = b_matrix.reshape(blocks, SPAN, state_dim)
    c_spans = c_matrix.reshape(blocks, SPAN, state_dim)
    step_c = step_size.reshape(blocks, SPAN, heads)
    cumul = jnp.cumsum(decay.reshape(blocks, SPAN, heads), axis=1)
    seg_c = segment.reshape(blocks, SPAN)
    rows_in = jnp.arange(SPAN, dtype=jnp.int32)
    lower = rows_in[:, None] >= rows_in[None, :]
    allowed = lower[None] & (seg_c[:, :, None] == seg_c[:, None, :])
    cumul_t = jnp.transpose(cumul, (0, 2, 1))
    differ = cumul_t[:, :, :, None] - cumul_t[:, :, None, :]
    weights_l = jnp.exp(jnp.where(allowed[:, None], differ, -10000.0))
    scores = jnp.einsum("cin,cjn->cij", c_spans, b_spans, precision=HIGH)
    mixing = weights_l * scores[:, None]
    scaled_in = values_c * step_c[..., None]
    y_intra = jnp.einsum("chij,cjhp->cihp", mixing, scaled_in, precision=HIGH)
    carried = jnp.zeros((heads, head_dim, state_dim), jnp.float32)
    before_seg = jnp.int32(-1)
    linked = (seg_c[0] == before_seg).astype(jnp.float32)
    reach = jnp.exp(cumul[0]) * linked[:, None]
    inter = jnp.einsum("in,hpn->ihp", c_spans[0], carried, precision=HIGH) * reach[:, :, None]
    pieces = [y_intra[0] + inter]
    y_all = jnp.concatenate(pieces, axis=0) + skip_gain[None, :, None] * values
    gated_pre = y_all.reshape(count, inner) * jax.nn.silu(gate_part)
    scaling = lax.rsqrt(jnp.mean(gated_pre * gated_pre, axis=1, keepdims=True) + EPS)
    return gated_pre * scaling * gate_gain[None, :]


def core_swap(values):
    return lax.ppermute(values, "core", [(0, 1), (1, 0)])


def gather_group(block):
    ring = lax.axis_size("shard_0")
    y = lax.axis_index("shard_1")
    z = lax.axis_index("shard_0")
    other_y = lax.ppermute(block, "shard_1", [(0, 1), (1, 0)])
    pair = jnp.where(y == 0, jnp.stack([block, other_y]), jnp.stack([other_y, block]))
    up = [(i, (i + 1) % ring) for i in range(ring)]
    down = [(i, (i - 1) % ring) for i in range(ring)]
    from_prev = lax.ppermute(pair, "shard_0", up)
    from_next = lax.ppermute(pair, "shard_0", down)
    half = block.shape[0] // 2
    far_a = lax.ppermute(from_prev[:, :half], "shard_0", up)
    far_b = lax.ppermute(from_next[:, half:], "shard_0", down)
    opposite = jnp.concatenate([far_a, far_b], axis=1)
    ordered = jnp.stack([pair, from_next, opposite, from_prev])
    doubled = jnp.concatenate([ordered, ordered], axis=0)
    start = (ring - z) % ring
    placed = lax.dynamic_slice_in_dim(doubled, start, ring, axis=0)
    return placed.reshape((ring * 2,) + block.shape)


def core_swap(values):
    return lax.ppermute(values, "core", [(0, 1), (1, 0)])


def gather_rows(weight, by_permutes=False):
    rows = weight.shape[0]
    half = rows // 2
    core = lax.axis_index("core")
    mine = lax.dynamic_slice_in_dim(weight, core * half, half, axis=0)
    if by_permutes:
        part = gather_group(mine)
    else:
        part = lax.all_gather(mine, SHARD, axis=0, tiled=False)
    other = core_swap(part)
    first = jnp.where(core == 0, part, other)
    second = jnp.where(core == 0, other, part)
    return jnp.stack([first, second], axis=1).reshape(-1, weight.shape[1])


def reduce_core(partial):
    groups = lax.axis_size(SHARD)
    cols = partial.shape[1]
    core = lax.axis_index("core")
    blocks = partial.reshape(groups, 2, -1, cols)
    keep = jnp.where(core == 0, blocks[:, 0], blocks[:, 1])
    give = jnp.where(core == 0, blocks[:, 1], blocks[:, 0])
    return keep + core_swap(give)


def reduce_rest(halves):
    core = lax.axis_index("core")
    owned = lax.psum_scatter(halves.astype(jnp.bfloat16), SHARD, scatter_dimension=0, tiled=False)
    owned = lax.psum(owned.astype(jnp.float32), "rep_hi")
    other = core_swap(owned)
    first = jnp.where(core == 0, owned, other)
    second = jnp.where(core == 0, other, owned)
    return jnp.concatenate([first, second], axis=0)


def reduce_rows(partial):
    return reduce_rest(reduce_core(partial))


def exchange_sum(values, axes):
    for axis in axes:
        size = lax.axis_size(axis)
        step = 1
        while step < size:
            pairs = [(i, i ^ step) for i in range(size)]
            values = values + lax.ppermute(values, axis, pairs)
            step *= 2
    return values


def on_device(
    layer_in,
    cotangent,
    seq_lengths,
    norm_gain,
    in_weight,
    conv_weight,
    conv_bias,
    step_bias,
    decay_log,
    skip_gain,
    gate_gain,
    out_weight,
):
    count = layer_in.shape[0]
    groups = lax.axis_size(SHARD)
    segment = segment_ids(seq_lengths[0], count)
    smalls = (norm_gain, conv_weight, conv_bias, step_bias, decay_log, skip_gain, gate_gain)
    flat = jnp.concatenate([a.reshape(-1) for a in smalls])
    flat_len = flat.shape[0]
    place = lax.axis_index(SHARD)
    spread = jnp.where(
        (jnp.arange(groups, dtype=jnp.int32) == place)[:, None], flat[None, :], 0.0
    )
    flat_all = exchange_sum(spread, ("shard_1", "shard_0"))
    pieces_full = []
    offset = 0
    for a in smalls:
        size = a.size
        block = flat_all[:, offset : offset + size]
        pieces_full.append(block.reshape((groups * a.shape[0],) + a.shape[1:]))
        offset += size
    norm_full, convw_full, convb_full, stepb_full, decay_full, skip_full, gategain_full = pieces_full
    normed_f, norm_back = jax.vjp(norm_input, layer_in, norm_full)
    normed = normed_f.astype(jnp.bfloat16)
    in_whole = gather_rows(in_weight, by_permutes=True)
    in_whole, out_weight = lax.optimization_barrier((in_whole, out_weight))
    out_whole = gather_rows(out_weight)
    projected = jnp.dot(normed, in_whole, preferred_element_type=jnp.float32)

    def bound_mixer(proj_arg, cw_arg, cb_arg, sb_arg, dl_arg, sk_arg, gg_arg):
        return mixer(proj_arg, segment, cw_arg, cb_arg, sb_arg, dl_arg, sk_arg, gg_arg)

    gated_f, mixer_back = jax.vjp(
        bound_mixer,
        projected,
        convw_full,
        convb_full,
        stepb_full,
        decay_full,
        skip_full,
        gategain_full,
    )
    gated = gated_f.astype(jnp.bfloat16)
    branch_out = jnp.dot(gated, out_whole, preferred_element_type=jnp.float32)
    layer_out = layer_in + branch_out
    cot_low = cotangent.astype(jnp.bfloat16)
    out_halves = reduce_core(row_product(gated, cot_low))
    gated_grad = back_product(cot_low, out_whole)
    out_halves, gated_grad = lax.optimization_barrier((out_halves, gated_grad))
    out_owned = reduce_rest(out_halves)
    proj_grad, g_convw, g_convb, g_stepb, g_decay, g_skip, g_gategain = mixer_back(gated_grad)
    proj_low = proj_grad.astype(jnp.bfloat16)
    normed_grad = back_product(proj_low, in_whole)
    back_in, g_norm = norm_back(normed_grad)
    input_grad = cotangent + back_in
    grads = (g_norm, g_convw, g_convb, g_stepb, g_decay, g_skip, g_gategain)
    small_blocks = jnp.concatenate([g.reshape(groups, -1) for g in grads], axis=1)
    cols = proj_low.shape[1]
    wide = -(-cols // 128) * 128
    proj_wide = jnp.pad(proj_low, ((0, 0), (0, wide - cols)))
    in_owned = reduce_rows(row_product(normed, proj_wide))[:, :cols]
    small_sum = exchange_sum(small_blocks, ("shard_1", "shard_0", "core", "rep_hi"))
    mine = lax.dynamic_index_in_dim(small_sum, lax.axis_index(SHARD), axis=0, keepdims=False)
    small_final = []
    offset = 0
    for g in grads:
        size = g.size // groups
        small_final.append(mine[offset : offset + size].reshape((g.shape[0] // groups,) + g.shape[1:]))
        offset += size
    return (
        layer_out,
        input_grad,
        small_final[0],
        in_owned,
        small_final[1],
        small_final[2],
        small_final[3],
        small_final[4],
        small_final[5],
        small_final[6],
        out_owned,
    )


def solution(mesh):
    split = Mesh(
        mesh.devices.reshape(mesh.shape["rep"] // 2, 2, 4, 2),
        ("rep_hi", "core", "shard_0", "shard_1"),
    )
    in_specs = (
        P(REP_SHARD, None),
        P(REP_SHARD, None),
        P(REP_SHARD, None),
        P(SHARD),
        P(SHARD, None),
        P(SHARD, None),
        P(SHARD),
        P(SHARD),
        P(SHARD),
        P(SHARD),
        P(SHARD),
        P(SHARD, None),
    )
    out_specs = (
        P(REP_SHARD, None),
        P(REP_SHARD, None),
        P(SHARD),
        P(SHARD, None),
        P(SHARD, None),
        P(SHARD),
        P(SHARD),
        P(SHARD),
        P(SHARD),
        P(SHARD),
        P(SHARD, None),
    )
    return jax.shard_map(
        on_device, mesh=split, in_specs=in_specs, out_specs=out_specs, check_vma=False
    )
```

```python
import math

import jax
import jax.numpy as jnp
from jax import lax
from jax.sharding import Mesh
from jax.sharding import PartitionSpec as P

SPAN = 256
SHARD = ("shard_0", "shard_1")
REP = ("rep_hi", "core")
REP_SHARD = ("rep_hi", "core", "shard_0", "shard_1")
ALL = REP_SHARD


EPS = 1e-05
HIGH = lax.Precision.HIGHEST


def side_by_side(arrays, axis, dim, along):
    widths = [math.prod(a.shape[along:]) for a in arrays]
    both = jnp.concatenate(
        [a.reshape(*a.shape[:along], w) for a, w in zip(arrays, widths)], axis=along
    )
    result = lax.all_gather(both, axis, axis=dim, tiled=True)
    blocks = jnp.split(result, [sum(widths[:k]) for k in range(1, len(widths))], axis=along)
    return tuple(
        (b.reshape(*result.shape[:along], *a.shape[along:]) for a, b in zip(arrays, blocks))
    )


def sum_by_axis(total, axes):
    for axis in axes:
        total = lax.psum_scatter(total, axis, scatter_dimension=0, tiled=True)
    return total


def in_blocks(shard, dim, size):
    before, after = (shard.shape[:dim], shard.shape[dim + 1 :])
    return jnp.moveaxis(shard.reshape(*before, size, -1, *after), dim, 0)


def sum_at_owner(shard, axis, dim):
    size = lax.axis_size(axis)
    blocks = lax.all_to_all(in_blocks(shard, dim, size), axis, 0, 0, tiled=True)
    return jnp.sum(blocks, axis=0)


def sent_together(arrays, axis, dim, along):
    widths = [math.prod(a.shape[along:]) for a in arrays]
    both = jnp.concatenate(
        [a.reshape(*a.shape[:along], w) for a, w in zip(arrays, widths)], axis=along
    )
    result = sum_at_owner(both, axis, dim)
    blocks = jnp.split(result, [sum(widths[:k]) for k in range(1, len(widths))], axis=along)
    return tuple(
        (b.reshape(*result.shape[:along], *a.shape[along:]) for a, b in zip(arrays, blocks))
    )


def shifted(values, lag):
    zeros_top = jnp.zeros((lag,) + values.shape[1:], values.dtype)
    return jnp.concatenate([zeros_top, values[:-lag]], axis=0)


def segment_ids(lengths_row, count):
    offsets = jnp.cumsum(lengths_row, dtype=jnp.int32) - lengths_row
    places = jnp.arange(count, dtype=jnp.int32)
    return (
        jnp.sum((places[:, None] >= offsets[None, :]).astype(jnp.int32), axis=1, dtype=jnp.int32)
        - 1
    )


def row_product(left, right):
    return lax.dot_general(
        left, right, (((0,), (0,)), ((), ())), preferred_element_type=jnp.float32
    )


def back_product(left, right):
    return lax.dot_general(
        left, right, (((1,), (1,)), ((), ())), preferred_element_type=jnp.float32
    )


def norm_input(inputs, gain_one):
    scaling = lax.rsqrt(jnp.mean(inputs * inputs, axis=1, keepdims=True) + EPS)
    return inputs * scaling * gain_one[None, :]


def mixer(projected, segment, conv_weight, conv_bias, step_bias, decay_log, skip_gain, gate_gain):
    count = projected.shape[0]
    inner = gate_gain.shape[0]
    heads = step_bias.shape[0]
    head_dim = inner // heads
    channels = conv_weight.shape[0]
    state_dim = (channels - inner) // 2
    taps = conv_weight.shape[1]
    gate_part = projected[:, :inner]
    conv_in = projected[:, inner : inner + channels]
    step_raw = projected[:, inner + channels :]
    places = jnp.arange(count, dtype=jnp.int32)
    conv_out = conv_bias[None, :] + conv_weight[:, taps - 1][None, :] * conv_in
    for lag in range(1, taps):
        same = (shifted(segment, lag) == segment) & (places >= lag)
        conv_out = conv_out + jnp.where(
            same[:, None], conv_weight[:, taps - 1 - lag][None, :] * shifted(conv_in, lag), 0.0
        )
    activated = jax.nn.silu(conv_out)
    values = activated[:, :inner].reshape(count, heads, head_dim)
    b_matrix = activated[:, inner : inner + state_dim]
    c_matrix = activated[:, inner + state_dim :]
    step_size = jax.nn.softplus(step_raw + step_bias[None, :])
    decay = -jnp.exp(decay_log)[None, :] * step_size
    blocks = count // SPAN
    values_c = values.reshape(blocks, SPAN, heads, head_dim)
    b_spans = b_matrix.reshape(blocks, SPAN, state_dim)
    c_spans = c_matrix.reshape(blocks, SPAN, state_dim)
    step_c = step_size.reshape(blocks, SPAN, heads)
    cumul = jnp.cumsum(decay.reshape(blocks, SPAN, heads), axis=1)
    seg_c = segment.reshape(blocks, SPAN)
    rows_in = jnp.arange(SPAN, dtype=jnp.int32)
    lower = rows_in[:, None] >= rows_in[None, :]
    allowed = lower[None] & (seg_c[:, :, None] == seg_c[:, None, :])
    cumul_t = jnp.transpose(cumul, (0, 2, 1))
    differ = cumul_t[:, :, :, None] - cumul_t[:, :, None, :]
    weights_l = jnp.exp(jnp.where(allowed[:, None], differ, -10000.0))
    scores = jnp.einsum("cin,cjn->cij", c_spans, b_spans, precision=HIGH)
    mixing = weights_l * scores[:, None]
    scaled_in = values_c * step_c[..., None]
    y_intra = jnp.einsum("chij,cjhp->cihp", mixing, scaled_in, precision=HIGH)
    carried = jnp.zeros((heads, head_dim, state_dim), jnp.float32)
    before_seg = jnp.int32(-1)
    linked = (seg_c[0] == before_seg).astype(jnp.float32)
    reach = jnp.exp(cumul[0]) * linked[:, None]
    inter = jnp.einsum("in,hpn->ihp", c_spans[0], carried, precision=HIGH) * reach[:, :, None]
    pieces = [y_intra[0] + inter]
    y_all = jnp.concatenate(pieces, axis=0) + skip_gain[None, :, None] * values
    gated_pre = y_all.reshape(count, inner) * jax.nn.silu(gate_part)
    scaling = lax.rsqrt(jnp.mean(gated_pre * gated_pre, axis=1, keepdims=True) + EPS)
    return gated_pre * scaling * gate_gain[None, :]


def reduce_group(halves):
    ring = lax.axis_size("shard_0")
    y = lax.axis_index("shard_1")
    z = lax.axis_index("shard_0")
    rows, cols = halves.shape[1], halves.shape[2]
    blocks = halves.reshape(ring, 2, rows, cols)
    doubled = jnp.concatenate([blocks, blocks], axis=0)
    rel = lax.dynamic_slice_in_dim(doubled, z, ring, axis=0)
    up = [(i, (i + 1) % ring) for i in range(ring)]
    down = [(i, (i - 1) % ring) for i in range(ring)]
    half = rows // 2
    low = lambda a: a.astype(jnp.bfloat16)
    acc_up = lax.ppermute(low(rel[3][:, :half]), "shard_0", up)
    acc_dn = lax.ppermute(low(rel[1][:, half:]), "shard_0", down)
    acc_up = lax.ppermute(low(acc_up + rel[2][:, :half]), "shard_0", up)
    acc_dn = lax.ppermute(low(acc_dn + rel[2][:, half:]), "shard_0", down)
    acc_up = lax.ppermute(low(acc_up + rel[1][:, :half]), "shard_0", up)
    acc_dn = lax.ppermute(low(acc_dn + rel[3][:, half:]), "shard_0", down)
    zsum = jnp.concatenate(
        [acc_up.astype(jnp.float32) + rel[0][:, :half], acc_dn.astype(jnp.float32) + rel[0][:, half:]],
        axis=1,
    )
    keep = lax.dynamic_index_in_dim(zsum, y, axis=0, keepdims=False)
    give = lax.dynamic_index_in_dim(zsum, 1 - y, axis=0, keepdims=False)
    return keep + lax.ppermute(low(give), "shard_1", [(0, 1), (1, 0)]).astype(jnp.float32)


def core_swap(values):
    return lax.ppermute(values, "core", [(0, 1), (1, 0)])


def gather_group(block):
    ring = lax.axis_size("shard_0")
    y = lax.axis_index("shard_1")
    z = lax.axis_index("shard_0")
    other_y = lax.ppermute(block, "shard_1", [(0, 1), (1, 0)])
    pair = jnp.where(y == 0, jnp.stack([block, other_y]), jnp.stack([other_y, block]))
    up = [(i, (i + 1) % ring) for i in range(ring)]
    down = [(i, (i - 1) % ring) for i in range(ring)]
    from_prev = lax.ppermute(pair, "shard_0", up)
    from_next = lax.ppermute(pair, "shard_0", down)
    half = block.shape[0] // 2
    far_a = lax.ppermute(from_prev[:, :half], "shard_0", up)
    far_b = lax.ppermute(from_next[:, half:], "shard_0", down)
    opposite = jnp.concatenate([far_a, far_b], axis=1)
    ordered = jnp.stack([pair, from_next, opposite, from_prev])
    doubled = jnp.concatenate([ordered, ordered], axis=0)
    start = (ring - z) % ring
    placed = lax.dynamic_slice_in_dim(doubled, start, ring, axis=0)
    return placed.reshape((ring * 2,) + block.shape)


def core_swap(values):
    return lax.ppermute(values, "core", [(0, 1), (1, 0)])


def gather_rows(weight, by_permutes=False):
    rows = weight.shape[0]
    half = rows // 2
    core = lax.axis_index("core")
    mine = lax.dynamic_slice_in_dim(weight, core * half, half, axis=0)
    if by_permutes:
        part = gather_group(mine)
    else:
        part = lax.all_gather(mine, SHARD, axis=0, tiled=False)
    other = core_swap(part)
    first = jnp.where(core == 0, part, other)
    second = jnp.where(core == 0, other, part)
    return jnp.stack([first, second], axis=1).reshape(-1, weight.shape[1])


def reduce_core(partial):
    groups = lax.axis_size(SHARD)
    cols = partial.shape[1]
    core = lax.axis_index("core")
    blocks = partial.reshape(groups, 2, -1, cols)
    keep = jnp.where(core == 0, blocks[:, 0], blocks[:, 1])
    give = jnp.where(core == 0, blocks[:, 1], blocks[:, 0])
    return keep + core_swap(give)


def reduce_rest(halves, wait_for=None):
    core = lax.axis_index("core")
    owned = reduce_group(halves)
    if wait_for is not None:
        owned, wait_for = lax.optimization_barrier((owned, wait_for))
    owned = lax.psum(owned, "rep_hi")
    other = core_swap(owned)
    first = jnp.where(core == 0, owned, other)
    second = jnp.where(core == 0, other, owned)
    return jnp.concatenate([first, second], axis=0)


def reduce_rows(partial, wait_for=None):
    return reduce_rest(reduce_core(partial), wait_for)


def exchange_sum(values, axes):
    for axis in axes:
        size = lax.axis_size(axis)
        step = 1
        while step < size:
            pairs = [(i, i ^ step) for i in range(size)]
            values = values + lax.ppermute(values, axis, pairs)
            step *= 2
    return values


def on_device(
    layer_in,
    cotangent,
    seq_lengths,
    norm_gain,
    in_weight,
    conv_weight,
    conv_bias,
    step_bias,
    decay_log,
    skip_gain,
    gate_gain,
    out_weight,
):
    count = layer_in.shape[0]
    groups = lax.axis_size(SHARD)
    segment = segment_ids(seq_lengths[0], count)
    smalls = (norm_gain, conv_weight, conv_bias, step_bias, decay_log, skip_gain, gate_gain)
    flat = jnp.concatenate([a.reshape(-1) for a in smalls])
    flat_len = flat.shape[0]
    place = lax.axis_index(SHARD)
    spread = jnp.where(
        (jnp.arange(groups, dtype=jnp.int32) == place)[:, None], flat[None, :], 0.0
    )
    flat_all = exchange_sum(spread, ("shard_1", "shard_0"))
    pieces_full = []
    offset = 0
    for a in smalls:
        size = a.size
        block = flat_all[:, offset : offset + size]
        pieces_full.append(block.reshape((groups * a.shape[0],) + a.shape[1:]))
        offset += size
    norm_full, convw_full, convb_full, stepb_full, decay_full, skip_full, gategain_full = pieces_full
    normed_f, norm_back = jax.vjp(norm_input, layer_in, norm_full)
    normed = normed_f.astype(jnp.bfloat16)
    in_whole = gather_rows(in_weight, by_permutes=True)
    in_whole, out_weight = lax.optimization_barrier((in_whole, out_weight))
    out_whole = gather_rows(out_weight)
    projected = jnp.dot(normed, in_whole, preferred_element_type=jnp.float32)

    def bound_mixer(proj_arg, cw_arg, cb_arg, sb_arg, dl_arg, sk_arg, gg_arg):
        return mixer(proj_arg, segment, cw_arg, cb_arg, sb_arg, dl_arg, sk_arg, gg_arg)

    gated_f, mixer_back = jax.vjp(
        bound_mixer,
        projected,
        convw_full,
        convb_full,
        stepb_full,
        decay_full,
        skip_full,
        gategain_full,
    )
    gated = gated_f.astype(jnp.bfloat16)
    branch_out = jnp.dot(gated, out_whole, preferred_element_type=jnp.float32)
    layer_out = layer_in + branch_out
    cot_low = cotangent.astype(jnp.bfloat16)
    out_halves = reduce_core(row_product(gated, cot_low))
    gated_grad = back_product(cot_low, out_whole)
    out_halves, gated_grad = lax.optimization_barrier((out_halves, gated_grad))
    out_owned = reduce_rest(out_halves)
    proj_grad, g_convw, g_convb, g_stepb, g_decay, g_skip, g_gategain = mixer_back(gated_grad)
    proj_low = proj_grad.astype(jnp.bfloat16)
    normed_grad = back_product(proj_low, in_whole)
    back_in, g_norm = norm_back(normed_grad)
    input_grad = cotangent + back_in
    grads = (g_norm, g_convw, g_convb, g_stepb, g_decay, g_skip, g_gategain)
    small_blocks = jnp.concatenate([g.reshape(groups, -1) for g in grads], axis=1)
    cols = proj_low.shape[1]
    wide = -(-cols // 128) * 128
    proj_wide = jnp.pad(proj_low, ((0, 0), (0, wide - cols)))
    in_owned = reduce_rows(row_product(normed, proj_wide), out_owned)[:, :cols]
    small_sum = exchange_sum(small_blocks, ("shard_1", "shard_0", "core", "rep_hi"))
    mine = lax.dynamic_index_in_dim(small_sum, lax.axis_index(SHARD), axis=0, keepdims=False)
    small_final = []
    offset = 0
    for g in grads:
        size = g.size // groups
        small_final.append(mine[offset : offset + size].reshape((g.shape[0] // groups,) + g.shape[1:]))
        offset += size
    return (
        layer_out,
        input_grad,
        small_final[0],
        in_owned,
        small_final[1],
        small_final[2],
        small_final[3],
        small_final[4],
        small_final[5],
        small_final[6],
        out_owned,
    )


def solution(mesh):
    split = Mesh(
        mesh.devices.reshape(mesh.shape["rep"] // 2, 2, 4, 2),
        ("rep_hi", "core", "shard_0", "shard_1"),
    )
    in_specs = (
        P(REP_SHARD, None),
        P(REP_SHARD, None),
        P(REP_SHARD, None),
        P(SHARD),
        P(SHARD, None),
        P(SHARD, None),
        P(SHARD),
        P(SHARD),
        P(SHARD),
        P(SHARD),
        P(SHARD),
        P(SHARD, None),
    )
    out_specs = (
        P(REP_SHARD, None),
        P(REP_SHARD, None),
        P(SHARD),
        P(SHARD, None),
        P(SHARD, None),
        P(SHARD),
        P(SHARD),
        P(SHARD),
        P(SHARD),
        P(SHARD),
        P(SHARD, None),
    )
    return jax.shard_map(
        on_device, mesh=split, in_specs=in_specs, out_specs=out_specs, check_vma=False
    )
```

```python
import math

import jax
import jax.numpy as jnp
from jax import lax
from jax.sharding import Mesh
from jax.sharding import PartitionSpec as P

SPAN = 256
SHARD = ("shard_0", "shard_1")
REP = ("rep_hi", "core")
REP_SHARD = ("rep_hi", "core", "shard_0", "shard_1")
ALL = REP_SHARD


EPS = 1e-05
HIGH = lax.Precision.HIGHEST


def side_by_side(arrays, axis, dim, along):
    widths = [math.prod(a.shape[along:]) for a in arrays]
    both = jnp.concatenate(
        [a.reshape(*a.shape[:along], w) for a, w in zip(arrays, widths)], axis=along
    )
    result = lax.all_gather(both, axis, axis=dim, tiled=True)
    blocks = jnp.split(result, [sum(widths[:k]) for k in range(1, len(widths))], axis=along)
    return tuple(
        (b.reshape(*result.shape[:along], *a.shape[along:]) for a, b in zip(arrays, blocks))
    )


def sum_by_axis(total, axes):
    for axis in axes:
        total = lax.psum_scatter(total, axis, scatter_dimension=0, tiled=True)
    return total


def in_blocks(shard, dim, size):
    before, after = (shard.shape[:dim], shard.shape[dim + 1 :])
    return jnp.moveaxis(shard.reshape(*before, size, -1, *after), dim, 0)


def sum_at_owner(shard, axis, dim):
    size = lax.axis_size(axis)
    blocks = lax.all_to_all(in_blocks(shard, dim, size), axis, 0, 0, tiled=True)
    return jnp.sum(blocks, axis=0)


def sent_together(arrays, axis, dim, along):
    widths = [math.prod(a.shape[along:]) for a in arrays]
    both = jnp.concatenate(
        [a.reshape(*a.shape[:along], w) for a, w in zip(arrays, widths)], axis=along
    )
    result = sum_at_owner(both, axis, dim)
    blocks = jnp.split(result, [sum(widths[:k]) for k in range(1, len(widths))], axis=along)
    return tuple(
        (b.reshape(*result.shape[:along], *a.shape[along:]) for a, b in zip(arrays, blocks))
    )


def shifted(values, lag):
    zeros_top = jnp.zeros((lag,) + values.shape[1:], values.dtype)
    return jnp.concatenate([zeros_top, values[:-lag]], axis=0)


def segment_ids(lengths_row, count):
    offsets = jnp.cumsum(lengths_row, dtype=jnp.int32) - lengths_row
    places = jnp.arange(count, dtype=jnp.int32)
    return (
        jnp.sum((places[:, None] >= offsets[None, :]).astype(jnp.int32), axis=1, dtype=jnp.int32)
        - 1
    )


def row_product(left, right):
    return lax.dot_general(
        left, right, (((0,), (0,)), ((), ())), preferred_element_type=jnp.float32
    )


def back_product(left, right):
    return lax.dot_general(
        left, right, (((1,), (1,)), ((), ())), preferred_element_type=jnp.float32
    )


def norm_input(inputs, gain_one):
    scaling = lax.rsqrt(jnp.mean(inputs * inputs, axis=1, keepdims=True) + EPS)
    return inputs * scaling * gain_one[None, :]


def mixer(projected, segment, conv_weight, conv_bias, step_bias, decay_log, skip_gain, gate_gain):
    count = projected.shape[0]
    inner = gate_gain.shape[0]
    heads = step_bias.shape[0]
    head_dim = inner // heads
    channels = conv_weight.shape[0]
    state_dim = (channels - inner) // 2
    taps = conv_weight.shape[1]
    gate_part = projected[:, :inner]
    conv_in = projected[:, inner : inner + channels]
    step_raw = projected[:, inner + channels :]
    places = jnp.arange(count, dtype=jnp.int32)
    conv_out = conv_bias[None, :] + conv_weight[:, taps - 1][None, :] * conv_in
    for lag in range(1, taps):
        same = (shifted(segment, lag) == segment) & (places >= lag)
        conv_out = conv_out + jnp.where(
            same[:, None], conv_weight[:, taps - 1 - lag][None, :] * shifted(conv_in, lag), 0.0
        )
    activated = jax.nn.silu(conv_out)
    values = activated[:, :inner].reshape(count, heads, head_dim)
    b_matrix = activated[:, inner : inner + state_dim]
    c_matrix = activated[:, inner + state_dim :]
    step_size = jax.nn.softplus(step_raw + step_bias[None, :])
    decay = -jnp.exp(decay_log)[None, :] * step_size
    blocks = count // SPAN
    values_c = values.reshape(blocks, SPAN, heads, head_dim)
    b_spans = b_matrix.reshape(blocks, SPAN, state_dim)
    c_spans = c_matrix.reshape(blocks, SPAN, state_dim)
    step_c = step_size.reshape(blocks, SPAN, heads)
    cumul = jnp.cumsum(decay.reshape(blocks, SPAN, heads), axis=1)
    seg_c = segment.reshape(blocks, SPAN)
    rows_in = jnp.arange(SPAN, dtype=jnp.int32)
    lower = rows_in[:, None] >= rows_in[None, :]
    allowed = lower[None] & (seg_c[:, :, None] == seg_c[:, None, :])
    cumul_t = jnp.transpose(cumul, (0, 2, 1))
    differ = cumul_t[:, :, :, None] - cumul_t[:, :, None, :]
    weights_l = jnp.exp(jnp.where(allowed[:, None], differ, -10000.0))
    scores = jnp.einsum("cin,cjn->cij", c_spans, b_spans, precision=HIGH)
    mixing = weights_l * scores[:, None]
    scaled_in = values_c * step_c[..., None]
    y_intra = jnp.einsum("chij,cjhp->cihp", mixing, scaled_in, precision=HIGH)
    carried = jnp.zeros((heads, head_dim, state_dim), jnp.float32)
    before_seg = jnp.int32(-1)
    linked = (seg_c[0] == before_seg).astype(jnp.float32)
    reach = jnp.exp(cumul[0]) * linked[:, None]
    inter = jnp.einsum("in,hpn->ihp", c_spans[0], carried, precision=HIGH) * reach[:, :, None]
    pieces = [y_intra[0] + inter]
    y_all = jnp.concatenate(pieces, axis=0) + skip_gain[None, :, None] * values
    gated_pre = y_all.reshape(count, inner) * jax.nn.silu(gate_part)
    scaling = lax.rsqrt(jnp.mean(gated_pre * gated_pre, axis=1, keepdims=True) + EPS)
    return gated_pre * scaling * gate_gain[None, :]


def reduce_group(halves):
    ring = lax.axis_size("shard_0")
    y = lax.axis_index("shard_1")
    z = lax.axis_index("shard_0")
    rows, cols = halves.shape[1], halves.shape[2]
    blocks = halves.reshape(ring, 2, rows, cols)
    doubled = jnp.concatenate([blocks, blocks], axis=0)
    rel = lax.dynamic_slice_in_dim(doubled, z, ring, axis=0)
    up = [(i, (i + 1) % ring) for i in range(ring)]
    down = [(i, (i - 1) % ring) for i in range(ring)]
    half = rows // 2
    low = lambda a: a.astype(jnp.bfloat16)
    acc_up = lax.ppermute(low(rel[3][:, :half]), "shard_0", up)
    acc_dn = lax.ppermute(low(rel[1][:, half:]), "shard_0", down)
    acc_up = lax.ppermute(low(acc_up + rel[2][:, :half]), "shard_0", up)
    acc_dn = lax.ppermute(low(acc_dn + rel[2][:, half:]), "shard_0", down)
    acc_up = lax.ppermute(low(acc_up + rel[1][:, :half]), "shard_0", up)
    acc_dn = lax.ppermute(low(acc_dn + rel[3][:, half:]), "shard_0", down)
    zsum = jnp.concatenate(
        [acc_up.astype(jnp.float32) + rel[0][:, :half], acc_dn.astype(jnp.float32) + rel[0][:, half:]],
        axis=1,
    )
    keep = lax.dynamic_index_in_dim(zsum, y, axis=0, keepdims=False)
    give = lax.dynamic_index_in_dim(zsum, 1 - y, axis=0, keepdims=False)
    return keep + lax.ppermute(low(give), "shard_1", [(0, 1), (1, 0)]).astype(jnp.float32)


def core_swap(values):
    return lax.ppermute(values, "core", [(0, 1), (1, 0)])


def gather_group(block):
    ring = lax.axis_size("shard_0")
    y = lax.axis_index("shard_1")
    z = lax.axis_index("shard_0")
    other_y = lax.ppermute(block, "shard_1", [(0, 1), (1, 0)])
    pair = jnp.where(y == 0, jnp.stack([block, other_y]), jnp.stack([other_y, block]))
    up = [(i, (i + 1) % ring) for i in range(ring)]
    down = [(i, (i - 1) % ring) for i in range(ring)]
    from_prev = lax.ppermute(pair, "shard_0", up)
    from_next = lax.ppermute(pair, "shard_0", down)
    half = block.shape[0] // 2
    far_a = lax.ppermute(from_prev[:, :half], "shard_0", up)
    far_b = lax.ppermute(from_next[:, half:], "shard_0", down)
    opposite = jnp.concatenate([far_a, far_b], axis=1)
    ordered = jnp.stack([pair, from_next, opposite, from_prev])
    doubled = jnp.concatenate([ordered, ordered], axis=0)
    start = (ring - z) % ring
    placed = lax.dynamic_slice_in_dim(doubled, start, ring, axis=0)
    return placed.reshape((ring * 2,) + block.shape)


def core_swap(values):
    return lax.ppermute(values, "core", [(0, 1), (1, 0)])


def gather_rows(weight, by_permutes=False):
    rows = weight.shape[0]
    half = rows // 2
    core = lax.axis_index("core")
    mine = lax.dynamic_slice_in_dim(weight, core * half, half, axis=0)
    if by_permutes:
        part = gather_group(mine)
    else:
        part = lax.all_gather(mine, SHARD, axis=0, tiled=False)
    other = core_swap(part)
    first = jnp.where(core == 0, part, other)
    second = jnp.where(core == 0, other, part)
    return jnp.stack([first, second], axis=1).reshape(-1, weight.shape[1])


def reduce_core(partial):
    groups = lax.axis_size(SHARD)
    cols = partial.shape[1]
    core = lax.axis_index("core")
    blocks = partial.reshape(groups, 2, -1, cols)
    keep = jnp.where(core == 0, blocks[:, 0], blocks[:, 1])
    give = jnp.where(core == 0, blocks[:, 1], blocks[:, 0])
    return keep + core_swap(give)


def reduce_rest(halves, wait_for=None):
    core = lax.axis_index("core")
    owned = reduce_group(halves)
    if wait_for is not None:
        owned, wait_for = lax.optimization_barrier((owned, wait_for))
    owned = lax.psum(owned, "rep_hi")
    other = core_swap(owned)
    first = jnp.where(core == 0, owned, other)
    second = jnp.where(core == 0, other, owned)
    return jnp.concatenate([first, second], axis=0)


def reduce_rows(partial, wait_for=None):
    return reduce_rest(reduce_core(partial), wait_for)


def exchange_sum(values, axes):
    for axis in axes:
        size = lax.axis_size(axis)
        step = 1
        while step < size:
            pairs = [(i, i ^ step) for i in range(size)]
            values = values + lax.ppermute(values, axis, pairs)
            step *= 2
    return values


def on_device(
    layer_in,
    cotangent,
    seq_lengths,
    norm_gain,
    in_weight,
    conv_weight,
    conv_bias,
    step_bias,
    decay_log,
    skip_gain,
    gate_gain,
    out_weight,
):
    count = layer_in.shape[0]
    groups = lax.axis_size(SHARD)
    segment = segment_ids(seq_lengths[0], count)
    smalls = (norm_gain, conv_weight, conv_bias, step_bias, decay_log, skip_gain, gate_gain)
    flat = jnp.concatenate([a.reshape(-1) for a in smalls])
    flat_len = flat.shape[0]
    place = lax.axis_index(SHARD)
    spread = jnp.where(
        (jnp.arange(groups, dtype=jnp.int32) == place)[:, None], flat[None, :], 0.0
    )
    flat_all = exchange_sum(spread, ("shard_1", "shard_0"))
    pieces_full = []
    offset = 0
    for a in smalls:
        size = a.size
        block = flat_all[:, offset : offset + size]
        pieces_full.append(block.reshape((groups * a.shape[0],) + a.shape[1:]))
        offset += size
    norm_full, convw_full, convb_full, stepb_full, decay_full, skip_full, gategain_full = pieces_full
    normed_f, norm_back = jax.vjp(norm_input, layer_in, norm_full)
    normed = normed_f.astype(jnp.bfloat16)
    in_whole = gather_rows(in_weight, by_permutes=True)
    in_whole, out_weight = lax.optimization_barrier((in_whole, out_weight))
    out_whole = gather_rows(out_weight)
    projected = jnp.dot(normed, in_whole, preferred_element_type=jnp.float32)

    def bound_mixer(proj_arg, cw_arg, cb_arg, sb_arg, dl_arg, sk_arg, gg_arg):
        return mixer(proj_arg, segment, cw_arg, cb_arg, sb_arg, dl_arg, sk_arg, gg_arg)

    gated_f, mixer_back = jax.vjp(
        bound_mixer,
        projected,
        convw_full,
        convb_full,
        stepb_full,
        decay_full,
        skip_full,
        gategain_full,
    )
    gated = gated_f.astype(jnp.bfloat16)
    branch_out = jnp.dot(gated, out_whole, preferred_element_type=jnp.float32)
    layer_out = layer_in + branch_out
    cot_low = cotangent.astype(jnp.bfloat16)
    out_halves = reduce_core(row_product(gated, cot_low))
    gated_grad = back_product(cot_low, out_whole)
    out_halves, gated_grad = lax.optimization_barrier((out_halves, gated_grad))
    out_owned = reduce_rest(out_halves)
    proj_grad, g_convw, g_convb, g_stepb, g_decay, g_skip, g_gategain = mixer_back(gated_grad)
    proj_low = proj_grad.astype(jnp.bfloat16)
    normed_grad = back_product(proj_low, in_whole)
    back_in, g_norm = norm_back(normed_grad)
    input_grad = cotangent + back_in
    grads = (g_norm, g_convw, g_convb, g_stepb, g_decay, g_skip, g_gategain)
    small_blocks = jnp.concatenate([g.reshape(groups, -1) for g in grads], axis=1)
    cols = proj_low.shape[1]
    wide = -(-cols // 128) * 128
    proj_wide = jnp.pad(proj_low, ((0, 0), (0, wide - cols)))
    in_owned = reduce_rows(row_product(normed, proj_wide))[:, :cols]
    small_sum = exchange_sum(small_blocks, ("shard_1", "shard_0", "core", "rep_hi"))
    mine = lax.dynamic_index_in_dim(small_sum, lax.axis_index(SHARD), axis=0, keepdims=False)
    small_final = []
    offset = 0
    for g in grads:
        size = g.size // groups
        small_final.append(mine[offset : offset + size].reshape((g.shape[0] // groups,) + g.shape[1:]))
        offset += size
    return (
        layer_out,
        input_grad,
        small_final[0],
        in_owned,
        small_final[1],
        small_final[2],
        small_final[3],
        small_final[4],
        small_final[5],
        small_final[6],
        out_owned,
    )


def solution(mesh):
    split = Mesh(
        mesh.devices.reshape(mesh.shape["rep"] // 2, 2, 4, 2),
        ("rep_hi", "core", "shard_0", "shard_1"),
    )
    in_specs = (
        P(REP_SHARD, None),
        P(REP_SHARD, None),
        P(REP_SHARD, None),
        P(SHARD),
        P(SHARD, None),
        P(SHARD, None),
        P(SHARD),
        P(SHARD),
        P(SHARD),
        P(SHARD),
        P(SHARD),
        P(SHARD, None),
    )
    out_specs = (
        P(REP_SHARD, None),
        P(REP_SHARD, None),
        P(SHARD),
        P(SHARD, None),
        P(SHARD, None),
        P(SHARD),
        P(SHARD),
        P(SHARD),
        P(SHARD),
        P(SHARD),
        P(SHARD, None),
    )
    return jax.shard_map(
        on_device, mesh=split, in_specs=in_specs, out_specs=out_specs, check_vma=False
    )
```

```python
import math

import jax
import jax.numpy as jnp
from jax import lax
from jax.sharding import Mesh
from jax.sharding import PartitionSpec as P

SPAN = 256
SHARD = ("shard_0", "shard_1")
REP = ("rep_hi", "core")
REP_SHARD = ("rep_hi", "core", "shard_0", "shard_1")
ALL = REP_SHARD


EPS = 1e-05
HIGH = lax.Precision.HIGHEST


def side_by_side(arrays, axis, dim, along):
    widths = [math.prod(a.shape[along:]) for a in arrays]
    both = jnp.concatenate(
        [a.reshape(*a.shape[:along], w) for a, w in zip(arrays, widths)], axis=along
    )
    result = lax.all_gather(both, axis, axis=dim, tiled=True)
    blocks = jnp.split(result, [sum(widths[:k]) for k in range(1, len(widths))], axis=along)
    return tuple(
        (b.reshape(*result.shape[:along], *a.shape[along:]) for a, b in zip(arrays, blocks))
    )


def sum_by_axis(total, axes):
    for axis in axes:
        total = lax.psum_scatter(total, axis, scatter_dimension=0, tiled=True)
    return total


def in_blocks(shard, dim, size):
    before, after = (shard.shape[:dim], shard.shape[dim + 1 :])
    return jnp.moveaxis(shard.reshape(*before, size, -1, *after), dim, 0)


def sum_at_owner(shard, axis, dim):
    size = lax.axis_size(axis)
    blocks = lax.all_to_all(in_blocks(shard, dim, size), axis, 0, 0, tiled=True)
    return jnp.sum(blocks, axis=0)


def sent_together(arrays, axis, dim, along):
    widths = [math.prod(a.shape[along:]) for a in arrays]
    both = jnp.concatenate(
        [a.reshape(*a.shape[:along], w) for a, w in zip(arrays, widths)], axis=along
    )
    result = sum_at_owner(both, axis, dim)
    blocks = jnp.split(result, [sum(widths[:k]) for k in range(1, len(widths))], axis=along)
    return tuple(
        (b.reshape(*result.shape[:along], *a.shape[along:]) for a, b in zip(arrays, blocks))
    )


def shifted(values, lag):
    zeros_top = jnp.zeros((lag,) + values.shape[1:], values.dtype)
    return jnp.concatenate([zeros_top, values[:-lag]], axis=0)


def segment_ids(lengths_row, count):
    offsets = jnp.cumsum(lengths_row, dtype=jnp.int32) - lengths_row
    places = jnp.arange(count, dtype=jnp.int32)
    return (
        jnp.sum((places[:, None] >= offsets[None, :]).astype(jnp.int32), axis=1, dtype=jnp.int32)
        - 1
    )


def row_product(left, right):
    return lax.dot_general(
        left, right, (((0,), (0,)), ((), ())), preferred_element_type=jnp.float32
    )


def back_product(left, right):
    return lax.dot_general(
        left, right, (((1,), (1,)), ((), ())), preferred_element_type=jnp.float32
    )


def norm_input(inputs, gain_one):
    scaling = lax.rsqrt(jnp.mean(inputs * inputs, axis=1, keepdims=True) + EPS)
    return inputs * scaling * gain_one[None, :]


def mixer(projected, segment, conv_weight, conv_bias, step_bias, decay_log, skip_gain, gate_gain):
    count = projected.shape[0]
    inner = gate_gain.shape[0]
    heads = step_bias.shape[0]
    head_dim = inner // heads
    channels = conv_weight.shape[0]
    state_dim = (channels - inner) // 2
    taps = conv_weight.shape[1]
    gate_part = projected[:, :inner]
    conv_in = projected[:, inner : inner + channels]
    step_raw = projected[:, inner + channels :]
    places = jnp.arange(count, dtype=jnp.int32)
    conv_out = conv_bias[None, :] + conv_weight[:, taps - 1][None, :] * conv_in
    for lag in range(1, taps):
        same = (shifted(segment, lag) == segment) & (places >= lag)
        conv_out = conv_out + jnp.where(
            same[:, None], conv_weight[:, taps - 1 - lag][None, :] * shifted(conv_in, lag), 0.0
        )
    activated = jax.nn.silu(conv_out)
    values = activated[:, :inner].reshape(count, heads, head_dim)
    b_matrix = activated[:, inner : inner + state_dim]
    c_matrix = activated[:, inner + state_dim :]
    step_size = jax.nn.softplus(step_raw + step_bias[None, :])
    decay = -jnp.exp(decay_log)[None, :] * step_size
    blocks = count // SPAN
    values_c = values.reshape(blocks, SPAN, heads, head_dim)
    b_spans = b_matrix.reshape(blocks, SPAN, state_dim)
    c_spans = c_matrix.reshape(blocks, SPAN, state_dim)
    step_c = step_size.reshape(blocks, SPAN, heads)
    cumul = jnp.cumsum(decay.reshape(blocks, SPAN, heads), axis=1)
    seg_c = segment.reshape(blocks, SPAN)
    rows_in = jnp.arange(SPAN, dtype=jnp.int32)
    lower = rows_in[:, None] >= rows_in[None, :]
    allowed = lower[None] & (seg_c[:, :, None] == seg_c[:, None, :])
    cumul_t = jnp.transpose(cumul, (0, 2, 1))
    differ = cumul_t[:, :, :, None] - cumul_t[:, :, None, :]
    weights_l = jnp.exp(jnp.where(allowed[:, None], differ, -10000.0))
    scores = jnp.einsum("cin,cjn->cij", c_spans, b_spans, precision=HIGH)
    mixing = weights_l * scores[:, None]
    scaled_in = values_c * step_c[..., None]
    y_intra = jnp.einsum("chij,cjhp->cihp", mixing, scaled_in, precision=HIGH)
    carried = jnp.zeros((heads, head_dim, state_dim), jnp.float32)
    before_seg = jnp.int32(-1)
    linked = (seg_c[0] == before_seg).astype(jnp.float32)
    reach = jnp.exp(cumul[0]) * linked[:, None]
    inter = jnp.einsum("in,hpn->ihp", c_spans[0], carried, precision=HIGH) * reach[:, :, None]
    pieces = [y_intra[0] + inter]
    y_all = jnp.concatenate(pieces, axis=0) + skip_gain[None, :, None] * values
    gated_pre = y_all.reshape(count, inner) * jax.nn.silu(gate_part)
    scaling = lax.rsqrt(jnp.mean(gated_pre * gated_pre, axis=1, keepdims=True) + EPS)
    return gated_pre * scaling * gate_gain[None, :]


def reduce_group(halves):
    ring = lax.axis_size("shard_0")
    y = lax.axis_index("shard_1")
    z = lax.axis_index("shard_0")
    rows, cols = halves.shape[1], halves.shape[2]
    blocks = halves.reshape(ring, 2, rows, cols)
    doubled = jnp.concatenate([blocks, blocks], axis=0)
    rel = lax.dynamic_slice_in_dim(doubled, z, ring, axis=0)
    up = [(i, (i + 1) % ring) for i in range(ring)]
    down = [(i, (i - 1) % ring) for i in range(ring)]
    half = rows // 2
    low = lambda a: a.astype(jnp.bfloat16)
    acc_up = lax.ppermute(low(rel[3][:, :half]), "shard_0", up)
    acc_dn = lax.ppermute(low(rel[1][:, half:]), "shard_0", down)
    acc_up = lax.ppermute(low(acc_up + rel[2][:, :half]), "shard_0", up)
    acc_dn = lax.ppermute(low(acc_dn + rel[2][:, half:]), "shard_0", down)
    acc_up = lax.ppermute(low(acc_up + rel[1][:, :half]), "shard_0", up)
    acc_dn = lax.ppermute(low(acc_dn + rel[3][:, half:]), "shard_0", down)
    zsum = jnp.concatenate(
        [acc_up.astype(jnp.float32) + rel[0][:, :half], acc_dn.astype(jnp.float32) + rel[0][:, half:]],
        axis=1,
    )
    keep = lax.dynamic_index_in_dim(zsum, y, axis=0, keepdims=False)
    give = lax.dynamic_index_in_dim(zsum, 1 - y, axis=0, keepdims=False)
    return keep + lax.ppermute(low(give), "shard_1", [(0, 1), (1, 0)]).astype(jnp.float32)


def allreduce_rep(values):
    ring = 4
    size = lax.axis_size("rep_hi")
    index = lax.axis_index("rep_hi")
    x = index % ring
    up = [(i, (i // ring) * ring + (i % ring + 1) % ring) for i in range(size)]
    down = [(i, (i // ring) * ring + (i % ring - 1) % ring) for i in range(size)]
    rows = values.shape[0]
    chunks = values.reshape(ring, rows // ring, values.shape[1])
    doubled = jnp.concatenate([chunks, chunks], axis=0)
    rel = lax.dynamic_slice_in_dim(doubled, x, ring, axis=0)
    half = rows // ring // 2
    a = lax.ppermute(rel[2][:half], "rep_hi", up)
    b = lax.ppermute(rel[2][half:], "rep_hi", down)
    up_msg = jnp.concatenate([a + rel[1][:half], rel[1][half:]], axis=0)
    down_msg = jnp.concatenate([rel[3][:half], b + rel[3][half:]], axis=0)
    mine = rel[0] + lax.ppermute(up_msg, "rep_hi", up) + lax.ppermute(down_msg, "rep_hi", down)
    step = ring
    while step < size:
        mine = mine + lax.ppermute(mine, "rep_hi", [(i, i ^ step) for i in range(size)])
        step *= 2
    from_prev = lax.ppermute(mine, "rep_hi", up)
    from_next = lax.ppermute(mine, "rep_hi", down)
    far_a = lax.ppermute(from_prev[:half], "rep_hi", up)
    far_b = lax.ppermute(from_next[half:], "rep_hi", down)
    opposite = jnp.concatenate([far_a, far_b], axis=0)
    ordered = jnp.stack([mine, from_next, opposite, from_prev])
    doubled = jnp.concatenate([ordered, ordered], axis=0)
    placed = lax.dynamic_slice_in_dim(doubled, (ring - x) % ring, ring, axis=0)
    return placed.reshape(values.shape)


def core_join(owned):
    core = lax.axis_index("core")
    other = core_swap(owned)
    first = jnp.where(core == 0, owned, other)
    second = jnp.where(core == 0, other, owned)
    return jnp.concatenate([first, second], axis=0)


def core_swap(values):
    return lax.ppermute(values, "core", [(0, 1), (1, 0)])


def gather_group(block):
    ring = lax.axis_size("shard_0")
    y = lax.axis_index("shard_1")
    z = lax.axis_index("shard_0")
    other_y = lax.ppermute(block, "shard_1", [(0, 1), (1, 0)])
    pair = jnp.where(y == 0, jnp.stack([block, other_y]), jnp.stack([other_y, block]))
    up = [(i, (i + 1) % ring) for i in range(ring)]
    down = [(i, (i - 1) % ring) for i in range(ring)]
    from_prev = lax.ppermute(pair, "shard_0", up)
    from_next = lax.ppermute(pair, "shard_0", down)
    half = block.shape[0] // 2
    far_a = lax.ppermute(from_prev[:, :half], "shard_0", up)
    far_b = lax.ppermute(from_next[:, half:], "shard_0", down)
    opposite = jnp.concatenate([far_a, far_b], axis=1)
    ordered = jnp.stack([pair, from_next, opposite, from_prev])
    doubled = jnp.concatenate([ordered, ordered], axis=0)
    start = (ring - z) % ring
    placed = lax.dynamic_slice_in_dim(doubled, start, ring, axis=0)
    return placed.reshape((ring * 2,) + block.shape)


def core_swap(values):
    return lax.ppermute(values, "core", [(0, 1), (1, 0)])


def gather_rows(weight, by_permutes=False):
    rows = weight.shape[0]
    half = rows // 2
    core = lax.axis_index("core")
    mine = lax.dynamic_slice_in_dim(weight, core * half, half, axis=0)
    if by_permutes:
        part = gather_group(mine)
    else:
        part = lax.all_gather(mine, SHARD, axis=0, tiled=False)
    other = core_swap(part)
    first = jnp.where(core == 0, part, other)
    second = jnp.where(core == 0, other, part)
    return jnp.stack([first, second], axis=1).reshape(-1, weight.shape[1])


def reduce_core(partial):
    groups = lax.axis_size(SHARD)
    cols = partial.shape[1]
    core = lax.axis_index("core")
    blocks = partial.reshape(groups, 2, -1, cols)
    keep = jnp.where(core == 0, blocks[:, 0], blocks[:, 1])
    give = jnp.where(core == 0, blocks[:, 1], blocks[:, 0])
    return keep + core_swap(give)


def reduce_rest(halves, wait_for=None):
    core = lax.axis_index("core")
    owned = reduce_group(halves)
    if wait_for is not None:
        owned, wait_for = lax.optimization_barrier((owned, wait_for))
    owned = lax.psum(owned, "rep_hi")
    other = core_swap(owned)
    first = jnp.where(core == 0, owned, other)
    second = jnp.where(core == 0, other, owned)
    return jnp.concatenate([first, second], axis=0)


def reduce_rows(partial, wait_for=None):
    return reduce_rest(reduce_core(partial), wait_for)


def exchange_sum(values, axes):
    for axis in axes:
        size = lax.axis_size(axis)
        step = 1
        while step < size:
            pairs = [(i, i ^ step) for i in range(size)]
            values = values + lax.ppermute(values, axis, pairs)
            step *= 2
    return values


def on_device(
    layer_in,
    cotangent,
    seq_lengths,
    norm_gain,
    in_weight,
    conv_weight,
    conv_bias,
    step_bias,
    decay_log,
    skip_gain,
    gate_gain,
    out_weight,
):
    count = layer_in.shape[0]
    groups = lax.axis_size(SHARD)
    segment = segment_ids(seq_lengths[0], count)
    smalls = (norm_gain, conv_weight, conv_bias, step_bias, decay_log, skip_gain, gate_gain)
    flat = jnp.concatenate([a.reshape(-1) for a in smalls])
    flat_len = flat.shape[0]
    place = lax.axis_index(SHARD)
    spread = jnp.where(
        (jnp.arange(groups, dtype=jnp.int32) == place)[:, None], flat[None, :], 0.0
    )
    flat_all = exchange_sum(spread, ("shard_1", "shard_0"))
    pieces_full = []
    offset = 0
    for a in smalls:
        size = a.size
        block = flat_all[:, offset : offset + size]
        pieces_full.append(block.reshape((groups * a.shape[0],) + a.shape[1:]))
        offset += size
    norm_full, convw_full, convb_full, stepb_full, decay_full, skip_full, gategain_full = pieces_full
    normed_f, norm_back = jax.vjp(norm_input, layer_in, norm_full)
    normed = normed_f.astype(jnp.bfloat16)
    in_whole = gather_rows(in_weight, by_permutes=True)
    out_whole = gather_rows(out_weight)
    projected = jnp.dot(normed, in_whole, preferred_element_type=jnp.float32)

    def bound_mixer(proj_arg, cw_arg, cb_arg, sb_arg, dl_arg, sk_arg, gg_arg):
        return mixer(proj_arg, segment, cw_arg, cb_arg, sb_arg, dl_arg, sk_arg, gg_arg)

    gated_f, mixer_back = jax.vjp(
        bound_mixer,
        projected,
        convw_full,
        convb_full,
        stepb_full,
        decay_full,
        skip_full,
        gategain_full,
    )
    gated = gated_f.astype(jnp.bfloat16)
    branch_out = jnp.dot(gated, out_whole, preferred_element_type=jnp.float32)
    layer_out = layer_in + branch_out
    cot_low = cotangent.astype(jnp.bfloat16)
    out_halves = reduce_core(row_product(gated, cot_low))
    gated_grad = back_product(cot_low, out_whole)
    out_halves, gated_grad = lax.optimization_barrier((out_halves, gated_grad))
    out_group = reduce_group(out_halves)
    proj_grad, g_convw, g_convb, g_stepb, g_decay, g_skip, g_gategain = mixer_back(gated_grad)
    proj_low = proj_grad.astype(jnp.bfloat16)
    normed_grad = back_product(proj_low, in_whole)
    back_in, g_norm = norm_back(normed_grad)
    input_grad = cotangent + back_in
    grads = (g_norm, g_convw, g_convb, g_stepb, g_decay, g_skip, g_gategain)
    small_blocks = jnp.concatenate([g.reshape(groups, -1) for g in grads], axis=1)
    cols = proj_low.shape[1]
    wide = -(-cols // 128) * 128
    proj_wide = jnp.pad(proj_low, ((0, 0), (0, wide - cols)))
    in_group = reduce_group(reduce_core(row_product(normed, proj_wide)))
    in_shape, out_shape = in_group.shape, out_group.shape
    joined = jnp.concatenate([in_group.reshape(-1, 128), out_group.reshape(-1, 128)], axis=0)
    joined = allreduce_rep(joined)
    split_at = in_group.size // 128
    in_owned = core_join(joined[:split_at].reshape(in_shape))[:, :cols]
    out_owned = core_join(joined[split_at:].reshape(out_shape))
    small_sum = exchange_sum(small_blocks, ("shard_1", "shard_0", "core", "rep_hi"))
    mine = lax.dynamic_index_in_dim(small_sum, lax.axis_index(SHARD), axis=0, keepdims=False)
    small_final = []
    offset = 0
    for g in grads:
        size = g.size // groups
        small_final.append(mine[offset : offset + size].reshape((g.shape[0] // groups,) + g.shape[1:]))
        offset += size
    return (
        layer_out,
        input_grad,
        small_final[0],
        in_owned,
        small_final[1],
        small_final[2],
        small_final[3],
        small_final[4],
        small_final[5],
        small_final[6],
        out_owned,
    )


def solution(mesh):
    split = Mesh(
        mesh.devices.reshape(mesh.shape["rep"] // 2, 2, 4, 2),
        ("rep_hi", "core", "shard_0", "shard_1"),
    )
    in_specs = (
        P(REP_SHARD, None),
        P(REP_SHARD, None),
        P(REP_SHARD, None),
        P(SHARD),
        P(SHARD, None),
        P(SHARD, None),
        P(SHARD),
        P(SHARD),
        P(SHARD),
        P(SHARD),
        P(SHARD),
        P(SHARD, None),
    )
    out_specs = (
        P(REP_SHARD, None),
        P(REP_SHARD, None),
        P(SHARD),
        P(SHARD, None),
        P(SHARD, None),
        P(SHARD),
        P(SHARD),
        P(SHARD),
        P(SHARD),
        P(SHARD),
        P(SHARD, None),
    )
    return jax.shard_map(
        on_device, mesh=split, in_specs=in_specs, out_specs=out_specs, check_vma=False
    )
```

```python
import math

import jax
import jax.numpy as jnp
from jax import lax
from jax.sharding import Mesh
from jax.sharding import PartitionSpec as P

SPAN = 256
SHARD = ("shard_0", "shard_1")
REP = ("rep_hi", "core")
REP_SHARD = ("rep_hi", "core", "shard_0", "shard_1")
ALL = REP_SHARD


EPS = 1e-05
HIGH = lax.Precision.HIGHEST


def side_by_side(arrays, axis, dim, along):
    widths = [math.prod(a.shape[along:]) for a in arrays]
    both = jnp.concatenate(
        [a.reshape(*a.shape[:along], w) for a, w in zip(arrays, widths)], axis=along
    )
    result = lax.all_gather(both, axis, axis=dim, tiled=True)
    blocks = jnp.split(result, [sum(widths[:k]) for k in range(1, len(widths))], axis=along)
    return tuple(
        (b.reshape(*result.shape[:along], *a.shape[along:]) for a, b in zip(arrays, blocks))
    )


def sum_by_axis(total, axes):
    for axis in axes:
        total = lax.psum_scatter(total, axis, scatter_dimension=0, tiled=True)
    return total


def in_blocks(shard, dim, size):
    before, after = (shard.shape[:dim], shard.shape[dim + 1 :])
    return jnp.moveaxis(shard.reshape(*before, size, -1, *after), dim, 0)


def sum_at_owner(shard, axis, dim):
    size = lax.axis_size(axis)
    blocks = lax.all_to_all(in_blocks(shard, dim, size), axis, 0, 0, tiled=True)
    return jnp.sum(blocks, axis=0)


def sent_together(arrays, axis, dim, along):
    widths = [math.prod(a.shape[along:]) for a in arrays]
    both = jnp.concatenate(
        [a.reshape(*a.shape[:along], w) for a, w in zip(arrays, widths)], axis=along
    )
    result = sum_at_owner(both, axis, dim)
    blocks = jnp.split(result, [sum(widths[:k]) for k in range(1, len(widths))], axis=along)
    return tuple(
        (b.reshape(*result.shape[:along], *a.shape[along:]) for a, b in zip(arrays, blocks))
    )


def shifted(values, lag):
    zeros_top = jnp.zeros((lag,) + values.shape[1:], values.dtype)
    return jnp.concatenate([zeros_top, values[:-lag]], axis=0)


def segment_ids(lengths_row, count):
    offsets = jnp.cumsum(lengths_row, dtype=jnp.int32) - lengths_row
    places = jnp.arange(count, dtype=jnp.int32)
    return (
        jnp.sum((places[:, None] >= offsets[None, :]).astype(jnp.int32), axis=1, dtype=jnp.int32)
        - 1
    )


def row_product(left, right):
    return lax.dot_general(
        left, right, (((0,), (0,)), ((), ())), preferred_element_type=jnp.float32
    )


def back_product(left, right):
    return lax.dot_general(
        left, right, (((1,), (1,)), ((), ())), preferred_element_type=jnp.float32
    )


def norm_input(inputs, gain_one):
    scaling = lax.rsqrt(jnp.mean(inputs * inputs, axis=1, keepdims=True) + EPS)
    return inputs * scaling * gain_one[None, :]


def mixer(projected, segment, conv_weight, conv_bias, step_bias, decay_log, skip_gain, gate_gain):
    count = projected.shape[0]
    inner = gate_gain.shape[0]
    heads = step_bias.shape[0]
    head_dim = inner // heads
    channels = conv_weight.shape[0]
    state_dim = (channels - inner) // 2
    taps = conv_weight.shape[1]
    gate_part = projected[:, :inner]
    conv_in = projected[:, inner : inner + channels]
    step_raw = projected[:, inner + channels :]
    places = jnp.arange(count, dtype=jnp.int32)
    conv_out = conv_bias[None, :] + conv_weight[:, taps - 1][None, :] * conv_in
    for lag in range(1, taps):
        same = (shifted(segment, lag) == segment) & (places >= lag)
        conv_out = conv_out + jnp.where(
            same[:, None], conv_weight[:, taps - 1 - lag][None, :] * shifted(conv_in, lag), 0.0
        )
    activated = jax.nn.silu(conv_out)
    values = activated[:, :inner].reshape(count, heads, head_dim)
    b_matrix = activated[:, inner : inner + state_dim]
    c_matrix = activated[:, inner + state_dim :]
    step_size = jax.nn.softplus(step_raw + step_bias[None, :])
    decay = -jnp.exp(decay_log)[None, :] * step_size
    blocks = count // SPAN
    values_c = values.reshape(blocks, SPAN, heads, head_dim)
    b_spans = b_matrix.reshape(blocks, SPAN, state_dim)
    c_spans = c_matrix.reshape(blocks, SPAN, state_dim)
    step_c = step_size.reshape(blocks, SPAN, heads)
    cumul = jnp.cumsum(decay.reshape(blocks, SPAN, heads), axis=1)
    seg_c = segment.reshape(blocks, SPAN)
    rows_in = jnp.arange(SPAN, dtype=jnp.int32)
    lower = rows_in[:, None] >= rows_in[None, :]
    allowed = lower[None] & (seg_c[:, :, None] == seg_c[:, None, :])
    cumul_t = jnp.transpose(cumul, (0, 2, 1))
    differ = cumul_t[:, :, :, None] - cumul_t[:, :, None, :]
    weights_l = jnp.exp(jnp.where(allowed[:, None], differ, -10000.0))
    scores = jnp.einsum("cin,cjn->cij", c_spans, b_spans, precision=HIGH)
    mixing = weights_l * scores[:, None]
    scaled_in = values_c * step_c[..., None]
    y_intra = jnp.einsum("chij,cjhp->cihp", mixing, scaled_in, precision=HIGH)
    carried = jnp.zeros((heads, head_dim, state_dim), jnp.float32)
    before_seg = jnp.int32(-1)
    linked = (seg_c[0] == before_seg).astype(jnp.float32)
    reach = jnp.exp(cumul[0]) * linked[:, None]
    inter = jnp.einsum("in,hpn->ihp", c_spans[0], carried, precision=HIGH) * reach[:, :, None]
    pieces = [y_intra[0] + inter]
    y_all = jnp.concatenate(pieces, axis=0) + skip_gain[None, :, None] * values
    gated_pre = y_all.reshape(count, inner) * jax.nn.silu(gate_part)
    scaling = lax.rsqrt(jnp.mean(gated_pre * gated_pre, axis=1, keepdims=True) + EPS)
    return gated_pre * scaling * gate_gain[None, :]


def reduce_group(halves, small=None):
    ring = lax.axis_size("shard_0")
    y = lax.axis_index("shard_1")
    z = lax.axis_index("shard_0")
    up = [(i, (i + 1) % ring) for i in range(ring)]
    down = [(i, (i - 1) % ring) for i in range(ring)]
    items = [(halves, jnp.bfloat16)] + ([] if small is None else [(small, jnp.float32)])
    rels, halfs = [], []
    for values, _ in items:
        blocks = values.reshape((ring, 2) + values.shape[1:])
        doubled = jnp.concatenate([blocks, blocks], axis=0)
        rels.append(lax.dynamic_slice_in_dim(doubled, z, ring, axis=0))
        halfs.append(values.shape[1] // 2)

    def send(parts, pairs):
        return [lax.ppermute(p.astype(w), "shard_0", pairs) for p, (_, w) in zip(parts, items)]

    acc_up = send([r[3][:, :h] for r, h in zip(rels, halfs)], up)
    acc_dn = send([r[1][:, h:] for r, h in zip(rels, halfs)], down)
    acc_up = send([a + r[2][:, :h] for a, r, h in zip(acc_up, rels, halfs)], up)
    acc_dn = send([a + r[2][:, h:] for a, r, h in zip(acc_dn, rels, halfs)], down)
    acc_up = send([a + r[1][:, :h] for a, r, h in zip(acc_up, rels, halfs)], up)
    acc_dn = send([a + r[3][:, h:] for a, r, h in zip(acc_dn, rels, halfs)], down)
    results = []
    for au, ad, r, h, (_, w) in zip(acc_up, acc_dn, rels, halfs, items):
        zsum = jnp.concatenate(
            [au.astype(jnp.float32) + r[0][:, :h], ad.astype(jnp.float32) + r[0][:, h:]], axis=1
        )
        keep = lax.dynamic_index_in_dim(zsum, y, axis=0, keepdims=False)
        give = lax.dynamic_index_in_dim(zsum, 1 - y, axis=0, keepdims=False)
        got = lax.ppermute(give.astype(w), "shard_1", [(0, 1), (1, 0)])
        results.append(keep + got.astype(jnp.float32))
    return results[0] if small is None else results


def allreduce_rep(values):
    ring = 4
    size = lax.axis_size("rep_hi")
    index = lax.axis_index("rep_hi")
    x = index % ring
    up = [(i, (i // ring) * ring + (i % ring + 1) % ring) for i in range(size)]
    down = [(i, (i // ring) * ring + (i % ring - 1) % ring) for i in range(size)]
    rows = values.shape[0]
    chunks = values.reshape(ring, rows // ring, values.shape[1])
    doubled = jnp.concatenate([chunks, chunks], axis=0)
    rel = lax.dynamic_slice_in_dim(doubled, x, ring, axis=0)
    half = rows // ring // 2
    a = lax.ppermute(rel[2][:half], "rep_hi", up)
    b = lax.ppermute(rel[2][half:], "rep_hi", down)
    up_msg = jnp.concatenate([a + rel[1][:half], rel[1][half:]], axis=0)
    down_msg = jnp.concatenate([rel[3][:half], b + rel[3][half:]], axis=0)
    mine = rel[0] + lax.ppermute(up_msg, "rep_hi", up) + lax.ppermute(down_msg, "rep_hi", down)
    step = ring
    while step < size:
        mine = mine + lax.ppermute(mine, "rep_hi", [(i, i ^ step) for i in range(size)])
        step *= 2
    from_prev = lax.ppermute(mine, "rep_hi", up)
    from_next = lax.ppermute(mine, "rep_hi", down)
    far_a = lax.ppermute(from_prev[:half], "rep_hi", up)
    far_b = lax.ppermute(from_next[half:], "rep_hi", down)
    opposite = jnp.concatenate([far_a, far_b], axis=0)
    ordered = jnp.stack([mine, from_next, opposite, from_prev])
    doubled = jnp.concatenate([ordered, ordered], axis=0)
    placed = lax.dynamic_slice_in_dim(doubled, (ring - x) % ring, ring, axis=0)
    return placed.reshape(values.shape)


def core_join(owned):
    core = lax.axis_index("core")
    other = core_swap(owned)
    first = jnp.where(core == 0, owned, other)
    second = jnp.where(core == 0, other, owned)
    return jnp.concatenate([first, second], axis=0)


def core_swap(values):
    return lax.ppermute(values, "core", [(0, 1), (1, 0)])


def gather_group(block):
    ring = lax.axis_size("shard_0")
    y = lax.axis_index("shard_1")
    z = lax.axis_index("shard_0")
    other_y = lax.ppermute(block, "shard_1", [(0, 1), (1, 0)])
    pair = jnp.where(y == 0, jnp.stack([block, other_y]), jnp.stack([other_y, block]))
    up = [(i, (i + 1) % ring) for i in range(ring)]
    down = [(i, (i - 1) % ring) for i in range(ring)]
    from_prev = lax.ppermute(pair, "shard_0", up)
    from_next = lax.ppermute(pair, "shard_0", down)
    half = block.shape[0] // 2
    far_a = lax.ppermute(from_prev[:, :half], "shard_0", up)
    far_b = lax.ppermute(from_next[:, half:], "shard_0", down)
    opposite = jnp.concatenate([far_a, far_b], axis=1)
    ordered = jnp.stack([pair, from_next, opposite, from_prev])
    doubled = jnp.concatenate([ordered, ordered], axis=0)
    start = (ring - z) % ring
    placed = lax.dynamic_slice_in_dim(doubled, start, ring, axis=0)
    return placed.reshape((ring * 2,) + block.shape)


def core_swap(values):
    return lax.ppermute(values, "core", [(0, 1), (1, 0)])


def gather_rows(weight, by_permutes=False):
    rows = weight.shape[0]
    half = rows // 2
    core = lax.axis_index("core")
    mine = lax.dynamic_slice_in_dim(weight, core * half, half, axis=0)
    if by_permutes:
        part = gather_group(mine)
    else:
        part = lax.all_gather(mine, SHARD, axis=0, tiled=False)
    other = core_swap(part)
    first = jnp.where(core == 0, part, other)
    second = jnp.where(core == 0, other, part)
    return jnp.stack([first, second], axis=1).reshape(-1, weight.shape[1])


def reduce_core(partial):
    groups = lax.axis_size(SHARD)
    cols = partial.shape[1]
    core = lax.axis_index("core")
    blocks = partial.reshape(groups, 2, -1, cols)
    keep = jnp.where(core == 0, blocks[:, 0], blocks[:, 1])
    give = jnp.where(core == 0, blocks[:, 1], blocks[:, 0])
    return keep + core_swap(give)


def reduce_rest(halves, wait_for=None):
    core = lax.axis_index("core")
    owned = reduce_group(halves)
    if wait_for is not None:
        owned, wait_for = lax.optimization_barrier((owned, wait_for))
    owned = lax.psum(owned, "rep_hi")
    other = core_swap(owned)
    first = jnp.where(core == 0, owned, other)
    second = jnp.where(core == 0, other, owned)
    return jnp.concatenate([first, second], axis=0)


def reduce_rows(partial, wait_for=None):
    return reduce_rest(reduce_core(partial), wait_for)


def exchange_sum(values, axes):
    for axis in axes:
        size = lax.axis_size(axis)
        step = 1
        while step < size:
            pairs = [(i, i ^ step) for i in range(size)]
            values = values + lax.ppermute(values, axis, pairs)
            step *= 2
    return values


def on_device(
    layer_in,
    cotangent,
    seq_lengths,
    norm_gain,
    in_weight,
    conv_weight,
    conv_bias,
    step_bias,
    decay_log,
    skip_gain,
    gate_gain,
    out_weight,
):
    count = layer_in.shape[0]
    groups = lax.axis_size(SHARD)
    segment = segment_ids(seq_lengths[0], count)
    smalls = (norm_gain, conv_weight, conv_bias, step_bias, decay_log, skip_gain, gate_gain)
    flat = jnp.concatenate([a.reshape(-1) for a in smalls])
    flat_len = flat.shape[0]
    place = lax.axis_index(SHARD)
    spread = jnp.where(
        (jnp.arange(groups, dtype=jnp.int32) == place)[:, None], flat[None, :], 0.0
    )
    flat_all = exchange_sum(spread, ("shard_1", "shard_0"))
    pieces_full = []
    offset = 0
    for a in smalls:
        size = a.size
        block = flat_all[:, offset : offset + size]
        pieces_full.append(block.reshape((groups * a.shape[0],) + a.shape[1:]))
        offset += size
    norm_full, convw_full, convb_full, stepb_full, decay_full, skip_full, gategain_full = pieces_full
    normed_f, norm_back = jax.vjp(norm_input, layer_in, norm_full)
    normed = normed_f.astype(jnp.bfloat16)
    in_whole = gather_rows(in_weight, by_permutes=True)
    out_whole = gather_rows(out_weight)
    projected = jnp.dot(normed, in_whole, preferred_element_type=jnp.float32)

    def bound_mixer(proj_arg, cw_arg, cb_arg, sb_arg, dl_arg, sk_arg, gg_arg):
        return mixer(proj_arg, segment, cw_arg, cb_arg, sb_arg, dl_arg, sk_arg, gg_arg)

    gated_f, mixer_back = jax.vjp(
        bound_mixer,
        projected,
        convw_full,
        convb_full,
        stepb_full,
        decay_full,
        skip_full,
        gategain_full,
    )
    gated = gated_f.astype(jnp.bfloat16)
    branch_out = jnp.dot(gated, out_whole, preferred_element_type=jnp.float32)
    layer_out = layer_in + branch_out
    cot_low = cotangent.astype(jnp.bfloat16)
    out_halves = reduce_core(row_product(gated, cot_low))
    gated_grad = back_product(cot_low, out_whole)
    out_halves, gated_grad = lax.optimization_barrier((out_halves, gated_grad))
    out_group = reduce_group(out_halves)
    proj_grad, g_convw, g_convb, g_stepb, g_decay, g_skip, g_gategain = mixer_back(gated_grad)
    proj_low = proj_grad.astype(jnp.bfloat16)
    normed_grad = back_product(proj_low, in_whole)
    back_in, g_norm = norm_back(normed_grad)
    input_grad = cotangent + back_in
    grads = (g_norm, g_convw, g_convb, g_stepb, g_decay, g_skip, g_gategain)
    small_blocks = jnp.concatenate([g.reshape(groups, -1) for g in grads], axis=1)
    small_len = small_blocks.shape[1]
    small_rows = -(-small_len // 2048) * 16
    small_blocks = jnp.pad(small_blocks, ((0, 0), (0, small_rows * 128 - small_len)))
    small_blocks = small_blocks.reshape(groups, small_rows, 128)
    small_blocks = small_blocks + core_swap(small_blocks)
    cols = proj_low.shape[1]
    wide = -(-cols // 128) * 128
    proj_wide = jnp.pad(proj_low, ((0, 0), (0, wide - cols)))
    in_group, small_group = reduce_group(
        reduce_core(row_product(normed, proj_wide)), small_blocks
    )
    in_shape, out_shape = in_group.shape, out_group.shape
    big_rows = (in_group.size + out_group.size) // 128
    tail_rows = -(-(big_rows + small_group.shape[0]) // 64) * 64 - big_rows
    small_group = jnp.pad(small_group, ((0, tail_rows - small_group.shape[0]), (0, 0)))
    joined = jnp.concatenate(
        [in_group.reshape(-1, 128), out_group.reshape(-1, 128), small_group], axis=0
    )
    joined = allreduce_rep(joined)
    split_at = in_group.size // 128
    split_out = split_at + out_group.size // 128
    in_owned = core_join(joined[:split_at].reshape(in_shape))[:, :cols]
    out_owned = core_join(joined[split_at:split_out].reshape(out_shape))
    mine = joined[split_out:].reshape(-1)[:small_len]
    small_final = []
    offset = 0
    for g in grads:
        size = g.size // groups
        small_final.append(mine[offset : offset + size].reshape((g.shape[0] // groups,) + g.shape[1:]))
        offset += size
    return (
        layer_out,
        input_grad,
        small_final[0],
        in_owned,
        small_final[1],
        small_final[2],
        small_final[3],
        small_final[4],
        small_final[5],
        small_final[6],
        out_owned,
    )


def solution(mesh):
    split = Mesh(
        mesh.devices.reshape(mesh.shape["rep"] // 2, 2, 4, 2),
        ("rep_hi", "core", "shard_0", "shard_1"),
    )
    in_specs = (
        P(REP_SHARD, None),
        P(REP_SHARD, None),
        P(REP_SHARD, None),
        P(SHARD),
        P(SHARD, None),
        P(SHARD, None),
        P(SHARD),
        P(SHARD),
        P(SHARD),
        P(SHARD),
        P(SHARD),
        P(SHARD, None),
    )
    out_specs = (
        P(REP_SHARD, None),
        P(REP_SHARD, None),
        P(SHARD),
        P(SHARD, None),
        P(SHARD, None),
        P(SHARD),
        P(SHARD),
        P(SHARD),
        P(SHARD),
        P(SHARD),
        P(SHARD, None),
    )
    return jax.shard_map(
        on_device, mesh=split, in_specs=in_specs, out_specs=out_specs, check_vma=False
    )
```

```python
import math

import jax
import jax.numpy as jnp
from jax import lax
from jax.sharding import Mesh
from jax.sharding import PartitionSpec as P

SPAN = 256
SHARD = ("shard_0", "shard_1")
REP = ("rep_hi", "core")
REP_SHARD = ("rep_hi", "core", "shard_0", "shard_1")
ALL = REP_SHARD


EPS = 1e-05
HIGH = lax.Precision.HIGHEST


def side_by_side(arrays, axis, dim, along):
    widths = [math.prod(a.shape[along:]) for a in arrays]
    both = jnp.concatenate(
        [a.reshape(*a.shape[:along], w) for a, w in zip(arrays, widths)], axis=along
    )
    result = lax.all_gather(both, axis, axis=dim, tiled=True)
    blocks = jnp.split(result, [sum(widths[:k]) for k in range(1, len(widths))], axis=along)
    return tuple(
        (b.reshape(*result.shape[:along], *a.shape[along:]) for a, b in zip(arrays, blocks))
    )


def sum_by_axis(total, axes):
    for axis in axes:
        total = lax.psum_scatter(total, axis, scatter_dimension=0, tiled=True)
    return total


def in_blocks(shard, dim, size):
    before, after = (shard.shape[:dim], shard.shape[dim + 1 :])
    return jnp.moveaxis(shard.reshape(*before, size, -1, *after), dim, 0)


def sum_at_owner(shard, axis, dim):
    size = lax.axis_size(axis)
    blocks = lax.all_to_all(in_blocks(shard, dim, size), axis, 0, 0, tiled=True)
    return jnp.sum(blocks, axis=0)


def sent_together(arrays, axis, dim, along):
    widths = [math.prod(a.shape[along:]) for a in arrays]
    both = jnp.concatenate(
        [a.reshape(*a.shape[:along], w) for a, w in zip(arrays, widths)], axis=along
    )
    result = sum_at_owner(both, axis, dim)
    blocks = jnp.split(result, [sum(widths[:k]) for k in range(1, len(widths))], axis=along)
    return tuple(
        (b.reshape(*result.shape[:along], *a.shape[along:]) for a, b in zip(arrays, blocks))
    )


def shifted(values, lag):
    zeros_top = jnp.zeros((lag,) + values.shape[1:], values.dtype)
    return jnp.concatenate([zeros_top, values[:-lag]], axis=0)


def segment_ids(lengths_row, count):
    offsets = jnp.cumsum(lengths_row, dtype=jnp.int32) - lengths_row
    places = jnp.arange(count, dtype=jnp.int32)
    return (
        jnp.sum((places[:, None] >= offsets[None, :]).astype(jnp.int32), axis=1, dtype=jnp.int32)
        - 1
    )


def row_product(left, right):
    return lax.dot_general(
        left, right, (((0,), (0,)), ((), ())), preferred_element_type=jnp.float32
    )


def back_product(left, right):
    return lax.dot_general(
        left, right, (((1,), (1,)), ((), ())), preferred_element_type=jnp.float32
    )


def norm_input(inputs, gain_one):
    scaling = lax.rsqrt(jnp.mean(inputs * inputs, axis=1, keepdims=True) + EPS)
    return inputs * scaling * gain_one[None, :]


def mixer(projected, segment, conv_weight, conv_bias, step_bias, decay_log, skip_gain, gate_gain):
    count = projected.shape[0]
    inner = gate_gain.shape[0]
    heads = step_bias.shape[0]
    head_dim = inner // heads
    channels = conv_weight.shape[0]
    state_dim = (channels - inner) // 2
    taps = conv_weight.shape[1]
    gate_part = projected[:, :inner]
    conv_in = projected[:, inner : inner + channels]
    step_raw = projected[:, inner + channels :]
    places = jnp.arange(count, dtype=jnp.int32)
    conv_out = conv_bias[None, :] + conv_weight[:, taps - 1][None, :] * conv_in
    for lag in range(1, taps):
        same = (shifted(segment, lag) == segment) & (places >= lag)
        conv_out = conv_out + jnp.where(
            same[:, None], conv_weight[:, taps - 1 - lag][None, :] * shifted(conv_in, lag), 0.0
        )
    activated = jax.nn.silu(conv_out)
    values = activated[:, :inner].reshape(count, heads, head_dim)
    b_matrix = activated[:, inner : inner + state_dim]
    c_matrix = activated[:, inner + state_dim :]
    step_size = jax.nn.softplus(step_raw + step_bias[None, :])
    decay = -jnp.exp(decay_log)[None, :] * step_size
    blocks = count // SPAN
    values_c = values.reshape(blocks, SPAN, heads, head_dim)
    b_spans = b_matrix.reshape(blocks, SPAN, state_dim)
    c_spans = c_matrix.reshape(blocks, SPAN, state_dim)
    step_c = step_size.reshape(blocks, SPAN, heads)
    cumul = jnp.cumsum(decay.reshape(blocks, SPAN, heads), axis=1)
    seg_c = segment.reshape(blocks, SPAN)
    rows_in = jnp.arange(SPAN, dtype=jnp.int32)
    lower = rows_in[:, None] >= rows_in[None, :]
    allowed = lower[None] & (seg_c[:, :, None] == seg_c[:, None, :])
    cumul_t = jnp.transpose(cumul, (0, 2, 1))
    differ = cumul_t[:, :, :, None] - cumul_t[:, :, None, :]
    weights_l = jnp.exp(jnp.where(allowed[:, None], differ, -10000.0))
    scores = jnp.einsum("cin,cjn->cij", c_spans, b_spans, precision=HIGH)
    mixing = weights_l * scores[:, None]
    scaled_in = values_c * step_c[..., None]
    y_intra = jnp.einsum("chij,cjhp->cihp", mixing, scaled_in, precision=HIGH)
    carried = jnp.zeros((heads, head_dim, state_dim), jnp.float32)
    before_seg = jnp.int32(-1)
    linked = (seg_c[0] == before_seg).astype(jnp.float32)
    reach = jnp.exp(cumul[0]) * linked[:, None]
    inter = jnp.einsum("in,hpn->ihp", c_spans[0], carried, precision=HIGH) * reach[:, :, None]
    pieces = [y_intra[0] + inter]
    y_all = jnp.concatenate(pieces, axis=0) + skip_gain[None, :, None] * values
    gated_pre = y_all.reshape(count, inner) * jax.nn.silu(gate_part)
    scaling = lax.rsqrt(jnp.mean(gated_pre * gated_pre, axis=1, keepdims=True) + EPS)
    return gated_pre * scaling * gate_gain[None, :]


def reduce_group(halves, small=None):
    ring = lax.axis_size("shard_0")
    y = lax.axis_index("shard_1")
    z = lax.axis_index("shard_0")
    up = [(i, (i + 1) % ring) for i in range(ring)]
    down = [(i, (i - 1) % ring) for i in range(ring)]
    items = [(halves, jnp.bfloat16)] + ([] if small is None else [(small, jnp.float32)])
    rels, halfs = [], []
    for values, _ in items:
        blocks = values.reshape((ring, 2) + values.shape[1:])
        doubled = jnp.concatenate([blocks, blocks], axis=0)
        rels.append(lax.dynamic_slice_in_dim(doubled, z, ring, axis=0))
        halfs.append(values.shape[1] // 2)

    def send(parts, pairs):
        return [lax.ppermute(p.astype(w), "shard_0", pairs) for p, (_, w) in zip(parts, items)]

    acc_up = send([r[3][:, :h] for r, h in zip(rels, halfs)], up)
    acc_dn = send([r[1][:, h:] for r, h in zip(rels, halfs)], down)
    acc_up = send([a + r[2][:, :h] for a, r, h in zip(acc_up, rels, halfs)], up)
    acc_dn = send([a + r[2][:, h:] for a, r, h in zip(acc_dn, rels, halfs)], down)
    acc_up = send([a + r[1][:, :h] for a, r, h in zip(acc_up, rels, halfs)], up)
    acc_dn = send([a + r[3][:, h:] for a, r, h in zip(acc_dn, rels, halfs)], down)
    results = []
    for au, ad, r, h, (_, w) in zip(acc_up, acc_dn, rels, halfs, items):
        zsum = jnp.concatenate(
            [au.astype(jnp.float32) + r[0][:, :h], ad.astype(jnp.float32) + r[0][:, h:]], axis=1
        )
        keep = lax.dynamic_index_in_dim(zsum, y, axis=0, keepdims=False)
        give = lax.dynamic_index_in_dim(zsum, 1 - y, axis=0, keepdims=False)
        got = lax.ppermute(give.astype(w), "shard_1", [(0, 1), (1, 0)])
        results.append(keep + got.astype(jnp.float32))
    return results[0] if small is None else results


def allreduce_rep(values):
    ring = 4
    size = lax.axis_size("rep_hi")
    index = lax.axis_index("rep_hi")
    x = index % ring
    up = [(i, (i // ring) * ring + (i % ring + 1) % ring) for i in range(size)]
    down = [(i, (i // ring) * ring + (i % ring - 1) % ring) for i in range(size)]
    rows = values.shape[0]
    chunks = values.reshape(ring, rows // ring, values.shape[1])
    doubled = jnp.concatenate([chunks, chunks], axis=0)
    rel = lax.dynamic_slice_in_dim(doubled, x, ring, axis=0)
    half = rows // ring // 2
    a = lax.ppermute(rel[2][:half], "rep_hi", up)
    b = lax.ppermute(rel[2][half:], "rep_hi", down)
    up_msg = jnp.concatenate([a + rel[1][:half], rel[1][half:]], axis=0)
    down_msg = jnp.concatenate([rel[3][:half], b + rel[3][half:]], axis=0)
    mine = rel[0] + lax.ppermute(up_msg, "rep_hi", up) + lax.ppermute(down_msg, "rep_hi", down)
    step = ring
    while step < size:
        mine = mine + lax.ppermute(mine, "rep_hi", [(i, i ^ step) for i in range(size)])
        step *= 2
    from_prev = lax.ppermute(mine, "rep_hi", up)
    from_next = lax.ppermute(mine, "rep_hi", down)
    far_a = lax.ppermute(from_prev[:half], "rep_hi", up)
    far_b = lax.ppermute(from_next[half:], "rep_hi", down)
    opposite = jnp.concatenate([far_a, far_b], axis=0)
    ordered = jnp.stack([mine, from_next, opposite, from_prev])
    doubled = jnp.concatenate([ordered, ordered], axis=0)
    placed = lax.dynamic_slice_in_dim(doubled, (ring - x) % ring, ring, axis=0)
    return placed.reshape(values.shape)


def core_join(owned):
    core = lax.axis_index("core")
    other = core_swap(owned)
    first = jnp.where(core == 0, owned, other)
    second = jnp.where(core == 0, other, owned)
    return jnp.concatenate([first, second], axis=0)


def core_swap(values):
    return lax.ppermute(values, "core", [(0, 1), (1, 0)])


def gather_group(block):
    ring = lax.axis_size("shard_0")
    y = lax.axis_index("shard_1")
    z = lax.axis_index("shard_0")
    other_y = lax.ppermute(block, "shard_1", [(0, 1), (1, 0)])
    pair = jnp.where(y == 0, jnp.stack([block, other_y]), jnp.stack([other_y, block]))
    up = [(i, (i + 1) % ring) for i in range(ring)]
    down = [(i, (i - 1) % ring) for i in range(ring)]
    from_prev = lax.ppermute(pair, "shard_0", up)
    from_next = lax.ppermute(pair, "shard_0", down)
    half = block.shape[0] // 2
    far_a = lax.ppermute(from_prev[:, :half], "shard_0", up)
    far_b = lax.ppermute(from_next[:, half:], "shard_0", down)
    opposite = jnp.concatenate([far_a, far_b], axis=1)
    ordered = jnp.stack([pair, from_next, opposite, from_prev])
    doubled = jnp.concatenate([ordered, ordered], axis=0)
    start = (ring - z) % ring
    placed = lax.dynamic_slice_in_dim(doubled, start, ring, axis=0)
    return placed.reshape((ring * 2,) + block.shape)


def core_swap(values):
    return lax.ppermute(values, "core", [(0, 1), (1, 0)])


def gather_rows(weight, by_permutes=False):
    rows = weight.shape[0]
    half = rows // 2
    core = lax.axis_index("core")
    mine = lax.dynamic_slice_in_dim(weight, core * half, half, axis=0)
    if by_permutes:
        part = gather_group(mine)
    else:
        part = lax.all_gather(mine, SHARD, axis=0, tiled=False)
    other = core_swap(part)
    return part.reshape(-1, weight.shape[1]), other.reshape(-1, weight.shape[1])


def split_cols(values, groups):
    core = lax.axis_index("core")
    blocks = values.reshape(values.shape[0], groups, 2, -1)
    own = lax.dynamic_index_in_dim(blocks, core, axis=2, keepdims=False)
    other = lax.dynamic_index_in_dim(blocks, 1 - core, axis=2, keepdims=False)
    return own.reshape(values.shape[0], -1), other.reshape(values.shape[0], -1)


def join_cols(own, other, groups):
    core = lax.axis_index("core")
    count = own.shape[0]
    pair = jnp.stack([own.reshape(count, groups, -1), other.reshape(count, groups, -1)], axis=2)
    doubled = jnp.concatenate([pair, pair], axis=2)
    placed = lax.dynamic_slice_in_dim(doubled, core, 2, axis=2)
    return placed.reshape(count, -1)


def halves_product(left, halves, groups):
    own_l, other_l = split_cols(left, groups)
    own_w, other_w = halves
    return jnp.dot(own_l, own_w, preferred_element_type=jnp.float32) + jnp.dot(
        other_l, other_w, preferred_element_type=jnp.float32
    )


def halves_back(left, halves, groups):
    own_w, other_w = halves
    return join_cols(back_product(left, own_w), back_product(left, other_w), groups)


def reduce_core(partial):
    groups = lax.axis_size(SHARD)
    cols = partial.shape[1]
    core = lax.axis_index("core")
    blocks = partial.reshape(groups, 2, -1, cols)
    keep = lax.dynamic_index_in_dim(blocks, core, axis=1, keepdims=False)
    give = lax.dynamic_index_in_dim(blocks, 1 - core, axis=1, keepdims=False)
    return keep + core_swap(give)


def reduce_rest(halves, wait_for=None):
    core = lax.axis_index("core")
    owned = reduce_group(halves)
    if wait_for is not None:
        owned, wait_for = lax.optimization_barrier((owned, wait_for))
    owned = lax.psum(owned, "rep_hi")
    other = core_swap(owned)
    first = jnp.where(core == 0, owned, other)
    second = jnp.where(core == 0, other, owned)
    return jnp.concatenate([first, second], axis=0)


def reduce_rows(partial, wait_for=None):
    return reduce_rest(reduce_core(partial), wait_for)


def exchange_sum(values, axes):
    for axis in axes:
        size = lax.axis_size(axis)
        step = 1
        while step < size:
            pairs = [(i, i ^ step) for i in range(size)]
            values = values + lax.ppermute(values, axis, pairs)
            step *= 2
    return values


def on_device(
    layer_in,
    cotangent,
    seq_lengths,
    norm_gain,
    in_weight,
    conv_weight,
    conv_bias,
    step_bias,
    decay_log,
    skip_gain,
    gate_gain,
    out_weight,
):
    count = layer_in.shape[0]
    groups = lax.axis_size(SHARD)
    segment = segment_ids(seq_lengths[0], count)
    smalls = (norm_gain, conv_weight, conv_bias, step_bias, decay_log, skip_gain, gate_gain)
    flat = jnp.concatenate([a.reshape(-1) for a in smalls])
    flat_len = flat.shape[0]
    place = lax.axis_index(SHARD)
    spread = jnp.where(
        (jnp.arange(groups, dtype=jnp.int32) == place)[:, None], flat[None, :], 0.0
    )
    flat_all = exchange_sum(spread, ("shard_1", "shard_0"))
    pieces_full = []
    offset = 0
    for a in smalls:
        size = a.size
        block = flat_all[:, offset : offset + size]
        pieces_full.append(block.reshape((groups * a.shape[0],) + a.shape[1:]))
        offset += size
    norm_full, convw_full, convb_full, stepb_full, decay_full, skip_full, gategain_full = pieces_full
    normed_f, norm_back = jax.vjp(norm_input, layer_in, norm_full)
    normed = normed_f.astype(jnp.bfloat16)
    in_whole = gather_rows(in_weight, by_permutes=True)
    out_whole = gather_rows(out_weight)
    projected = halves_product(normed, in_whole, groups)

    def bound_mixer(proj_arg, cw_arg, cb_arg, sb_arg, dl_arg, sk_arg, gg_arg):
        return mixer(proj_arg, segment, cw_arg, cb_arg, sb_arg, dl_arg, sk_arg, gg_arg)

    gated_f, mixer_back = jax.vjp(
        bound_mixer,
        projected,
        convw_full,
        convb_full,
        stepb_full,
        decay_full,
        skip_full,
        gategain_full,
    )
    gated = gated_f.astype(jnp.bfloat16)
    branch_out = halves_product(gated, out_whole, groups)
    layer_out = layer_in + branch_out
    cot_low = cotangent.astype(jnp.bfloat16)
    out_halves = reduce_core(row_product(gated, cot_low))
    gated_grad = halves_back(cot_low, out_whole, groups)
    out_halves, gated_grad = lax.optimization_barrier((out_halves, gated_grad))
    out_group = reduce_group(out_halves)
    proj_grad, g_convw, g_convb, g_stepb, g_decay, g_skip, g_gategain = mixer_back(gated_grad)
    proj_low = proj_grad.astype(jnp.bfloat16)
    normed_grad = halves_back(proj_low, in_whole, groups)
    back_in, g_norm = norm_back(normed_grad)
    input_grad = cotangent + back_in
    grads = (g_norm, g_convw, g_convb, g_stepb, g_decay, g_skip, g_gategain)
    small_blocks = jnp.concatenate([g.reshape(groups, -1) for g in grads], axis=1)
    small_len = small_blocks.shape[1]
    small_rows = -(-small_len // 2048) * 16
    small_blocks = jnp.pad(small_blocks, ((0, 0), (0, small_rows * 128 - small_len)))
    small_blocks = small_blocks.reshape(groups, small_rows, 128)
    small_blocks = small_blocks + core_swap(small_blocks)
    cols = proj_low.shape[1]
    wide = -(-cols // 128) * 128
    proj_wide = jnp.pad(proj_low, ((0, 0), (0, wide - cols)))
    in_group, small_group = reduce_group(
        reduce_core(row_product(normed, proj_wide)), small_blocks
    )
    in_shape, out_shape = in_group.shape, out_group.shape
    big_rows = (in_group.size + out_group.size) // 128
    tail_rows = -(-(big_rows + small_group.shape[0]) // 64) * 64 - big_rows
    small_group = jnp.pad(small_group, ((0, tail_rows - small_group.shape[0]), (0, 0)))
    joined = jnp.concatenate(
        [in_group.reshape(-1, 128), out_group.reshape(-1, 128), small_group], axis=0
    )
    joined = allreduce_rep(joined)
    split_at = in_group.size // 128
    split_out = split_at + out_group.size // 128
    in_owned = core_join(joined[:split_at].reshape(in_shape))[:, :cols]
    out_owned = core_join(joined[split_at:split_out].reshape(out_shape))
    mine = joined[split_out:].reshape(-1)[:small_len]
    small_final = []
    offset = 0
    for g in grads:
        size = g.size // groups
        small_final.append(mine[offset : offset + size].reshape((g.shape[0] // groups,) + g.shape[1:]))
        offset += size
    return (
        layer_out,
        input_grad,
        small_final[0],
        in_owned,
        small_final[1],
        small_final[2],
        small_final[3],
        small_final[4],
        small_final[5],
        small_final[6],
        out_owned,
    )


def solution(mesh):
    split = Mesh(
        mesh.devices.reshape(mesh.shape["rep"] // 2, 2, 4, 2),
        ("rep_hi", "core", "shard_0", "shard_1"),
    )
    in_specs = (
        P(REP_SHARD, None),
        P(REP_SHARD, None),
        P(REP_SHARD, None),
        P(SHARD),
        P(SHARD, None),
        P(SHARD, None),
        P(SHARD),
        P(SHARD),
        P(SHARD),
        P(SHARD),
        P(SHARD),
        P(SHARD, None),
    )
    out_specs = (
        P(REP_SHARD, None),
        P(REP_SHARD, None),
        P(SHARD),
        P(SHARD, None),
        P(SHARD, None),
        P(SHARD),
        P(SHARD),
        P(SHARD),
        P(SHARD),
        P(SHARD),
        P(SHARD, None),
    )
    return jax.shard_map(
        on_device, mesh=split, in_specs=in_specs, out_specs=out_specs, check_vma=False
    )
```

```python
import math

import jax
import jax.numpy as jnp
from jax import lax
from jax.sharding import Mesh
from jax.sharding import PartitionSpec as P

SPAN = 256
SHARD = ("shard_0", "shard_1")
REP = ("rep_hi", "core")
REP_SHARD = ("rep_hi", "core", "shard_0", "shard_1")
ALL = REP_SHARD


EPS = 1e-05
HIGH = lax.Precision.HIGHEST


def side_by_side(arrays, axis, dim, along):
    widths = [math.prod(a.shape[along:]) for a in arrays]
    both = jnp.concatenate(
        [a.reshape(*a.shape[:along], w) for a, w in zip(arrays, widths)], axis=along
    )
    result = lax.all_gather(both, axis, axis=dim, tiled=True)
    blocks = jnp.split(result, [sum(widths[:k]) for k in range(1, len(widths))], axis=along)
    return tuple(
        (b.reshape(*result.shape[:along], *a.shape[along:]) for a, b in zip(arrays, blocks))
    )


def sum_by_axis(total, axes):
    for axis in axes:
        total = lax.psum_scatter(total, axis, scatter_dimension=0, tiled=True)
    return total


def in_blocks(shard, dim, size):
    before, after = (shard.shape[:dim], shard.shape[dim + 1 :])
    return jnp.moveaxis(shard.reshape(*before, size, -1, *after), dim, 0)


def sum_at_owner(shard, axis, dim):
    size = lax.axis_size(axis)
    blocks = lax.all_to_all(in_blocks(shard, dim, size), axis, 0, 0, tiled=True)
    return jnp.sum(blocks, axis=0)


def sent_together(arrays, axis, dim, along):
    widths = [math.prod(a.shape[along:]) for a in arrays]
    both = jnp.concatenate(
        [a.reshape(*a.shape[:along], w) for a, w in zip(arrays, widths)], axis=along
    )
    result = sum_at_owner(both, axis, dim)
    blocks = jnp.split(result, [sum(widths[:k]) for k in range(1, len(widths))], axis=along)
    return tuple(
        (b.reshape(*result.shape[:along], *a.shape[along:]) for a, b in zip(arrays, blocks))
    )


def shifted(values, lag):
    zeros_top = jnp.zeros((lag,) + values.shape[1:], values.dtype)
    return jnp.concatenate([zeros_top, values[:-lag]], axis=0)


def segment_ids(lengths_row, count):
    offsets = jnp.cumsum(lengths_row, dtype=jnp.int32) - lengths_row
    places = jnp.arange(count, dtype=jnp.int32)
    return (
        jnp.sum((places[:, None] >= offsets[None, :]).astype(jnp.int32), axis=1, dtype=jnp.int32)
        - 1
    )


def row_product(left, right):
    return lax.dot_general(
        left, right, (((0,), (0,)), ((), ())), preferred_element_type=jnp.float32
    )


def back_product(left, right):
    return lax.dot_general(
        left, right, (((1,), (1,)), ((), ())), preferred_element_type=jnp.float32
    )


def norm_input(inputs, gain_one):
    scaling = lax.rsqrt(jnp.mean(inputs * inputs, axis=1, keepdims=True) + EPS)
    return inputs * scaling * gain_one[None, :]


def mixer(projected, segment, conv_weight, conv_bias, step_bias, decay_log, skip_gain, gate_gain):
    count = projected.shape[0]
    inner = gate_gain.shape[0]
    heads = step_bias.shape[0]
    head_dim = inner // heads
    channels = conv_weight.shape[0]
    state_dim = (channels - inner) // 2
    taps = conv_weight.shape[1]
    gate_part = projected[:, :inner]
    conv_in = projected[:, inner : inner + channels]
    step_raw = projected[:, inner + channels :]
    places = jnp.arange(count, dtype=jnp.int32)
    conv_out = conv_bias[None, :] + conv_weight[:, taps - 1][None, :] * conv_in
    for lag in range(1, taps):
        same = (shifted(segment, lag) == segment) & (places >= lag)
        conv_out = conv_out + jnp.where(
            same[:, None], conv_weight[:, taps - 1 - lag][None, :] * shifted(conv_in, lag), 0.0
        )
    activated = jax.nn.silu(conv_out)
    values = activated[:, :inner].reshape(count, heads, head_dim)
    b_matrix = activated[:, inner : inner + state_dim]
    c_matrix = activated[:, inner + state_dim :]
    step_size = jax.nn.softplus(step_raw + step_bias[None, :])
    decay = -jnp.exp(decay_log)[None, :] * step_size
    blocks = count // SPAN
    values_c = values.reshape(blocks, SPAN, heads, head_dim)
    b_spans = b_matrix.reshape(blocks, SPAN, state_dim)
    c_spans = c_matrix.reshape(blocks, SPAN, state_dim)
    step_c = step_size.reshape(blocks, SPAN, heads)
    cumul = jnp.cumsum(decay.reshape(blocks, SPAN, heads), axis=1)
    seg_c = segment.reshape(blocks, SPAN)
    rows_in = jnp.arange(SPAN, dtype=jnp.int32)
    lower = rows_in[:, None] >= rows_in[None, :]
    allowed = lower[None] & (seg_c[:, :, None] == seg_c[:, None, :])
    cumul_t = jnp.transpose(cumul, (0, 2, 1))
    differ = cumul_t[:, :, :, None] - cumul_t[:, :, None, :]
    weights_l = jnp.exp(jnp.where(allowed[:, None], differ, -10000.0))
    scores = jnp.einsum("cin,cjn->cij", c_spans, b_spans, precision=HIGH)
    mixing = weights_l * scores[:, None]
    scaled_in = values_c * step_c[..., None]
    y_intra = jnp.einsum("chij,cjhp->cihp", mixing, scaled_in, precision=HIGH)
    carried = jnp.zeros((heads, head_dim, state_dim), jnp.float32)
    before_seg = jnp.int32(-1)
    linked = (seg_c[0] == before_seg).astype(jnp.float32)
    reach = jnp.exp(cumul[0]) * linked[:, None]
    inter = jnp.einsum("in,hpn->ihp", c_spans[0], carried, precision=HIGH) * reach[:, :, None]
    pieces = [y_intra[0] + inter]
    y_all = jnp.concatenate(pieces, axis=0) + skip_gain[None, :, None] * values
    gated_pre = y_all.reshape(count, inner) * jax.nn.silu(gate_part)
    scaling = lax.rsqrt(jnp.mean(gated_pre * gated_pre, axis=1, keepdims=True) + EPS)
    return gated_pre * scaling * gate_gain[None, :]


def reduce_group(halves, small=None):
    ring = lax.axis_size("shard_0")
    y = lax.axis_index("shard_1")
    z = lax.axis_index("shard_0")
    up = [(i, (i + 1) % ring) for i in range(ring)]
    down = [(i, (i - 1) % ring) for i in range(ring)]
    items = [(halves, jnp.bfloat16)] + ([] if small is None else [(small, jnp.float32)])
    rels, halfs = [], []
    for values, _ in items:
        blocks = values.reshape((ring, 2) + values.shape[1:])
        doubled = jnp.concatenate([blocks, blocks], axis=0)
        rels.append(lax.dynamic_slice_in_dim(doubled, z, ring, axis=0))
        halfs.append(values.shape[1] // 2)

    def send(parts, pairs):
        return [lax.ppermute(p.astype(w), "shard_0", pairs) for p, (_, w) in zip(parts, items)]

    acc_up = send([r[3][:, :h] for r, h in zip(rels, halfs)], up)
    acc_dn = send([r[1][:, h:] for r, h in zip(rels, halfs)], down)
    acc_up = send([a + r[2][:, :h] for a, r, h in zip(acc_up, rels, halfs)], up)
    acc_dn = send([a + r[2][:, h:] for a, r, h in zip(acc_dn, rels, halfs)], down)
    acc_up = send([a + r[1][:, :h] for a, r, h in zip(acc_up, rels, halfs)], up)
    acc_dn = send([a + r[3][:, h:] for a, r, h in zip(acc_dn, rels, halfs)], down)
    results = []
    for au, ad, r, h, (_, w) in zip(acc_up, acc_dn, rels, halfs, items):
        zsum = jnp.concatenate(
            [au.astype(jnp.float32) + r[0][:, :h], ad.astype(jnp.float32) + r[0][:, h:]], axis=1
        )
        keep = lax.dynamic_index_in_dim(zsum, y, axis=0, keepdims=False)
        give = lax.dynamic_index_in_dim(zsum, 1 - y, axis=0, keepdims=False)
        got = lax.ppermute(give.astype(w), "shard_1", [(0, 1), (1, 0)])
        results.append(keep + got.astype(jnp.float32))
    return results[0] if small is None else results


def allreduce_rep(values):
    ring = 4
    size = lax.axis_size("rep_hi")
    index = lax.axis_index("rep_hi")
    x = index % ring
    up = [(i, (i // ring) * ring + (i % ring + 1) % ring) for i in range(size)]
    down = [(i, (i // ring) * ring + (i % ring - 1) % ring) for i in range(size)]
    rows = values.shape[0]
    chunks = values.reshape(ring, rows // ring, values.shape[1])
    doubled = jnp.concatenate([chunks, chunks], axis=0)
    rel = lax.dynamic_slice_in_dim(doubled, x, ring, axis=0)
    half = rows // ring // 2
    a = lax.ppermute(rel[2][:half], "rep_hi", up)
    b = lax.ppermute(rel[2][half:], "rep_hi", down)
    up_msg = jnp.concatenate([a + rel[1][:half], rel[1][half:]], axis=0)
    down_msg = jnp.concatenate([rel[3][:half], b + rel[3][half:]], axis=0)
    mine = rel[0] + lax.ppermute(up_msg, "rep_hi", up) + lax.ppermute(down_msg, "rep_hi", down)
    step = ring
    while step < size:
        mine = mine + lax.ppermute(mine, "rep_hi", [(i, i ^ step) for i in range(size)])
        step *= 2
    from_prev = lax.ppermute(mine, "rep_hi", up)
    from_next = lax.ppermute(mine, "rep_hi", down)
    far_a = lax.ppermute(from_prev[:half], "rep_hi", up)
    far_b = lax.ppermute(from_next[half:], "rep_hi", down)
    opposite = jnp.concatenate([far_a, far_b], axis=0)
    ordered = jnp.stack([mine, from_next, opposite, from_prev])
    doubled = jnp.concatenate([ordered, ordered], axis=0)
    placed = lax.dynamic_slice_in_dim(doubled, (ring - x) % ring, ring, axis=0)
    return placed.reshape(values.shape)


def core_join(owned):
    core = lax.axis_index("core")
    other = core_swap(owned)
    first = jnp.where(core == 0, owned, other)
    second = jnp.where(core == 0, other, owned)
    return jnp.concatenate([first, second], axis=0)


def core_swap(values):
    return lax.ppermute(values, "core", [(0, 1), (1, 0)])


def gather_group(block, sibling):
    ring = lax.axis_size("shard_0")
    y = lax.axis_index("shard_1")
    z = lax.axis_index("shard_0")
    up = [(i, (i + 1) % ring) for i in range(ring)]
    down = [(i, (i - 1) % ring) for i in range(ring)]
    half = block.shape[0] // 2

    def place(own, got):
        return jnp.where(y == 0, jnp.stack([own, got]), jnp.stack([got, own]))

    def arrange(pair, from_next, opposite, from_prev):
        ordered = jnp.stack([pair, from_next, opposite, from_prev])
        doubled = jnp.concatenate([ordered, ordered], axis=0)
        placed = lax.dynamic_slice_in_dim(doubled, (ring - z) % ring, ring, axis=0)
        return placed.reshape((ring * 2,) + block.shape)

    other_y = lax.ppermute(block, "shard_1", [(0, 1), (1, 0)])
    pair = place(block, other_y)
    from_prev = lax.ppermute(pair, "shard_0", up)
    from_next = lax.ppermute(pair, "shard_0", down)
    pair_s = place(sibling, core_swap(other_y))
    far_a = lax.ppermute(from_prev[:, :half], "shard_0", up)
    far_b = lax.ppermute(from_next[:, half:], "shard_0", down)
    from_prev_s = core_swap(from_prev)
    from_next_s = core_swap(from_next)
    opposite = jnp.concatenate([far_a, far_b], axis=1)
    opposite_s = core_swap(opposite)
    return (
        arrange(pair, from_next, opposite, from_prev),
        arrange(pair_s, from_next_s, opposite_s, from_prev_s),
    )


def core_swap(values):
    return lax.ppermute(values, "core", [(0, 1), (1, 0)])


def gather_rows(weight, by_permutes=False):
    rows = weight.shape[0]
    half = rows // 2
    core = lax.axis_index("core")
    mine = lax.dynamic_slice_in_dim(weight, core * half, half, axis=0)
    if by_permutes:
        sibling = lax.dynamic_slice_in_dim(weight, (1 - core) * half, half, axis=0)
        part, other = gather_group(mine, sibling)
    else:
        part = lax.all_gather(mine, SHARD, axis=0, tiled=False)
        other = core_swap(part)
    return part.reshape(-1, weight.shape[1]), other.reshape(-1, weight.shape[1])


def split_cols(values, groups):
    core = lax.axis_index("core")
    blocks = values.reshape(values.shape[0], groups, 2, -1)
    own = lax.dynamic_index_in_dim(blocks, core, axis=2, keepdims=False)
    other = lax.dynamic_index_in_dim(blocks, 1 - core, axis=2, keepdims=False)
    return own.reshape(values.shape[0], -1), other.reshape(values.shape[0], -1)


def join_cols(own, other, groups):
    core = lax.axis_index("core")
    count = own.shape[0]
    pair = jnp.stack([own.reshape(count, groups, -1), other.reshape(count, groups, -1)], axis=2)
    doubled = jnp.concatenate([pair, pair], axis=2)
    placed = lax.dynamic_slice_in_dim(doubled, core, 2, axis=2)
    return placed.reshape(count, -1)


def halves_product(left, halves, groups):
    own_l, other_l = split_cols(left, groups)
    own_w, other_w = halves
    return jnp.dot(own_l, own_w, preferred_element_type=jnp.float32) + jnp.dot(
        other_l, other_w, preferred_element_type=jnp.float32
    )


def halves_back(left, halves, groups):
    own_w, other_w = halves
    return join_cols(back_product(left, own_w), back_product(left, other_w), groups)


def reduce_core(partial):
    groups = lax.axis_size(SHARD)
    cols = partial.shape[1]
    core = lax.axis_index("core")
    blocks = partial.reshape(groups, 2, -1, cols)
    keep = lax.dynamic_index_in_dim(blocks, core, axis=1, keepdims=False)
    give = lax.dynamic_index_in_dim(blocks, 1 - core, axis=1, keepdims=False)
    return keep + core_swap(give)


def reduce_rest(halves, wait_for=None):
    core = lax.axis_index("core")
    owned = reduce_group(halves)
    if wait_for is not None:
        owned, wait_for = lax.optimization_barrier((owned, wait_for))
    owned = lax.psum(owned, "rep_hi")
    other = core_swap(owned)
    first = jnp.where(core == 0, owned, other)
    second = jnp.where(core == 0, other, owned)
    return jnp.concatenate([first, second], axis=0)


def reduce_rows(partial, wait_for=None):
    return reduce_rest(reduce_core(partial), wait_for)


def exchange_sum(values, axes):
    for axis in axes:
        size = lax.axis_size(axis)
        step = 1
        while step < size:
            pairs = [(i, i ^ step) for i in range(size)]
            values = values + lax.ppermute(values, axis, pairs)
            step *= 2
    return values


def on_device(
    layer_in,
    cotangent,
    seq_lengths,
    norm_gain,
    in_weight,
    conv_weight,
    conv_bias,
    step_bias,
    decay_log,
    skip_gain,
    gate_gain,
    out_weight,
):
    count = layer_in.shape[0]
    groups = lax.axis_size(SHARD)
    segment = segment_ids(seq_lengths[0], count)
    smalls = (norm_gain, conv_weight, conv_bias, step_bias, decay_log, skip_gain, gate_gain)
    flat = jnp.concatenate([a.reshape(-1) for a in smalls])
    flat_len = flat.shape[0]
    place = lax.axis_index(SHARD)
    spread = jnp.where(
        (jnp.arange(groups, dtype=jnp.int32) == place)[:, None], flat[None, :], 0.0
    )
    flat_all = exchange_sum(spread, ("shard_1", "shard_0"))
    pieces_full = []
    offset = 0
    for a in smalls:
        size = a.size
        block = flat_all[:, offset : offset + size]
        pieces_full.append(block.reshape((groups * a.shape[0],) + a.shape[1:]))
        offset += size
    norm_full, convw_full, convb_full, stepb_full, decay_full, skip_full, gategain_full = pieces_full
    normed_f, norm_back = jax.vjp(norm_input, layer_in, norm_full)
    normed = normed_f.astype(jnp.bfloat16)
    in_whole = gather_rows(in_weight, by_permutes=True)
    out_whole = gather_rows(out_weight)
    projected = halves_product(normed, in_whole, groups)

    def bound_mixer(proj_arg, cw_arg, cb_arg, sb_arg, dl_arg, sk_arg, gg_arg):
        return mixer(proj_arg, segment, cw_arg, cb_arg, sb_arg, dl_arg, sk_arg, gg_arg)

    gated_f, mixer_back = jax.vjp(
        bound_mixer,
        projected,
        convw_full,
        convb_full,
        stepb_full,
        decay_full,
        skip_full,
        gategain_full,
    )
    gated = gated_f.astype(jnp.bfloat16)
    branch_out = halves_product(gated, out_whole, groups)
    layer_out = layer_in + branch_out
    cot_low = cotangent.astype(jnp.bfloat16)
    out_halves = reduce_core(row_product(gated, cot_low))
    gated_grad = halves_back(cot_low, out_whole, groups)
    out_halves, gated_grad = lax.optimization_barrier((out_halves, gated_grad))
    out_group = reduce_group(out_halves)
    proj_grad, g_convw, g_convb, g_stepb, g_decay, g_skip, g_gategain = mixer_back(gated_grad)
    proj_low = proj_grad.astype(jnp.bfloat16)
    normed_grad = halves_back(proj_low, in_whole, groups)
    back_in, g_norm = norm_back(normed_grad)
    input_grad = cotangent + back_in
    grads = (g_norm, g_convw, g_convb, g_stepb, g_decay, g_skip, g_gategain)
    small_blocks = jnp.concatenate([g.reshape(groups, -1) for g in grads], axis=1)
    small_len = small_blocks.shape[1]
    small_rows = -(-small_len // 2048) * 16
    small_blocks = jnp.pad(small_blocks, ((0, 0), (0, small_rows * 128 - small_len)))
    small_blocks = small_blocks.reshape(groups, small_rows, 128)
    small_blocks = small_blocks + core_swap(small_blocks)
    cols = proj_low.shape[1]
    wide = -(-cols // 128) * 128
    proj_wide = jnp.pad(proj_low, ((0, 0), (0, wide - cols)))
    in_group, small_group = reduce_group(
        reduce_core(row_product(normed, proj_wide)), small_blocks
    )
    in_shape, out_shape = in_group.shape, out_group.shape
    big_rows = (in_group.size + out_group.size) // 128
    tail_rows = -(-(big_rows + small_group.shape[0]) // 64) * 64 - big_rows
    small_group = jnp.pad(small_group, ((0, tail_rows - small_group.shape[0]), (0, 0)))
    joined = jnp.concatenate(
        [in_group.reshape(-1, 128), out_group.reshape(-1, 128), small_group], axis=0
    )
    joined = allreduce_rep(joined)
    split_at = in_group.size // 128
    split_out = split_at + out_group.size // 128
    in_owned = core_join(joined[:split_at].reshape(in_shape))[:, :cols]
    out_owned = core_join(joined[split_at:split_out].reshape(out_shape))
    mine = joined[split_out:].reshape(-1)[:small_len]
    small_final = []
    offset = 0
    for g in grads:
        size = g.size // groups
        small_final.append(mine[offset : offset + size].reshape((g.shape[0] // groups,) + g.shape[1:]))
        offset += size
    return (
        layer_out,
        input_grad,
        small_final[0],
        in_owned,
        small_final[1],
        small_final[2],
        small_final[3],
        small_final[4],
        small_final[5],
        small_final[6],
        out_owned,
    )


def solution(mesh):
    split = Mesh(
        mesh.devices.reshape(mesh.shape["rep"] // 2, 2, 4, 2),
        ("rep_hi", "core", "shard_0", "shard_1"),
    )
    in_specs = (
        P(REP_SHARD, None),
        P(REP_SHARD, None),
        P(REP_SHARD, None),
        P(SHARD),
        P(SHARD, None),
        P(SHARD, None),
        P(SHARD),
        P(SHARD),
        P(SHARD),
        P(SHARD),
        P(SHARD),
        P(SHARD, None),
    )
    out_specs = (
        P(REP_SHARD, None),
        P(REP_SHARD, None),
        P(SHARD),
        P(SHARD, None),
        P(SHARD, None),
        P(SHARD),
        P(SHARD),
        P(SHARD),
        P(SHARD),
        P(SHARD),
        P(SHARD, None),
    )
    return jax.shard_map(
        on_device, mesh=split, in_specs=in_specs, out_specs=out_specs, check_vma=False
    )
```

```python
import math

import jax
import jax.numpy as jnp
from jax import lax
from jax.sharding import Mesh
from jax.sharding import PartitionSpec as P

SPAN = 256
SHARD = ("shard_0", "shard_1")
REP = ("rep_hi", "core")
REP_SHARD = ("rep_hi", "core", "shard_0", "shard_1")
ALL = REP_SHARD


EPS = 1e-05
HIGH = lax.Precision.HIGHEST


def side_by_side(arrays, axis, dim, along):
    widths = [math.prod(a.shape[along:]) for a in arrays]
    both = jnp.concatenate(
        [a.reshape(*a.shape[:along], w) for a, w in zip(arrays, widths)], axis=along
    )
    result = lax.all_gather(both, axis, axis=dim, tiled=True)
    blocks = jnp.split(result, [sum(widths[:k]) for k in range(1, len(widths))], axis=along)
    return tuple(
        (b.reshape(*result.shape[:along], *a.shape[along:]) for a, b in zip(arrays, blocks))
    )


def sum_by_axis(total, axes):
    for axis in axes:
        total = lax.psum_scatter(total, axis, scatter_dimension=0, tiled=True)
    return total


def in_blocks(shard, dim, size):
    before, after = (shard.shape[:dim], shard.shape[dim + 1 :])
    return jnp.moveaxis(shard.reshape(*before, size, -1, *after), dim, 0)


def sum_at_owner(shard, axis, dim):
    size = lax.axis_size(axis)
    blocks = lax.all_to_all(in_blocks(shard, dim, size), axis, 0, 0, tiled=True)
    return jnp.sum(blocks, axis=0)


def sent_together(arrays, axis, dim, along):
    widths = [math.prod(a.shape[along:]) for a in arrays]
    both = jnp.concatenate(
        [a.reshape(*a.shape[:along], w) for a, w in zip(arrays, widths)], axis=along
    )
    result = sum_at_owner(both, axis, dim)
    blocks = jnp.split(result, [sum(widths[:k]) for k in range(1, len(widths))], axis=along)
    return tuple(
        (b.reshape(*result.shape[:along], *a.shape[along:]) for a, b in zip(arrays, blocks))
    )


def shifted(values, lag):
    zeros_top = jnp.zeros((lag,) + values.shape[1:], values.dtype)
    return jnp.concatenate([zeros_top, values[:-lag]], axis=0)


def segment_ids(lengths_row, count):
    offsets = jnp.cumsum(lengths_row, dtype=jnp.int32) - lengths_row
    places = jnp.arange(count, dtype=jnp.int32)
    return (
        jnp.sum((places[:, None] >= offsets[None, :]).astype(jnp.int32), axis=1, dtype=jnp.int32)
        - 1
    )


def row_product(left, right):
    return lax.dot_general(
        left, right, (((0,), (0,)), ((), ())), preferred_element_type=jnp.float32
    )


def back_product(left, right):
    return lax.dot_general(
        left, right, (((1,), (1,)), ((), ())), preferred_element_type=jnp.float32
    )


def norm_input(inputs, gain_one):
    scaling = lax.rsqrt(jnp.mean(inputs * inputs, axis=1, keepdims=True) + EPS)
    return inputs * scaling * gain_one[None, :]


def mixer(projected, segment, conv_weight, conv_bias, step_bias, decay_log, skip_gain, gate_gain):
    count = projected.shape[0]
    inner = gate_gain.shape[0]
    heads = step_bias.shape[0]
    head_dim = inner // heads
    channels = conv_weight.shape[0]
    state_dim = (channels - inner) // 2
    taps = conv_weight.shape[1]
    gate_part = projected[:, :inner]
    conv_in = projected[:, inner : inner + channels]
    step_raw = projected[:, inner + channels :]
    places = jnp.arange(count, dtype=jnp.int32)
    conv_out = conv_bias[None, :] + conv_weight[:, taps - 1][None, :] * conv_in
    for lag in range(1, taps):
        same = (shifted(segment, lag) == segment) & (places >= lag)
        conv_out = conv_out + jnp.where(
            same[:, None], conv_weight[:, taps - 1 - lag][None, :] * shifted(conv_in, lag), 0.0
        )
    activated = jax.nn.silu(conv_out)
    values = activated[:, :inner].reshape(count, heads, head_dim)
    b_matrix = activated[:, inner : inner + state_dim]
    c_matrix = activated[:, inner + state_dim :]
    step_size = jax.nn.softplus(step_raw + step_bias[None, :])
    decay = -jnp.exp(decay_log)[None, :] * step_size
    blocks = count // SPAN
    values_c = values.reshape(blocks, SPAN, heads, head_dim)
    b_spans = b_matrix.reshape(blocks, SPAN, state_dim)
    c_spans = c_matrix.reshape(blocks, SPAN, state_dim)
    step_c = step_size.reshape(blocks, SPAN, heads)
    cumul = jnp.cumsum(decay.reshape(blocks, SPAN, heads), axis=1)
    seg_c = segment.reshape(blocks, SPAN)
    rows_in = jnp.arange(SPAN, dtype=jnp.int32)
    lower = rows_in[:, None] >= rows_in[None, :]
    allowed = lower[None] & (seg_c[:, :, None] == seg_c[:, None, :])
    cumul_t = jnp.transpose(cumul, (0, 2, 1))
    differ = cumul_t[:, :, :, None] - cumul_t[:, :, None, :]
    weights_l = jnp.exp(jnp.where(allowed[:, None], differ, -10000.0))
    scores = jnp.einsum("cin,cjn->cij", c_spans, b_spans, precision=HIGH)
    mixing = weights_l * scores[:, None]
    scaled_in = values_c * step_c[..., None]
    y_intra = jnp.einsum("chij,cjhp->cihp", mixing, scaled_in, precision=HIGH)
    carried = jnp.zeros((heads, head_dim, state_dim), jnp.float32)
    before_seg = jnp.int32(-1)
    linked = (seg_c[0] == before_seg).astype(jnp.float32)
    reach = jnp.exp(cumul[0]) * linked[:, None]
    inter = jnp.einsum("in,hpn->ihp", c_spans[0], carried, precision=HIGH) * reach[:, :, None]
    pieces = [y_intra[0] + inter]
    y_all = jnp.concatenate(pieces, axis=0) + skip_gain[None, :, None] * values
    gated_pre = y_all.reshape(count, inner) * jax.nn.silu(gate_part)
    scaling = lax.rsqrt(jnp.mean(gated_pre * gated_pre, axis=1, keepdims=True) + EPS)
    return gated_pre * scaling * gate_gain[None, :]


def reduce_group(halves, small=None):
    ring = lax.axis_size("shard_0")
    y = lax.axis_index("shard_1")
    z = lax.axis_index("shard_0")
    up = [(i, (i + 1) % ring) for i in range(ring)]
    down = [(i, (i - 1) % ring) for i in range(ring)]
    items = [(halves, jnp.bfloat16)] + ([] if small is None else [(small, jnp.float32)])
    rels, halfs = [], []
    for values, _ in items:
        blocks = values.reshape((ring, 2) + values.shape[1:])
        doubled = jnp.concatenate([blocks, blocks], axis=0)
        rels.append(lax.dynamic_slice_in_dim(doubled, z, ring, axis=0))
        halfs.append(values.shape[1] // 2)

    def send(parts, pairs):
        return [lax.ppermute(p.astype(w), "shard_0", pairs) for p, (_, w) in zip(parts, items)]

    acc_up = send([r[3][:, :h] for r, h in zip(rels, halfs)], up)
    acc_dn = send([r[1][:, h:] for r, h in zip(rels, halfs)], down)
    acc_up = send([a + r[2][:, :h] for a, r, h in zip(acc_up, rels, halfs)], up)
    acc_dn = send([a + r[2][:, h:] for a, r, h in zip(acc_dn, rels, halfs)], down)
    acc_up = send([a + r[1][:, :h] for a, r, h in zip(acc_up, rels, halfs)], up)
    acc_dn = send([a + r[3][:, h:] for a, r, h in zip(acc_dn, rels, halfs)], down)
    results = []
    for au, ad, r, h, (_, w) in zip(acc_up, acc_dn, rels, halfs, items):
        zsum = jnp.concatenate(
            [au.astype(jnp.float32) + r[0][:, :h], ad.astype(jnp.float32) + r[0][:, h:]], axis=1
        )
        keep = lax.dynamic_index_in_dim(zsum, y, axis=0, keepdims=False)
        give = lax.dynamic_index_in_dim(zsum, 1 - y, axis=0, keepdims=False)
        got = lax.ppermute(give.astype(w), "shard_1", [(0, 1), (1, 0)])
        results.append(keep + got.astype(jnp.float32))
    return results[0] if small is None else results


def allreduce_rep(values):
    ring = 4
    size = lax.axis_size("rep_hi")
    index = lax.axis_index("rep_hi")
    x = index % ring
    up = [(i, (i // ring) * ring + (i % ring + 1) % ring) for i in range(size)]
    down = [(i, (i // ring) * ring + (i % ring - 1) % ring) for i in range(size)]
    rows = values.shape[0]
    chunks = values.reshape(ring, rows // ring, values.shape[1])
    doubled = jnp.concatenate([chunks, chunks], axis=0)
    rel = lax.dynamic_slice_in_dim(doubled, x, ring, axis=0)
    half = rows // ring // 2
    a = lax.ppermute(rel[2][:half], "rep_hi", up)
    b = lax.ppermute(rel[2][half:], "rep_hi", down)
    up_msg = jnp.concatenate([a + rel[1][:half], rel[1][half:]], axis=0)
    down_msg = jnp.concatenate([rel[3][:half], b + rel[3][half:]], axis=0)
    mine = rel[0] + lax.ppermute(up_msg, "rep_hi", up) + lax.ppermute(down_msg, "rep_hi", down)
    step = ring
    while step < size:
        mine = mine + lax.ppermute(mine, "rep_hi", [(i, i ^ step) for i in range(size)])
        step *= 2
    from_prev = lax.ppermute(mine, "rep_hi", up)
    from_next = lax.ppermute(mine, "rep_hi", down)
    far_a = lax.ppermute(from_prev[:half], "rep_hi", up)
    far_b = lax.ppermute(from_next[half:], "rep_hi", down)
    opposite = jnp.concatenate([far_a, far_b], axis=0)
    ordered = jnp.stack([mine, from_next, opposite, from_prev])
    doubled = jnp.concatenate([ordered, ordered], axis=0)
    placed = lax.dynamic_slice_in_dim(doubled, (ring - x) % ring, ring, axis=0)
    return placed.reshape(values.shape)


def core_join(owned):
    core = lax.axis_index("core")
    other = core_swap(owned)
    first = jnp.where(core == 0, owned, other)
    second = jnp.where(core == 0, other, owned)
    return jnp.concatenate([first, second], axis=0)


def core_swap(values):
    return lax.ppermute(values, "core", [(0, 1), (1, 0)])


def gather_group(block, sibling):
    ring = lax.axis_size("shard_0")
    y = lax.axis_index("shard_1")
    z = lax.axis_index("shard_0")
    up = [(i, (i + 1) % ring) for i in range(ring)]
    down = [(i, (i - 1) % ring) for i in range(ring)]
    half = block.shape[0] // 2

    def place(own, got):
        return jnp.where(y == 0, jnp.stack([own, got]), jnp.stack([got, own]))

    def arrange(pair, from_next, opposite, from_prev):
        ordered = jnp.stack([pair, from_next, opposite, from_prev])
        doubled = jnp.concatenate([ordered, ordered], axis=0)
        placed = lax.dynamic_slice_in_dim(doubled, (ring - z) % ring, ring, axis=0)
        return placed.reshape((ring * 2,) + block.shape)

    other_y = lax.ppermute(block, "shard_1", [(0, 1), (1, 0)])
    pair = place(block, other_y)
    from_prev = lax.ppermute(pair, "shard_0", up)
    from_next = lax.ppermute(pair, "shard_0", down)
    pair_s = place(sibling, core_swap(other_y))
    far_a = lax.ppermute(from_prev[:, :half], "shard_0", up)
    far_b = lax.ppermute(from_next[:, half:], "shard_0", down)
    from_prev_s = core_swap(from_prev)
    from_next_s = core_swap(from_next)
    opposite = jnp.concatenate([far_a, far_b], axis=1)
    opposite_s = core_swap(opposite)
    return (
        arrange(pair, from_next, opposite, from_prev),
        arrange(pair_s, from_next_s, opposite_s, from_prev_s),
    )


def core_swap(values):
    return lax.ppermute(values, "core", [(0, 1), (1, 0)])


def gather_rows(weight, by_permutes=False):
    rows = weight.shape[0]
    half = rows // 2
    core = lax.axis_index("core")
    mine = lax.dynamic_slice_in_dim(weight, core * half, half, axis=0)
    if by_permutes:
        sibling = lax.dynamic_slice_in_dim(weight, (1 - core) * half, half, axis=0)
        part, other = gather_group(mine, sibling)
    else:
        part = lax.all_gather(mine, SHARD, axis=0, tiled=False)
        other = core_swap(part)
    return part.reshape(-1, weight.shape[1]), other.reshape(-1, weight.shape[1])


def split_cols(values, groups):
    core = lax.axis_index("core")
    blocks = values.reshape(values.shape[0], groups, 2, -1)
    own = lax.dynamic_index_in_dim(blocks, core, axis=2, keepdims=False)
    other = lax.dynamic_index_in_dim(blocks, 1 - core, axis=2, keepdims=False)
    return own.reshape(values.shape[0], -1), other.reshape(values.shape[0], -1)


def join_cols(own, other, groups):
    core = lax.axis_index("core")
    count = own.shape[0]
    pair = jnp.stack([own.reshape(count, groups, -1), other.reshape(count, groups, -1)], axis=2)
    doubled = jnp.concatenate([pair, pair], axis=2)
    placed = lax.dynamic_slice_in_dim(doubled, core, 2, axis=2)
    return placed.reshape(count, -1)


def halves_product(left, halves, groups):
    own_l, other_l = split_cols(left, groups)
    own_w, other_w = halves
    return jnp.dot(own_l, own_w, preferred_element_type=jnp.float32) + jnp.dot(
        other_l, other_w, preferred_element_type=jnp.float32
    )


def halves_back(left, halves, groups):
    own_w, other_w = halves
    return join_cols(back_product(left, own_w), back_product(left, other_w), groups)


def reduce_core(partial):
    groups = lax.axis_size(SHARD)
    cols = partial.shape[1]
    core = lax.axis_index("core")
    blocks = partial.reshape(groups, 2, -1, cols)
    keep = lax.dynamic_index_in_dim(blocks, core, axis=1, keepdims=False)
    give = lax.dynamic_index_in_dim(blocks, 1 - core, axis=1, keepdims=False)
    return keep + core_swap(give)


def reduce_rest(halves, wait_for=None):
    core = lax.axis_index("core")
    owned = reduce_group(halves)
    if wait_for is not None:
        owned, wait_for = lax.optimization_barrier((owned, wait_for))
    owned = lax.psum(owned, "rep_hi")
    other = core_swap(owned)
    first = jnp.where(core == 0, owned, other)
    second = jnp.where(core == 0, other, owned)
    return jnp.concatenate([first, second], axis=0)


def reduce_rows(partial, wait_for=None):
    return reduce_rest(reduce_core(partial), wait_for)


def exchange_sum(values, axes):
    for axis in axes:
        size = lax.axis_size(axis)
        step = 1
        while step < size:
            pairs = [(i, i ^ step) for i in range(size)]
            values = values + lax.ppermute(values, axis, pairs)
            step *= 2
    return values


def on_device(
    layer_in,
    cotangent,
    seq_lengths,
    norm_gain,
    in_weight,
    conv_weight,
    conv_bias,
    step_bias,
    decay_log,
    skip_gain,
    gate_gain,
    out_weight,
):
    count = layer_in.shape[0]
    groups = lax.axis_size(SHARD)
    segment = segment_ids(seq_lengths[0], count)
    smalls = (norm_gain, conv_weight, conv_bias, step_bias, decay_log, skip_gain, gate_gain)
    flat = jnp.concatenate([a.reshape(-1) for a in smalls])
    flat_len = flat.shape[0]
    place = lax.axis_index(SHARD)
    spread = jnp.where(
        (jnp.arange(groups, dtype=jnp.int32) == place)[:, None], flat[None, :], 0.0
    )
    flat_all = exchange_sum(spread, ("shard_1", "shard_0"))
    pieces_full = []
    offset = 0
    for a in smalls:
        size = a.size
        block = flat_all[:, offset : offset + size]
        pieces_full.append(block.reshape((groups * a.shape[0],) + a.shape[1:]))
        offset += size
    norm_full, convw_full, convb_full, stepb_full, decay_full, skip_full, gategain_full = pieces_full
    normed_f, norm_back = jax.vjp(norm_input, layer_in, norm_full)
    normed = normed_f.astype(jnp.bfloat16)
    in_whole = gather_rows(in_weight, by_permutes=True)
    out_whole = gather_rows(out_weight)
    projected = halves_product(normed, in_whole, groups)

    def bound_mixer(proj_arg, cw_arg, cb_arg, sb_arg, dl_arg, sk_arg, gg_arg):
        return mixer(proj_arg, segment, cw_arg, cb_arg, sb_arg, dl_arg, sk_arg, gg_arg)

    gated_f, mixer_back = jax.vjp(
        bound_mixer,
        projected,
        convw_full,
        convb_full,
        stepb_full,
        decay_full,
        skip_full,
        gategain_full,
    )
    gated = gated_f.astype(jnp.bfloat16)
    branch_out = halves_product(gated, out_whole, groups)
    layer_out = layer_in + branch_out
    cot_low = cotangent.astype(jnp.bfloat16)
    out_halves = reduce_core(row_product(gated, cot_low))
    gated_grad = halves_back(cot_low, out_whole, groups)
    out_group = reduce_group(out_halves)
    proj_grad, g_convw, g_convb, g_stepb, g_decay, g_skip, g_gategain = mixer_back(gated_grad)
    proj_low = proj_grad.astype(jnp.bfloat16)
    normed_grad = halves_back(proj_low, in_whole, groups)
    back_in, g_norm = norm_back(normed_grad)
    input_grad = cotangent + back_in
    grads = (g_norm, g_convw, g_convb, g_stepb, g_decay, g_skip, g_gategain)
    small_blocks = jnp.concatenate([g.reshape(groups, -1) for g in grads], axis=1)
    small_len = small_blocks.shape[1]
    small_rows = -(-small_len // 2048) * 16
    small_blocks = jnp.pad(small_blocks, ((0, 0), (0, small_rows * 128 - small_len)))
    small_blocks = small_blocks.reshape(groups, small_rows, 128)
    small_blocks = small_blocks + core_swap(small_blocks)
    cols = proj_low.shape[1]
    wide = -(-cols // 128) * 128
    proj_wide = jnp.pad(proj_low, ((0, 0), (0, wide - cols)))
    in_group, small_group = reduce_group(
        reduce_core(row_product(normed, proj_wide)), small_blocks
    )
    in_shape, out_shape = in_group.shape, out_group.shape
    big_rows = (in_group.size + out_group.size) // 128
    tail_rows = -(-(big_rows + small_group.shape[0]) // 64) * 64 - big_rows
    small_group = jnp.pad(small_group, ((0, tail_rows - small_group.shape[0]), (0, 0)))
    joined = jnp.concatenate(
        [in_group.reshape(-1, 128), out_group.reshape(-1, 128), small_group], axis=0
    )
    joined = allreduce_rep(joined)
    split_at = in_group.size // 128
    split_out = split_at + out_group.size // 128
    in_owned = core_join(joined[:split_at].reshape(in_shape))[:, :cols]
    out_owned = core_join(joined[split_at:split_out].reshape(out_shape))
    mine = joined[split_out:].reshape(-1)[:small_len]
    small_final = []
    offset = 0
    for g in grads:
        size = g.size // groups
        small_final.append(mine[offset : offset + size].reshape((g.shape[0] // groups,) + g.shape[1:]))
        offset += size
    return (
        layer_out,
        input_grad,
        small_final[0],
        in_owned,
        small_final[1],
        small_final[2],
        small_final[3],
        small_final[4],
        small_final[5],
        small_final[6],
        out_owned,
    )


def solution(mesh):
    split = Mesh(
        mesh.devices.reshape(mesh.shape["rep"] // 2, 2, 4, 2),
        ("rep_hi", "core", "shard_0", "shard_1"),
    )
    in_specs = (
        P(REP_SHARD, None),
        P(REP_SHARD, None),
        P(REP_SHARD, None),
        P(SHARD),
        P(SHARD, None),
        P(SHARD, None),
        P(SHARD),
        P(SHARD),
        P(SHARD),
        P(SHARD),
        P(SHARD),
        P(SHARD, None),
    )
    out_specs = (
        P(REP_SHARD, None),
        P(REP_SHARD, None),
        P(SHARD),
        P(SHARD, None),
        P(SHARD, None),
        P(SHARD),
        P(SHARD),
        P(SHARD),
        P(SHARD),
        P(SHARD),
        P(SHARD, None),
    )
    return jax.shard_map(
        on_device, mesh=split, in_specs=in_specs, out_specs=out_specs, check_vma=False
    )
```

```python
import math

import jax
import jax.numpy as jnp
from jax import lax
from jax.sharding import Mesh
from jax.sharding import PartitionSpec as P

SPAN = 256
SHARD = ("shard_0", "shard_1")
REP = ("rep_hi", "core")
REP_SHARD = ("rep_hi", "core", "shard_0", "shard_1")
ALL = REP_SHARD


EPS = 1e-05
HIGH = lax.Precision.HIGHEST


def side_by_side(arrays, axis, dim, along):
    widths = [math.prod(a.shape[along:]) for a in arrays]
    both = jnp.concatenate(
        [a.reshape(*a.shape[:along], w) for a, w in zip(arrays, widths)], axis=along
    )
    result = lax.all_gather(both, axis, axis=dim, tiled=True)
    blocks = jnp.split(result, [sum(widths[:k]) for k in range(1, len(widths))], axis=along)
    return tuple(
        (b.reshape(*result.shape[:along], *a.shape[along:]) for a, b in zip(arrays, blocks))
    )


def sum_by_axis(total, axes):
    for axis in axes:
        total = lax.psum_scatter(total, axis, scatter_dimension=0, tiled=True)
    return total


def in_blocks(shard, dim, size):
    before, after = (shard.shape[:dim], shard.shape[dim + 1 :])
    return jnp.moveaxis(shard.reshape(*before, size, -1, *after), dim, 0)


def sum_at_owner(shard, axis, dim):
    size = lax.axis_size(axis)
    blocks = lax.all_to_all(in_blocks(shard, dim, size), axis, 0, 0, tiled=True)
    return jnp.sum(blocks, axis=0)


def sent_together(arrays, axis, dim, along):
    widths = [math.prod(a.shape[along:]) for a in arrays]
    both = jnp.concatenate(
        [a.reshape(*a.shape[:along], w) for a, w in zip(arrays, widths)], axis=along
    )
    result = sum_at_owner(both, axis, dim)
    blocks = jnp.split(result, [sum(widths[:k]) for k in range(1, len(widths))], axis=along)
    return tuple(
        (b.reshape(*result.shape[:along], *a.shape[along:]) for a, b in zip(arrays, blocks))
    )


def shifted(values, lag):
    zeros_top = jnp.zeros((lag,) + values.shape[1:], values.dtype)
    return jnp.concatenate([zeros_top, values[:-lag]], axis=0)


def segment_ids(lengths_row, count):
    offsets = jnp.cumsum(lengths_row, dtype=jnp.int32) - lengths_row
    places = jnp.arange(count, dtype=jnp.int32)
    return (
        jnp.sum((places[:, None] >= offsets[None, :]).astype(jnp.int32), axis=1, dtype=jnp.int32)
        - 1
    )


def row_product(left, right):
    return lax.dot_general(
        left, right, (((0,), (0,)), ((), ())), preferred_element_type=jnp.float32
    )


def back_product(left, right):
    return lax.dot_general(
        left, right, (((1,), (1,)), ((), ())), preferred_element_type=jnp.float32
    )


def norm_input(inputs, gain_one):
    scaling = lax.rsqrt(jnp.mean(inputs * inputs, axis=1, keepdims=True) + EPS)
    return inputs * scaling * gain_one[None, :]


def mixer(projected, segment, conv_weight, conv_bias, step_bias, decay_log, skip_gain, gate_gain):
    count = projected.shape[0]
    inner = gate_gain.shape[0]
    heads = step_bias.shape[0]
    head_dim = inner // heads
    channels = conv_weight.shape[0]
    state_dim = (channels - inner) // 2
    taps = conv_weight.shape[1]
    gate_part = projected[:, :inner]
    conv_in = projected[:, inner : inner + channels]
    step_raw = projected[:, inner + channels :]
    places = jnp.arange(count, dtype=jnp.int32)
    conv_out = conv_bias[None, :] + conv_weight[:, taps - 1][None, :] * conv_in
    for lag in range(1, taps):
        same = (shifted(segment, lag) == segment) & (places >= lag)
        conv_out = conv_out + jnp.where(
            same[:, None], conv_weight[:, taps - 1 - lag][None, :] * shifted(conv_in, lag), 0.0
        )
    activated = jax.nn.silu(conv_out)
    values = activated[:, :inner].reshape(count, heads, head_dim)
    b_matrix = activated[:, inner : inner + state_dim]
    c_matrix = activated[:, inner + state_dim :]
    step_size = jax.nn.softplus(step_raw + step_bias[None, :])
    decay = -jnp.exp(decay_log)[None, :] * step_size
    blocks = count // SPAN
    values_c = values.reshape(blocks, SPAN, heads, head_dim)
    b_spans = b_matrix.reshape(blocks, SPAN, state_dim)
    c_spans = c_matrix.reshape(blocks, SPAN, state_dim)
    step_c = step_size.reshape(blocks, SPAN, heads)
    cumul = jnp.cumsum(decay.reshape(blocks, SPAN, heads), axis=1)
    seg_c = segment.reshape(blocks, SPAN)
    rows_in = jnp.arange(SPAN, dtype=jnp.int32)
    lower = rows_in[:, None] >= rows_in[None, :]
    allowed = lower[None] & (seg_c[:, :, None] == seg_c[:, None, :])
    cumul_t = jnp.transpose(cumul, (0, 2, 1))
    differ = cumul_t[:, :, :, None] - cumul_t[:, :, None, :]
    weights_l = jnp.exp(jnp.where(allowed[:, None], differ, -10000.0))
    scores = jnp.einsum("cin,cjn->cij", c_spans, b_spans, precision=HIGH)
    mixing = weights_l * scores[:, None]
    scaled_in = values_c * step_c[..., None]
    y_intra = jnp.einsum("chij,cjhp->cihp", mixing, scaled_in, precision=HIGH)
    carried = jnp.zeros((heads, head_dim, state_dim), jnp.float32)
    before_seg = jnp.int32(-1)
    linked = (seg_c[0] == before_seg).astype(jnp.float32)
    reach = jnp.exp(cumul[0]) * linked[:, None]
    inter = jnp.einsum("in,hpn->ihp", c_spans[0], carried, precision=HIGH) * reach[:, :, None]
    pieces = [y_intra[0] + inter]
    y_all = jnp.concatenate(pieces, axis=0) + skip_gain[None, :, None] * values
    gated_pre = y_all.reshape(count, inner) * jax.nn.silu(gate_part)
    scaling = lax.rsqrt(jnp.mean(gated_pre * gated_pre, axis=1, keepdims=True) + EPS)
    return gated_pre * scaling * gate_gain[None, :]


def reduce_group(halves, small=None):
    ring = lax.axis_size("shard_0")
    y = lax.axis_index("shard_1")
    z = lax.axis_index("shard_0")
    up = [(i, (i + 1) % ring) for i in range(ring)]
    down = [(i, (i - 1) % ring) for i in range(ring)]
    items = [(halves, jnp.bfloat16)] + ([] if small is None else [(small, jnp.float32)])
    rels, halfs = [], []
    for values, _ in items:
        blocks = values.reshape((ring, 2) + values.shape[1:])
        doubled = jnp.concatenate([blocks, blocks], axis=0)
        rels.append(lax.dynamic_slice_in_dim(doubled, z, ring, axis=0))
        halfs.append(values.shape[1] // 2)

    def send(parts, pairs):
        return [lax.ppermute(p.astype(w), "shard_0", pairs) for p, (_, w) in zip(parts, items)]

    acc_up = send([r[3][:, :h] for r, h in zip(rels, halfs)], up)
    acc_dn = send([r[1][:, h:] for r, h in zip(rels, halfs)], down)
    acc_up = send([a + r[2][:, :h] for a, r, h in zip(acc_up, rels, halfs)], up)
    acc_dn = send([a + r[2][:, h:] for a, r, h in zip(acc_dn, rels, halfs)], down)
    acc_up = send([a + r[1][:, :h] for a, r, h in zip(acc_up, rels, halfs)], up)
    acc_dn = send([a + r[3][:, h:] for a, r, h in zip(acc_dn, rels, halfs)], down)
    results = []
    for au, ad, r, h, (_, w) in zip(acc_up, acc_dn, rels, halfs, items):
        zsum = jnp.concatenate(
            [au.astype(jnp.float32) + r[0][:, :h], ad.astype(jnp.float32) + r[0][:, h:]], axis=1
        )
        keep = lax.dynamic_index_in_dim(zsum, y, axis=0, keepdims=False)
        give = lax.dynamic_index_in_dim(zsum, 1 - y, axis=0, keepdims=False)
        got = lax.ppermute(give.astype(w), "shard_1", [(0, 1), (1, 0)])
        results.append(keep + got.astype(jnp.float32))
    return results[0] if small is None else results


def allreduce_rep(values):
    ring = 4
    size = lax.axis_size("rep_hi")
    index = lax.axis_index("rep_hi")
    x = index % ring
    up = [(i, (i // ring) * ring + (i % ring + 1) % ring) for i in range(size)]
    down = [(i, (i // ring) * ring + (i % ring - 1) % ring) for i in range(size)]
    rows = values.shape[0]
    chunks = values.reshape(ring, rows // ring, values.shape[1])
    doubled = jnp.concatenate([chunks, chunks], axis=0)
    rel = lax.dynamic_slice_in_dim(doubled, x, ring, axis=0)
    half = rows // ring // 2
    a = lax.ppermute(rel[2][:half], "rep_hi", up)
    b = lax.ppermute(rel[2][half:], "rep_hi", down)
    up_msg = jnp.concatenate([a + rel[1][:half], rel[1][half:]], axis=0)
    down_msg = jnp.concatenate([rel[3][:half], b + rel[3][half:]], axis=0)
    mine = rel[0] + lax.ppermute(up_msg, "rep_hi", up) + lax.ppermute(down_msg, "rep_hi", down)
    step = ring
    while step < size:
        mine = mine + lax.ppermute(mine, "rep_hi", [(i, i ^ step) for i in range(size)])
        step *= 2
    from_prev = lax.ppermute(mine, "rep_hi", up)
    from_next = lax.ppermute(mine, "rep_hi", down)
    far_a = lax.ppermute(from_prev[:half], "rep_hi", up)
    far_b = lax.ppermute(from_next[half:], "rep_hi", down)
    opposite = jnp.concatenate([far_a, far_b], axis=0)
    ordered = jnp.stack([mine, from_next, opposite, from_prev])
    doubled = jnp.concatenate([ordered, ordered], axis=0)
    placed = lax.dynamic_slice_in_dim(doubled, (ring - x) % ring, ring, axis=0)
    return placed.reshape(values.shape)


def core_join(owned):
    core = lax.axis_index("core")
    other = core_swap(owned)
    first = jnp.where(core == 0, owned, other)
    second = jnp.where(core == 0, other, owned)
    return jnp.concatenate([first, second], axis=0)


def core_swap(values):
    return lax.ppermute(values, "core", [(0, 1), (1, 0)])


def gather_group(block, sibling):
    ring = lax.axis_size("shard_0")
    y = lax.axis_index("shard_1")
    z = lax.axis_index("shard_0")
    up = [(i, (i + 1) % ring) for i in range(ring)]
    down = [(i, (i - 1) % ring) for i in range(ring)]
    half = block.shape[0] // 2

    def place(own, got):
        return jnp.where(y == 0, jnp.stack([own, got]), jnp.stack([got, own]))

    def arrange(pair, from_next, opposite, from_prev):
        ordered = jnp.stack([pair, from_next, opposite, from_prev])
        doubled = jnp.concatenate([ordered, ordered], axis=0)
        placed = lax.dynamic_slice_in_dim(doubled, (ring - z) % ring, ring, axis=0)
        return placed.reshape((ring * 2,) + block.shape)

    other_y = lax.ppermute(block, "shard_1", [(0, 1), (1, 0)])
    pair = place(block, other_y)
    from_prev = lax.ppermute(pair, "shard_0", up)
    from_next = lax.ppermute(pair, "shard_0", down)
    pair_s = place(sibling, core_swap(other_y))
    far_a = lax.ppermute(from_prev[:, :half], "shard_0", up)
    far_b = lax.ppermute(from_next[:, half:], "shard_0", down)
    from_prev_s = core_swap(from_prev)
    from_next_s = core_swap(from_next)
    opposite = jnp.concatenate([far_a, far_b], axis=1)
    opposite_s = core_swap(opposite)
    return (
        arrange(pair, from_next, opposite, from_prev),
        arrange(pair_s, from_next_s, opposite_s, from_prev_s),
    )


def core_swap(values):
    return lax.ppermute(values, "core", [(0, 1), (1, 0)])


def gather_rows(weight, by_permutes=False):
    rows = weight.shape[0]
    half = rows // 2
    core = lax.axis_index("core")
    mine = lax.dynamic_slice_in_dim(weight, core * half, half, axis=0)
    if by_permutes:
        sibling = lax.dynamic_slice_in_dim(weight, (1 - core) * half, half, axis=0)
        part, other = gather_group(mine, sibling)
    else:
        part = lax.all_gather(mine, SHARD, axis=0, tiled=False)
        other = core_swap(part)
    return part.reshape(-1, weight.shape[1]), other.reshape(-1, weight.shape[1])


def split_cols(values, groups):
    core = lax.axis_index("core")
    blocks = values.reshape(values.shape[0], groups, 2, -1)
    own = lax.dynamic_index_in_dim(blocks, core, axis=2, keepdims=False)
    other = lax.dynamic_index_in_dim(blocks, 1 - core, axis=2, keepdims=False)
    return own.reshape(values.shape[0], -1), other.reshape(values.shape[0], -1)


def join_cols(own, other, groups):
    core = lax.axis_index("core")
    count = own.shape[0]
    pair = jnp.stack([own.reshape(count, groups, -1), other.reshape(count, groups, -1)], axis=2)
    doubled = jnp.concatenate([pair, pair], axis=2)
    placed = lax.dynamic_slice_in_dim(doubled, core, 2, axis=2)
    return placed.reshape(count, -1)


def halves_product(left, halves, groups):
    own_l, other_l = split_cols(left, groups)
    own_w, other_w = halves
    return jnp.dot(own_l, own_w, preferred_element_type=jnp.float32) + jnp.dot(
        other_l, other_w, preferred_element_type=jnp.float32
    )


def halves_back(left, halves, groups):
    own_w, other_w = halves
    return join_cols(back_product(left, own_w), back_product(left, other_w), groups)


def reduce_core(partial):
    groups = lax.axis_size(SHARD)
    cols = partial.shape[1]
    core = lax.axis_index("core")
    blocks = partial.reshape(groups, 2, -1, cols)
    keep = lax.dynamic_index_in_dim(blocks, core, axis=1, keepdims=False)
    give = lax.dynamic_index_in_dim(blocks, 1 - core, axis=1, keepdims=False)
    return keep + core_swap(give)


def reduce_rest(halves, wait_for=None):
    core = lax.axis_index("core")
    owned = reduce_group(halves)
    if wait_for is not None:
        owned, wait_for = lax.optimization_barrier((owned, wait_for))
    owned = lax.psum(owned, "rep_hi")
    other = core_swap(owned)
    first = jnp.where(core == 0, owned, other)
    second = jnp.where(core == 0, other, owned)
    return jnp.concatenate([first, second], axis=0)


def reduce_rows(partial, wait_for=None):
    return reduce_rest(reduce_core(partial), wait_for)


def exchange_sum(values, axes):
    for axis in axes:
        size = lax.axis_size(axis)
        step = 1
        while step < size:
            pairs = [(i, i ^ step) for i in range(size)]
            values = values + lax.ppermute(values, axis, pairs)
            step *= 2
    return values


def on_device(
    layer_in,
    cotangent,
    seq_lengths,
    norm_gain,
    in_weight,
    conv_weight,
    conv_bias,
    step_bias,
    decay_log,
    skip_gain,
    gate_gain,
    out_weight,
):
    count = layer_in.shape[0]
    groups = lax.axis_size(SHARD)
    segment = segment_ids(seq_lengths[0], count)
    smalls = (norm_gain, conv_weight, conv_bias, step_bias, decay_log, skip_gain, gate_gain)
    flat = jnp.concatenate([a.reshape(-1) for a in smalls])
    flat_len = flat.shape[0]
    place = lax.axis_index(SHARD)
    spread = jnp.where(
        (jnp.arange(groups, dtype=jnp.int32) == place)[:, None], flat[None, :], 0.0
    )
    flat_all = exchange_sum(spread, ("shard_1", "shard_0"))
    pieces_full = []
    offset = 0
    for a in smalls:
        size = a.size
        block = flat_all[:, offset : offset + size]
        pieces_full.append(block.reshape((groups * a.shape[0],) + a.shape[1:]))
        offset += size
    norm_full, convw_full, convb_full, stepb_full, decay_full, skip_full, gategain_full = pieces_full
    normed_f, norm_back = jax.vjp(norm_input, layer_in, norm_full)
    normed = normed_f.astype(jnp.bfloat16)
    in_whole = gather_rows(in_weight, by_permutes=True)
    in_whole, out_weight = lax.optimization_barrier((in_whole, out_weight))
    out_whole = gather_rows(out_weight, by_permutes=True)
    projected = halves_product(normed, in_whole, groups)

    def bound_mixer(proj_arg, cw_arg, cb_arg, sb_arg, dl_arg, sk_arg, gg_arg):
        return mixer(proj_arg, segment, cw_arg, cb_arg, sb_arg, dl_arg, sk_arg, gg_arg)

    gated_f, mixer_back = jax.vjp(
        bound_mixer,
        projected,
        convw_full,
        convb_full,
        stepb_full,
        decay_full,
        skip_full,
        gategain_full,
    )
    gated = gated_f.astype(jnp.bfloat16)
    branch_out = halves_product(gated, out_whole, groups)
    layer_out = layer_in + branch_out
    cot_low = cotangent.astype(jnp.bfloat16)
    out_halves = reduce_core(row_product(gated, cot_low))
    gated_grad = halves_back(cot_low, out_whole, groups)
    out_group = reduce_group(out_halves)
    proj_grad, g_convw, g_convb, g_stepb, g_decay, g_skip, g_gategain = mixer_back(gated_grad)
    proj_low = proj_grad.astype(jnp.bfloat16)
    normed_grad = halves_back(proj_low, in_whole, groups)
    back_in, g_norm = norm_back(normed_grad)
    input_grad = cotangent + back_in
    grads = (g_norm, g_convw, g_convb, g_stepb, g_decay, g_skip, g_gategain)
    small_blocks = jnp.concatenate([g.reshape(groups, -1) for g in grads], axis=1)
    small_len = small_blocks.shape[1]
    small_rows = -(-small_len // 2048) * 16
    small_blocks = jnp.pad(small_blocks, ((0, 0), (0, small_rows * 128 - small_len)))
    small_blocks = small_blocks.reshape(groups, small_rows, 128)
    small_blocks = small_blocks + core_swap(small_blocks)
    cols = proj_low.shape[1]
    wide = -(-cols // 128) * 128
    proj_wide = jnp.pad(proj_low, ((0, 0), (0, wide - cols)))
    in_group, small_group = reduce_group(
        reduce_core(row_product(normed, proj_wide)), small_blocks
    )
    in_shape, out_shape = in_group.shape, out_group.shape
    big_rows = (in_group.size + out_group.size) // 128
    tail_rows = -(-(big_rows + small_group.shape[0]) // 64) * 64 - big_rows
    small_group = jnp.pad(small_group, ((0, tail_rows - small_group.shape[0]), (0, 0)))
    joined = jnp.concatenate(
        [in_group.reshape(-1, 128), out_group.reshape(-1, 128), small_group], axis=0
    )
    joined = allreduce_rep(joined)
    split_at = in_group.size // 128
    split_out = split_at + out_group.size // 128
    in_owned = core_join(joined[:split_at].reshape(in_shape))[:, :cols]
    out_owned = core_join(joined[split_at:split_out].reshape(out_shape))
    mine = joined[split_out:].reshape(-1)[:small_len]
    small_final = []
    offset = 0
    for g in grads:
        size = g.size // groups
        small_final.append(mine[offset : offset + size].reshape((g.shape[0] // groups,) + g.shape[1:]))
        offset += size
    return (
        layer_out,
        input_grad,
        small_final[0],
        in_owned,
        small_final[1],
        small_final[2],
        small_final[3],
        small_final[4],
        small_final[5],
        small_final[6],
        out_owned,
    )


def solution(mesh):
    split = Mesh(
        mesh.devices.reshape(mesh.shape["rep"] // 2, 2, 4, 2),
        ("rep_hi", "core", "shard_0", "shard_1"),
    )
    in_specs = (
        P(REP_SHARD, None),
        P(REP_SHARD, None),
        P(REP_SHARD, None),
        P(SHARD),
        P(SHARD, None),
        P(SHARD, None),
        P(SHARD),
        P(SHARD),
        P(SHARD),
        P(SHARD),
        P(SHARD),
        P(SHARD, None),
    )
    out_specs = (
        P(REP_SHARD, None),
        P(REP_SHARD, None),
        P(SHARD),
        P(SHARD, None),
        P(SHARD, None),
        P(SHARD),
        P(SHARD),
        P(SHARD),
        P(SHARD),
        P(SHARD),
        P(SHARD, None),
    )
    return jax.shard_map(
        on_device, mesh=split, in_specs=in_specs, out_specs=out_specs, check_vma=False
    )
```

```python
import math

import jax
import jax.numpy as jnp
from jax import lax
from jax.sharding import Mesh
from jax.sharding import PartitionSpec as P

SPAN = 256
SHARD = ("shard_0", "shard_1")
REP = ("rep_hi", "core")
REP_SHARD = ("rep_hi", "core", "shard_0", "shard_1")
ALL = REP_SHARD


EPS = 1e-05
HIGH = lax.Precision.HIGHEST


def side_by_side(arrays, axis, dim, along):
    widths = [math.prod(a.shape[along:]) for a in arrays]
    both = jnp.concatenate(
        [a.reshape(*a.shape[:along], w) for a, w in zip(arrays, widths)], axis=along
    )
    result = lax.all_gather(both, axis, axis=dim, tiled=True)
    blocks = jnp.split(result, [sum(widths[:k]) for k in range(1, len(widths))], axis=along)
    return tuple(
        (b.reshape(*result.shape[:along], *a.shape[along:]) for a, b in zip(arrays, blocks))
    )


def sum_by_axis(total, axes):
    for axis in axes:
        total = lax.psum_scatter(total, axis, scatter_dimension=0, tiled=True)
    return total


def in_blocks(shard, dim, size):
    before, after = (shard.shape[:dim], shard.shape[dim + 1 :])
    return jnp.moveaxis(shard.reshape(*before, size, -1, *after), dim, 0)


def sum_at_owner(shard, axis, dim):
    size = lax.axis_size(axis)
    blocks = lax.all_to_all(in_blocks(shard, dim, size), axis, 0, 0, tiled=True)
    return jnp.sum(blocks, axis=0)


def sent_together(arrays, axis, dim, along):
    widths = [math.prod(a.shape[along:]) for a in arrays]
    both = jnp.concatenate(
        [a.reshape(*a.shape[:along], w) for a, w in zip(arrays, widths)], axis=along
    )
    result = sum_at_owner(both, axis, dim)
    blocks = jnp.split(result, [sum(widths[:k]) for k in range(1, len(widths))], axis=along)
    return tuple(
        (b.reshape(*result.shape[:along], *a.shape[along:]) for a, b in zip(arrays, blocks))
    )


def shifted(values, lag):
    zeros_top = jnp.zeros((lag,) + values.shape[1:], values.dtype)
    return jnp.concatenate([zeros_top, values[:-lag]], axis=0)


def segment_ids(lengths_row, count):
    offsets = jnp.cumsum(lengths_row, dtype=jnp.int32) - lengths_row
    places = jnp.arange(count, dtype=jnp.int32)
    return (
        jnp.sum((places[:, None] >= offsets[None, :]).astype(jnp.int32), axis=1, dtype=jnp.int32)
        - 1
    )


def row_product(left, right):
    return lax.dot_general(
        left, right, (((0,), (0,)), ((), ())), preferred_element_type=jnp.float32
    )


def back_product(left, right):
    return lax.dot_general(
        left, right, (((1,), (1,)), ((), ())), preferred_element_type=jnp.float32
    )


def norm_input(inputs, gain_one):
    scaling = lax.rsqrt(jnp.mean(inputs * inputs, axis=1, keepdims=True) + EPS)
    return inputs * scaling * gain_one[None, :]


def mixer(projected, segment, conv_weight, conv_bias, step_bias, decay_log, skip_gain, gate_gain):
    count = projected.shape[0]
    inner = gate_gain.shape[0]
    heads = step_bias.shape[0]
    head_dim = inner // heads
    channels = conv_weight.shape[0]
    state_dim = (channels - inner) // 2
    taps = conv_weight.shape[1]
    gate_part = projected[:, :inner]
    conv_in = projected[:, inner : inner + channels]
    step_raw = projected[:, inner + channels :]
    places = jnp.arange(count, dtype=jnp.int32)
    conv_out = conv_bias[None, :] + conv_weight[:, taps - 1][None, :] * conv_in
    for lag in range(1, taps):
        same = (shifted(segment, lag) == segment) & (places >= lag)
        conv_out = conv_out + jnp.where(
            same[:, None], conv_weight[:, taps - 1 - lag][None, :] * shifted(conv_in, lag), 0.0
        )
    activated = jax.nn.silu(conv_out)
    values = activated[:, :inner].reshape(count, heads, head_dim)
    b_matrix = activated[:, inner : inner + state_dim]
    c_matrix = activated[:, inner + state_dim :]
    step_size = jax.nn.softplus(step_raw + step_bias[None, :])
    decay = -jnp.exp(decay_log)[None, :] * step_size
    blocks = count // SPAN
    values_c = values.reshape(blocks, SPAN, heads, head_dim)
    b_spans = b_matrix.reshape(blocks, SPAN, state_dim)
    c_spans = c_matrix.reshape(blocks, SPAN, state_dim)
    step_c = step_size.reshape(blocks, SPAN, heads)
    cumul = jnp.cumsum(decay.reshape(blocks, SPAN, heads), axis=1)
    seg_c = segment.reshape(blocks, SPAN)
    rows_in = jnp.arange(SPAN, dtype=jnp.int32)
    lower = rows_in[:, None] >= rows_in[None, :]
    allowed = lower[None] & (seg_c[:, :, None] == seg_c[:, None, :])
    cumul_t = jnp.transpose(cumul, (0, 2, 1))
    differ = cumul_t[:, :, :, None] - cumul_t[:, :, None, :]
    weights_l = jnp.exp(jnp.where(allowed[:, None], differ, -10000.0))
    scores = jnp.einsum("cin,cjn->cij", c_spans, b_spans, precision=HIGH)
    mixing = weights_l * scores[:, None]
    scaled_in = values_c * step_c[..., None]
    y_intra = jnp.einsum("chij,cjhp->cihp", mixing, scaled_in, precision=HIGH)
    carried = jnp.zeros((heads, head_dim, state_dim), jnp.float32)
    before_seg = jnp.int32(-1)
    linked = (seg_c[0] == before_seg).astype(jnp.float32)
    reach = jnp.exp(cumul[0]) * linked[:, None]
    inter = jnp.einsum("in,hpn->ihp", c_spans[0], carried, precision=HIGH) * reach[:, :, None]
    pieces = [y_intra[0] + inter]
    y_all = jnp.concatenate(pieces, axis=0) + skip_gain[None, :, None] * values
    gated_pre = y_all.reshape(count, inner) * jax.nn.silu(gate_part)
    scaling = lax.rsqrt(jnp.mean(gated_pre * gated_pre, axis=1, keepdims=True) + EPS)
    return gated_pre * scaling * gate_gain[None, :]


def reduce_group(halves, small=None):
    ring = lax.axis_size("shard_0")
    y = lax.axis_index("shard_1")
    z = lax.axis_index("shard_0")
    up = [(i, (i + 1) % ring) for i in range(ring)]
    down = [(i, (i - 1) % ring) for i in range(ring)]
    items = [(halves, jnp.bfloat16)] + ([] if small is None else [(small, jnp.float32)])
    rels, halfs = [], []
    for values, _ in items:
        blocks = values.reshape((ring, 2) + values.shape[1:])
        doubled = jnp.concatenate([blocks, blocks], axis=0)
        rels.append(lax.dynamic_slice_in_dim(doubled, z, ring, axis=0))
        halfs.append(values.shape[1] // 2)

    def send(parts, pairs):
        return [lax.ppermute(p.astype(w), "shard_0", pairs) for p, (_, w) in zip(parts, items)]

    acc_up = send([r[3][:, :h] for r, h in zip(rels, halfs)], up)
    acc_dn = send([r[1][:, h:] for r, h in zip(rels, halfs)], down)
    acc_up = send([a + r[2][:, :h] for a, r, h in zip(acc_up, rels, halfs)], up)
    acc_dn = send([a + r[2][:, h:] for a, r, h in zip(acc_dn, rels, halfs)], down)
    acc_up = send([a + r[1][:, :h] for a, r, h in zip(acc_up, rels, halfs)], up)
    acc_dn = send([a + r[3][:, h:] for a, r, h in zip(acc_dn, rels, halfs)], down)
    results = []
    for au, ad, r, h, (_, w) in zip(acc_up, acc_dn, rels, halfs, items):
        zsum = jnp.concatenate(
            [au.astype(jnp.float32) + r[0][:, :h], ad.astype(jnp.float32) + r[0][:, h:]], axis=1
        )
        keep = lax.dynamic_index_in_dim(zsum, y, axis=0, keepdims=False)
        give = lax.dynamic_index_in_dim(zsum, 1 - y, axis=0, keepdims=False)
        got = lax.ppermute(give.astype(w), "shard_1", [(0, 1), (1, 0)])
        results.append(keep + got.astype(jnp.float32))
    return results[0] if small is None else results


def allreduce_rep(values):
    ring = 4
    size = lax.axis_size("rep_hi")
    index = lax.axis_index("rep_hi")
    x = index % ring
    up = [(i, (i // ring) * ring + (i % ring + 1) % ring) for i in range(size)]
    down = [(i, (i // ring) * ring + (i % ring - 1) % ring) for i in range(size)]
    rows = values.shape[0]
    chunks = values.reshape(ring, rows // ring, values.shape[1])
    doubled = jnp.concatenate([chunks, chunks], axis=0)
    rel = lax.dynamic_slice_in_dim(doubled, x, ring, axis=0)
    half = rows // ring // 2
    a = lax.ppermute(rel[2][:half], "rep_hi", up)
    b = lax.ppermute(rel[2][half:], "rep_hi", down)
    up_msg = jnp.concatenate([a + rel[1][:half], rel[1][half:]], axis=0)
    down_msg = jnp.concatenate([rel[3][:half], b + rel[3][half:]], axis=0)
    mine = rel[0] + lax.ppermute(up_msg, "rep_hi", up) + lax.ppermute(down_msg, "rep_hi", down)
    step = ring
    while step < size:
        mine = mine + lax.ppermute(mine, "rep_hi", [(i, i ^ step) for i in range(size)])
        step *= 2
    from_prev = lax.ppermute(mine, "rep_hi", up)
    from_next = lax.ppermute(mine, "rep_hi", down)
    far_a = lax.ppermute(from_prev[:half], "rep_hi", up)
    far_b = lax.ppermute(from_next[half:], "rep_hi", down)
    opposite = jnp.concatenate([far_a, far_b], axis=0)
    ordered = jnp.stack([mine, from_next, opposite, from_prev])
    doubled = jnp.concatenate([ordered, ordered], axis=0)
    placed = lax.dynamic_slice_in_dim(doubled, (ring - x) % ring, ring, axis=0)
    return placed.reshape(values.shape)


def core_join(owned):
    core = lax.axis_index("core")
    other = core_swap(owned)
    first = jnp.where(core == 0, owned, other)
    second = jnp.where(core == 0, other, owned)
    return jnp.concatenate([first, second], axis=0)


def core_swap(values):
    return lax.ppermute(values, "core", [(0, 1), (1, 0)])


def gather_group(block, sibling):
    ring = lax.axis_size("shard_0")
    y = lax.axis_index("shard_1")
    z = lax.axis_index("shard_0")
    up = [(i, (i + 1) % ring) for i in range(ring)]
    down = [(i, (i - 1) % ring) for i in range(ring)]
    half = block.shape[0] // 2

    def place(own, got):
        return jnp.where(y == 0, jnp.stack([own, got]), jnp.stack([got, own]))

    def arrange(pair, from_next, opposite, from_prev):
        ordered = jnp.stack([pair, from_next, opposite, from_prev])
        doubled = jnp.concatenate([ordered, ordered], axis=0)
        placed = lax.dynamic_slice_in_dim(doubled, (ring - z) % ring, ring, axis=0)
        return placed.reshape((ring * 2,) + block.shape)

    other_y = lax.ppermute(block, "shard_1", [(0, 1), (1, 0)])
    pair = place(block, other_y)
    from_prev = lax.ppermute(pair, "shard_0", up)
    from_next = lax.ppermute(pair, "shard_0", down)
    pair_s = place(sibling, core_swap(other_y))
    far_a = lax.ppermute(from_prev[:, :half], "shard_0", up)
    far_b = lax.ppermute(from_next[:, half:], "shard_0", down)
    from_prev_s = core_swap(from_prev)
    from_next_s = core_swap(from_next)
    opposite = jnp.concatenate([far_a, far_b], axis=1)
    opposite_s = core_swap(opposite)
    return (
        arrange(pair, from_next, opposite, from_prev),
        arrange(pair_s, from_next_s, opposite_s, from_prev_s),
    )


def core_swap(values):
    return lax.ppermute(values, "core", [(0, 1), (1, 0)])


def gather_rows(weight, by_permutes=False):
    rows = weight.shape[0]
    half = rows // 2
    core = lax.axis_index("core")
    mine = lax.dynamic_slice_in_dim(weight, core * half, half, axis=0)
    if by_permutes:
        sibling = lax.dynamic_slice_in_dim(weight, (1 - core) * half, half, axis=0)
        part, other = gather_group(mine, sibling)
    else:
        part = lax.all_gather(mine, SHARD, axis=0, tiled=False)
        other = core_swap(part)
    return part.reshape(-1, weight.shape[1]), other.reshape(-1, weight.shape[1])


def split_cols(values, groups):
    core = lax.axis_index("core")
    blocks = values.reshape(values.shape[0], groups, 2, -1)
    own = lax.dynamic_index_in_dim(blocks, core, axis=2, keepdims=False)
    other = lax.dynamic_index_in_dim(blocks, 1 - core, axis=2, keepdims=False)
    return own.reshape(values.shape[0], -1), other.reshape(values.shape[0], -1)


def join_cols(own, other, groups):
    core = lax.axis_index("core")
    count = own.shape[0]
    pair = jnp.stack([own.reshape(count, groups, -1), other.reshape(count, groups, -1)], axis=2)
    doubled = jnp.concatenate([pair, pair], axis=2)
    placed = lax.dynamic_slice_in_dim(doubled, core, 2, axis=2)
    return placed.reshape(count, -1)


def halves_product(left, halves, groups):
    own_l, other_l = split_cols(left, groups)
    own_w, other_w = halves
    return jnp.dot(own_l, own_w, preferred_element_type=jnp.float32) + jnp.dot(
        other_l, other_w, preferred_element_type=jnp.float32
    )


def halves_back(left, halves, groups):
    own_w, other_w = halves
    return join_cols(back_product(left, own_w), back_product(left, other_w), groups)


def reduce_core(partial):
    groups = lax.axis_size(SHARD)
    cols = partial.shape[1]
    core = lax.axis_index("core")
    blocks = partial.reshape(groups, 2, -1, cols)
    keep = lax.dynamic_index_in_dim(blocks, core, axis=1, keepdims=False)
    give = lax.dynamic_index_in_dim(blocks, 1 - core, axis=1, keepdims=False)
    return keep + core_swap(give)


def reduce_rest(halves, wait_for=None):
    core = lax.axis_index("core")
    owned = reduce_group(halves)
    if wait_for is not None:
        owned, wait_for = lax.optimization_barrier((owned, wait_for))
    owned = lax.psum(owned, "rep_hi")
    other = core_swap(owned)
    first = jnp.where(core == 0, owned, other)
    second = jnp.where(core == 0, other, owned)
    return jnp.concatenate([first, second], axis=0)


def reduce_rows(partial, wait_for=None):
    return reduce_rest(reduce_core(partial), wait_for)


def exchange_sum(values, axes):
    for axis in axes:
        size = lax.axis_size(axis)
        step = 1
        while step < size:
            pairs = [(i, i ^ step) for i in range(size)]
            values = values + lax.ppermute(values, axis, pairs)
            step *= 2
    return values


def on_device(
    layer_in,
    cotangent,
    seq_lengths,
    norm_gain,
    in_weight,
    conv_weight,
    conv_bias,
    step_bias,
    decay_log,
    skip_gain,
    gate_gain,
    out_weight,
):
    count = layer_in.shape[0]
    groups = lax.axis_size(SHARD)
    segment = segment_ids(seq_lengths[0], count)
    smalls = (norm_gain, conv_weight, conv_bias, step_bias, decay_log, skip_gain, gate_gain)
    flat = jnp.concatenate([a.reshape(-1) for a in smalls])
    flat_len = flat.shape[0]
    place = lax.axis_index(SHARD)
    spread = jnp.where(
        (jnp.arange(groups, dtype=jnp.int32) == place)[:, None], flat[None, :], 0.0
    )
    flat_all = exchange_sum(spread, ("shard_1", "shard_0"))
    pieces_full = []
    offset = 0
    for a in smalls:
        size = a.size
        block = flat_all[:, offset : offset + size]
        pieces_full.append(block.reshape((groups * a.shape[0],) + a.shape[1:]))
        offset += size
    norm_full, convw_full, convb_full, stepb_full, decay_full, skip_full, gategain_full = pieces_full
    normed_f, norm_back = jax.vjp(norm_input, layer_in, norm_full)
    normed = normed_f.astype(jnp.bfloat16)
    in_whole = gather_rows(in_weight, by_permutes=True)
    out_whole = gather_rows(out_weight)
    projected = halves_product(normed, in_whole, groups)

    def bound_mixer(proj_arg, cw_arg, cb_arg, sb_arg, dl_arg, sk_arg, gg_arg):
        return mixer(proj_arg, segment, cw_arg, cb_arg, sb_arg, dl_arg, sk_arg, gg_arg)

    gated_f, mixer_back = jax.vjp(
        bound_mixer,
        projected,
        convw_full,
        convb_full,
        stepb_full,
        decay_full,
        skip_full,
        gategain_full,
    )
    gated = gated_f.astype(jnp.bfloat16)
    branch_out = halves_product(gated, out_whole, groups)
    layer_out = layer_in + branch_out
    cot_low = cotangent.astype(jnp.bfloat16)
    out_halves = reduce_core(row_product(gated, cot_low))
    gated_grad = halves_back(cot_low, out_whole, groups)
    out_group = reduce_group(out_halves)
    proj_grad, g_convw, g_convb, g_stepb, g_decay, g_skip, g_gategain = mixer_back(gated_grad)
    proj_low = proj_grad.astype(jnp.bfloat16)
    normed_grad = halves_back(proj_low, in_whole, groups)
    back_in, g_norm = norm_back(normed_grad)
    input_grad = cotangent + back_in
    grads = (g_norm, g_convw, g_convb, g_stepb, g_decay, g_skip, g_gategain)
    small_blocks = jnp.concatenate([g.reshape(groups, -1) for g in grads], axis=1)
    small_len = small_blocks.shape[1]
    small_rows = -(-small_len // 2048) * 16
    small_blocks = jnp.pad(small_blocks, ((0, 0), (0, small_rows * 128 - small_len)))
    small_blocks = small_blocks.reshape(groups, small_rows, 128)
    small_blocks = small_blocks + core_swap(small_blocks)
    cols = proj_low.shape[1]
    wide = -(-cols // 128) * 128
    proj_wide = jnp.pad(proj_low, ((0, 0), (0, wide - cols)))
    in_partial = row_product(normed, proj_wide)
    pieces = in_partial.reshape(groups, 2, 2, -1, in_partial.shape[1])
    first, small_group = reduce_group(
        reduce_core(pieces[:, :, 0].reshape(-1, in_partial.shape[1])), small_blocks
    )
    second = reduce_group(reduce_core(pieces[:, :, 1].reshape(-1, in_partial.shape[1])))
    in_group = jnp.concatenate([first, second], axis=0)
    in_shape, out_shape = in_group.shape, out_group.shape
    big_rows = (in_group.size + out_group.size) // 128
    tail_rows = -(-(big_rows + small_group.shape[0]) // 64) * 64 - big_rows
    small_group = jnp.pad(small_group, ((0, tail_rows - small_group.shape[0]), (0, 0)))
    joined = jnp.concatenate(
        [in_group.reshape(-1, 128), out_group.reshape(-1, 128), small_group], axis=0
    )
    joined = allreduce_rep(joined)
    split_at = in_group.size // 128
    split_out = split_at + out_group.size // 128
    in_owned = core_join(joined[:split_at].reshape(in_shape))[:, :cols]
    out_owned = core_join(joined[split_at:split_out].reshape(out_shape))
    mine = joined[split_out:].reshape(-1)[:small_len]
    small_final = []
    offset = 0
    for g in grads:
        size = g.size // groups
        small_final.append(mine[offset : offset + size].reshape((g.shape[0] // groups,) + g.shape[1:]))
        offset += size
    return (
        layer_out,
        input_grad,
        small_final[0],
        in_owned,
        small_final[1],
        small_final[2],
        small_final[3],
        small_final[4],
        small_final[5],
        small_final[6],
        out_owned,
    )


def solution(mesh):
    split = Mesh(
        mesh.devices.reshape(mesh.shape["rep"] // 2, 2, 4, 2),
        ("rep_hi", "core", "shard_0", "shard_1"),
    )
    in_specs = (
        P(REP_SHARD, None),
        P(REP_SHARD, None),
        P(REP_SHARD, None),
        P(SHARD),
        P(SHARD, None),
        P(SHARD, None),
        P(SHARD),
        P(SHARD),
        P(SHARD),
        P(SHARD),
        P(SHARD),
        P(SHARD, None),
    )
    out_specs = (
        P(REP_SHARD, None),
        P(REP_SHARD, None),
        P(SHARD),
        P(SHARD, None),
        P(SHARD, None),
        P(SHARD),
        P(SHARD),
        P(SHARD),
        P(SHARD),
        P(SHARD),
        P(SHARD, None),
    )
    return jax.shard_map(
        on_device, mesh=split, in_specs=in_specs, out_specs=out_specs, check_vma=False
    )
```

```python
import math

import jax
import jax.numpy as jnp
from jax import lax
from jax.sharding import Mesh
from jax.sharding import PartitionSpec as P

SPAN = 256
SHARD = ("shard_0", "shard_1")
REP = ("rep_hi", "core")
REP_SHARD = ("rep_hi", "core", "shard_0", "shard_1")
ALL = REP_SHARD


EPS = 1e-05
HIGH = lax.Precision.HIGHEST


def side_by_side(arrays, axis, dim, along):
    widths = [math.prod(a.shape[along:]) for a in arrays]
    both = jnp.concatenate(
        [a.reshape(*a.shape[:along], w) for a, w in zip(arrays, widths)], axis=along
    )
    result = lax.all_gather(both, axis, axis=dim, tiled=True)
    blocks = jnp.split(result, [sum(widths[:k]) for k in range(1, len(widths))], axis=along)
    return tuple(
        (b.reshape(*result.shape[:along], *a.shape[along:]) for a, b in zip(arrays, blocks))
    )


def sum_by_axis(total, axes):
    for axis in axes:
        total = lax.psum_scatter(total, axis, scatter_dimension=0, tiled=True)
    return total


def in_blocks(shard, dim, size):
    before, after = (shard.shape[:dim], shard.shape[dim + 1 :])
    return jnp.moveaxis(shard.reshape(*before, size, -1, *after), dim, 0)


def sum_at_owner(shard, axis, dim):
    size = lax.axis_size(axis)
    blocks = lax.all_to_all(in_blocks(shard, dim, size), axis, 0, 0, tiled=True)
    return jnp.sum(blocks, axis=0)


def sent_together(arrays, axis, dim, along):
    widths = [math.prod(a.shape[along:]) for a in arrays]
    both = jnp.concatenate(
        [a.reshape(*a.shape[:along], w) for a, w in zip(arrays, widths)], axis=along
    )
    result = sum_at_owner(both, axis, dim)
    blocks = jnp.split(result, [sum(widths[:k]) for k in range(1, len(widths))], axis=along)
    return tuple(
        (b.reshape(*result.shape[:along], *a.shape[along:]) for a, b in zip(arrays, blocks))
    )


def shifted(values, lag):
    zeros_top = jnp.zeros((lag,) + values.shape[1:], values.dtype)
    return jnp.concatenate([zeros_top, values[:-lag]], axis=0)


def segment_ids(lengths_row, count):
    offsets = jnp.cumsum(lengths_row, dtype=jnp.int32) - lengths_row
    places = jnp.arange(count, dtype=jnp.int32)
    return (
        jnp.sum((places[:, None] >= offsets[None, :]).astype(jnp.int32), axis=1, dtype=jnp.int32)
        - 1
    )


def row_product(left, right):
    return lax.dot_general(
        left, right, (((0,), (0,)), ((), ())), preferred_element_type=jnp.float32
    )


def back_product(left, right):
    return lax.dot_general(
        left, right, (((1,), (1,)), ((), ())), preferred_element_type=jnp.float32
    )


def norm_input(inputs, gain_one):
    scaling = lax.rsqrt(jnp.mean(inputs * inputs, axis=1, keepdims=True) + EPS)
    return inputs * scaling * gain_one[None, :]


def mixer(projected, segment, conv_weight, conv_bias, step_bias, decay_log, skip_gain, gate_gain):
    count = projected.shape[0]
    inner = gate_gain.shape[0]
    heads = step_bias.shape[0]
    head_dim = inner // heads
    channels = conv_weight.shape[0]
    state_dim = (channels - inner) // 2
    taps = conv_weight.shape[1]
    gate_part = projected[:, :inner]
    conv_in = projected[:, inner : inner + channels]
    step_raw = projected[:, inner + channels :]
    places = jnp.arange(count, dtype=jnp.int32)
    conv_out = conv_bias[None, :] + conv_weight[:, taps - 1][None, :] * conv_in
    for lag in range(1, taps):
        same = (shifted(segment, lag) == segment) & (places >= lag)
        conv_out = conv_out + jnp.where(
            same[:, None], conv_weight[:, taps - 1 - lag][None, :] * shifted(conv_in, lag), 0.0
        )
    activated = jax.nn.silu(conv_out)
    values = activated[:, :inner].reshape(count, heads, head_dim)
    b_matrix = activated[:, inner : inner + state_dim]
    c_matrix = activated[:, inner + state_dim :]
    step_size = jax.nn.softplus(step_raw + step_bias[None, :])
    decay = -jnp.exp(decay_log)[None, :] * step_size
    blocks = count // SPAN
    values_c = values.reshape(blocks, SPAN, heads, head_dim)
    b_spans = b_matrix.reshape(blocks, SPAN, state_dim)
    c_spans = c_matrix.reshape(blocks, SPAN, state_dim)
    step_c = step_size.reshape(blocks, SPAN, heads)
    cumul = jnp.cumsum(decay.reshape(blocks, SPAN, heads), axis=1)
    seg_c = segment.reshape(blocks, SPAN)
    rows_in = jnp.arange(SPAN, dtype=jnp.int32)
    lower = rows_in[:, None] >= rows_in[None, :]
    allowed = lower[None] & (seg_c[:, :, None] == seg_c[:, None, :])
    cumul_t = jnp.transpose(cumul, (0, 2, 1))
    differ = cumul_t[:, :, :, None] - cumul_t[:, :, None, :]
    weights_l = jnp.exp(jnp.where(allowed[:, None], differ, -10000.0))
    scores = jnp.einsum("cin,cjn->cij", c_spans, b_spans, precision=HIGH)
    mixing = weights_l * scores[:, None]
    scaled_in = values_c * step_c[..., None]
    y_intra = jnp.einsum("chij,cjhp->cihp", mixing, scaled_in, precision=HIGH)
    carried = jnp.zeros((heads, head_dim, state_dim), jnp.float32)
    before_seg = jnp.int32(-1)
    linked = (seg_c[0] == before_seg).astype(jnp.float32)
    reach = jnp.exp(cumul[0]) * linked[:, None]
    inter = jnp.einsum("in,hpn->ihp", c_spans[0], carried, precision=HIGH) * reach[:, :, None]
    pieces = [y_intra[0] + inter]
    y_all = jnp.concatenate(pieces, axis=0) + skip_gain[None, :, None] * values
    gated_pre = y_all.reshape(count, inner) * jax.nn.silu(gate_part)
    scaling = lax.rsqrt(jnp.mean(gated_pre * gated_pre, axis=1, keepdims=True) + EPS)
    return gated_pre * scaling * gate_gain[None, :]


def reduce_group(halves, small=None):
    ring = lax.axis_size("shard_0")
    y = lax.axis_index("shard_1")
    z = lax.axis_index("shard_0")
    up = [(i, (i + 1) % ring) for i in range(ring)]
    down = [(i, (i - 1) % ring) for i in range(ring)]
    items = [(halves, jnp.bfloat16)] + ([] if small is None else [(small, jnp.float32)])
    rels, halfs = [], []
    for values, _ in items:
        blocks = values.reshape((ring, 2) + values.shape[1:])
        doubled = jnp.concatenate([blocks, blocks], axis=0)
        rels.append(lax.dynamic_slice_in_dim(doubled, z, ring, axis=0))
        halfs.append(values.shape[1] // 2)

    def send(parts, pairs):
        return [lax.ppermute(p.astype(w), "shard_0", pairs) for p, (_, w) in zip(parts, items)]

    acc_up = send([r[3][:, :h] for r, h in zip(rels, halfs)], up)
    acc_dn = send([r[1][:, h:] for r, h in zip(rels, halfs)], down)
    acc_up = send([a + r[2][:, :h] for a, r, h in zip(acc_up, rels, halfs)], up)
    acc_dn = send([a + r[2][:, h:] for a, r, h in zip(acc_dn, rels, halfs)], down)
    acc_up = send([a + r[1][:, :h] for a, r, h in zip(acc_up, rels, halfs)], up)
    acc_dn = send([a + r[3][:, h:] for a, r, h in zip(acc_dn, rels, halfs)], down)
    results = []
    for au, ad, r, h, (_, w) in zip(acc_up, acc_dn, rels, halfs, items):
        zsum = jnp.concatenate(
            [au.astype(jnp.float32) + r[0][:, :h], ad.astype(jnp.float32) + r[0][:, h:]], axis=1
        )
        keep = lax.dynamic_index_in_dim(zsum, y, axis=0, keepdims=False)
        give = lax.dynamic_index_in_dim(zsum, 1 - y, axis=0, keepdims=False)
        got = lax.ppermute(give.astype(w), "shard_1", [(0, 1), (1, 0)])
        results.append(keep + got.astype(jnp.float32))
    return results[0] if small is None else results


def allreduce_rep(values):
    ring = 4
    size = lax.axis_size("rep_hi")
    index = lax.axis_index("rep_hi")
    x = index % ring
    up = [(i, (i // ring) * ring + (i % ring + 1) % ring) for i in range(size)]
    down = [(i, (i // ring) * ring + (i % ring - 1) % ring) for i in range(size)]
    rows = values.shape[0]
    chunks = values.reshape(ring, rows // ring, values.shape[1])
    doubled = jnp.concatenate([chunks, chunks], axis=0)
    rel = lax.dynamic_slice_in_dim(doubled, x, ring, axis=0)
    half = rows // ring // 2
    a = lax.ppermute(rel[2][:half], "rep_hi", up)
    b = lax.ppermute(rel[2][half:], "rep_hi", down)
    up_msg = jnp.concatenate([a + rel[1][:half], rel[1][half:]], axis=0)
    down_msg = jnp.concatenate([rel[3][:half], b + rel[3][half:]], axis=0)
    mine = rel[0] + lax.ppermute(up_msg, "rep_hi", up) + lax.ppermute(down_msg, "rep_hi", down)
    step = ring
    while step < size:
        mine = mine + lax.ppermute(mine, "rep_hi", [(i, i ^ step) for i in range(size)])
        step *= 2
    from_prev = lax.ppermute(mine, "rep_hi", up)
    from_next = lax.ppermute(mine, "rep_hi", down)
    far_a = lax.ppermute(from_prev[:half], "rep_hi", up)
    far_b = lax.ppermute(from_next[half:], "rep_hi", down)
    opposite = jnp.concatenate([far_a, far_b], axis=0)
    ordered = jnp.stack([mine, from_next, opposite, from_prev])
    doubled = jnp.concatenate([ordered, ordered], axis=0)
    placed = lax.dynamic_slice_in_dim(doubled, (ring - x) % ring, ring, axis=0)
    return placed.reshape(values.shape)


def core_join(owned):
    core = lax.axis_index("core")
    other = core_swap(owned)
    first = jnp.where(core == 0, owned, other)
    second = jnp.where(core == 0, other, owned)
    return jnp.concatenate([first, second], axis=0)


def core_swap(values):
    return lax.ppermute(values, "core", [(0, 1), (1, 0)])


def gather_group(block, sibling):
    ring = lax.axis_size("shard_0")
    y = lax.axis_index("shard_1")
    z = lax.axis_index("shard_0")
    up = [(i, (i + 1) % ring) for i in range(ring)]
    down = [(i, (i - 1) % ring) for i in range(ring)]
    half = block.shape[0] // 2

    def place(own, got):
        return jnp.where(y == 0, jnp.stack([own, got]), jnp.stack([got, own]))

    def arrange(pair, from_next, opposite, from_prev):
        ordered = jnp.stack([pair, from_next, opposite, from_prev])
        doubled = jnp.concatenate([ordered, ordered], axis=0)
        placed = lax.dynamic_slice_in_dim(doubled, (ring - z) % ring, ring, axis=0)
        return placed.reshape((ring * 2,) + block.shape)

    other_y = lax.ppermute(block, "shard_1", [(0, 1), (1, 0)])
    pair = place(block, other_y)
    from_prev = lax.ppermute(pair, "shard_0", up)
    from_next = lax.ppermute(pair, "shard_0", down)
    pair_s = place(sibling, core_swap(other_y))
    far_a = lax.ppermute(from_prev[:, :half], "shard_0", up)
    far_b = lax.ppermute(from_next[:, half:], "shard_0", down)
    from_prev_s = core_swap(from_prev)
    from_next_s = core_swap(from_next)
    opposite = jnp.concatenate([far_a, far_b], axis=1)
    opposite_s = core_swap(opposite)
    return (
        arrange(pair, from_next, opposite, from_prev),
        arrange(pair_s, from_next_s, opposite_s, from_prev_s),
    )


def core_swap(values):
    return lax.ppermute(values, "core", [(0, 1), (1, 0)])


def gather_rows(weight, by_permutes=False):
    rows = weight.shape[0]
    half = rows // 2
    core = lax.axis_index("core")
    mine = lax.dynamic_slice_in_dim(weight, core * half, half, axis=0)
    if by_permutes:
        sibling = lax.dynamic_slice_in_dim(weight, (1 - core) * half, half, axis=0)
        part, other = gather_group(mine, sibling)
    else:
        part = lax.all_gather(mine, SHARD, axis=0, tiled=False)
        other = core_swap(part)
    return part.reshape(-1, weight.shape[1]), other.reshape(-1, weight.shape[1])


def split_cols(values, groups):
    core = lax.axis_index("core")
    blocks = values.reshape(values.shape[0], groups, 2, -1)
    own = lax.dynamic_index_in_dim(blocks, core, axis=2, keepdims=False)
    other = lax.dynamic_index_in_dim(blocks, 1 - core, axis=2, keepdims=False)
    return own.reshape(values.shape[0], -1), other.reshape(values.shape[0], -1)


def join_cols(own, other, groups):
    core = lax.axis_index("core")
    count = own.shape[0]
    pair = jnp.stack([own.reshape(count, groups, -1), other.reshape(count, groups, -1)], axis=2)
    doubled = jnp.concatenate([pair, pair], axis=2)
    placed = lax.dynamic_slice_in_dim(doubled, core, 2, axis=2)
    return placed.reshape(count, -1)


def halves_product(left, halves, groups):
    own_l, other_l = split_cols(left, groups)
    own_w, other_w = halves
    return jnp.dot(own_l, own_w, preferred_element_type=jnp.float32) + jnp.dot(
        other_l, other_w, preferred_element_type=jnp.float32
    )


def halves_back(left, halves, groups):
    own_w, other_w = halves
    return join_cols(back_product(left, own_w), back_product(left, other_w), groups)


def reduce_core(partial):
    groups = lax.axis_size(SHARD)
    cols = partial.shape[1]
    core = lax.axis_index("core")
    blocks = partial.reshape(groups, 2, -1, cols)
    keep = lax.dynamic_index_in_dim(blocks, core, axis=1, keepdims=False)
    give = lax.dynamic_index_in_dim(blocks, 1 - core, axis=1, keepdims=False)
    return keep + core_swap(give)


def reduce_rest(halves, wait_for=None):
    core = lax.axis_index("core")
    owned = reduce_group(halves)
    if wait_for is not None:
        owned, wait_for = lax.optimization_barrier((owned, wait_for))
    owned = lax.psum(owned, "rep_hi")
    other = core_swap(owned)
    first = jnp.where(core == 0, owned, other)
    second = jnp.where(core == 0, other, owned)
    return jnp.concatenate([first, second], axis=0)


def reduce_rows(partial, wait_for=None):
    return reduce_rest(reduce_core(partial), wait_for)


def exchange_sum(values, axes):
    for axis in axes:
        size = lax.axis_size(axis)
        step = 1
        while step < size:
            pairs = [(i, i ^ step) for i in range(size)]
            values = values + lax.ppermute(values, axis, pairs)
            step *= 2
    return values


def on_device(
    layer_in,
    cotangent,
    seq_lengths,
    norm_gain,
    in_weight,
    conv_weight,
    conv_bias,
    step_bias,
    decay_log,
    skip_gain,
    gate_gain,
    out_weight,
):
    count = layer_in.shape[0]
    groups = lax.axis_size(SHARD)
    segment = segment_ids(seq_lengths[0], count)
    smalls = (norm_gain, conv_weight, conv_bias, step_bias, decay_log, skip_gain, gate_gain)
    flat = jnp.concatenate([a.reshape(-1) for a in smalls])
    flat_len = flat.shape[0]
    place = lax.axis_index(SHARD)
    spread = jnp.where(
        (jnp.arange(groups, dtype=jnp.int32) == place)[:, None], flat[None, :], 0.0
    )
    flat_all = exchange_sum(spread, ("shard_1", "shard_0"))
    pieces_full = []
    offset = 0
    for a in smalls:
        size = a.size
        block = flat_all[:, offset : offset + size]
        pieces_full.append(block.reshape((groups * a.shape[0],) + a.shape[1:]))
        offset += size
    norm_full, convw_full, convb_full, stepb_full, decay_full, skip_full, gategain_full = pieces_full
    normed_f, norm_back = jax.vjp(norm_input, layer_in, norm_full)
    normed = normed_f.astype(jnp.bfloat16)
    in_whole = gather_rows(in_weight, by_permutes=True)
    in_whole, out_weight = lax.optimization_barrier((in_whole, out_weight))
    out_whole = gather_rows(out_weight)
    projected = halves_product(normed, in_whole, groups)

    def bound_mixer(proj_arg, cw_arg, cb_arg, sb_arg, dl_arg, sk_arg, gg_arg):
        return mixer(proj_arg, segment, cw_arg, cb_arg, sb_arg, dl_arg, sk_arg, gg_arg)

    gated_f, mixer_back = jax.vjp(
        bound_mixer,
        projected,
        convw_full,
        convb_full,
        stepb_full,
        decay_full,
        skip_full,
        gategain_full,
    )
    gated = gated_f.astype(jnp.bfloat16)
    branch_out = halves_product(gated, out_whole, groups)
    layer_out = layer_in + branch_out
    cot_low = cotangent.astype(jnp.bfloat16)
    out_halves = reduce_core(row_product(gated, cot_low))
    gated_grad = halves_back(cot_low, out_whole, groups)
    out_group = reduce_group(out_halves)
    proj_grad, g_convw, g_convb, g_stepb, g_decay, g_skip, g_gategain = mixer_back(gated_grad)
    proj_low = proj_grad.astype(jnp.bfloat16)
    normed_grad = halves_back(proj_low, in_whole, groups)
    back_in, g_norm = norm_back(normed_grad)
    input_grad = cotangent + back_in
    grads = (g_norm, g_convw, g_convb, g_stepb, g_decay, g_skip, g_gategain)
    small_blocks = jnp.concatenate([g.reshape(groups, -1) for g in grads], axis=1)
    small_len = small_blocks.shape[1]
    small_rows = -(-small_len // 2048) * 16
    small_blocks = jnp.pad(small_blocks, ((0, 0), (0, small_rows * 128 - small_len)))
    small_blocks = small_blocks.reshape(groups, small_rows, 128)
    small_blocks = small_blocks + core_swap(small_blocks)
    cols = proj_low.shape[1]
    wide = -(-cols // 128) * 128
    proj_wide = jnp.pad(proj_low, ((0, 0), (0, wide - cols)))
    in_group, small_group = reduce_group(
        reduce_core(row_product(normed, proj_wide)), small_blocks
    )
    in_shape, out_shape = in_group.shape, out_group.shape
    big_rows = (in_group.size + out_group.size) // 128
    tail_rows = -(-(big_rows + small_group.shape[0]) // 64) * 64 - big_rows
    small_group = jnp.pad(small_group, ((0, tail_rows - small_group.shape[0]), (0, 0)))
    joined = jnp.concatenate(
        [in_group.reshape(-1, 128), out_group.reshape(-1, 128), small_group], axis=0
    )
    joined = allreduce_rep(joined)
    split_at = in_group.size // 128
    split_out = split_at + out_group.size // 128
    in_owned = core_join(joined[:split_at].reshape(in_shape))[:, :cols]
    out_owned = core_join(joined[split_at:split_out].reshape(out_shape))
    mine = joined[split_out:].reshape(-1)[:small_len]
    small_final = []
    offset = 0
    for g in grads:
        size = g.size // groups
        small_final.append(mine[offset : offset + size].reshape((g.shape[0] // groups,) + g.shape[1:]))
        offset += size
    return (
        layer_out,
        input_grad,
        small_final[0],
        in_owned,
        small_final[1],
        small_final[2],
        small_final[3],
        small_final[4],
        small_final[5],
        small_final[6],
        out_owned,
    )


def solution(mesh):
    split = Mesh(
        mesh.devices.reshape(mesh.shape["rep"] // 2, 2, 4, 2),
        ("rep_hi", "core", "shard_0", "shard_1"),
    )
    in_specs = (
        P(REP_SHARD, None),
        P(REP_SHARD, None),
        P(REP_SHARD, None),
        P(SHARD),
        P(SHARD, None),
        P(SHARD, None),
        P(SHARD),
        P(SHARD),
        P(SHARD),
        P(SHARD),
        P(SHARD),
        P(SHARD, None),
    )
    out_specs = (
        P(REP_SHARD, None),
        P(REP_SHARD, None),
        P(SHARD),
        P(SHARD, None),
        P(SHARD, None),
        P(SHARD),
        P(SHARD),
        P(SHARD),
        P(SHARD),
        P(SHARD),
        P(SHARD, None),
    )
    return jax.shard_map(
        on_device, mesh=split, in_specs=in_specs, out_specs=out_specs, check_vma=False
    )
```

```python
import math

import jax
import jax.numpy as jnp
from jax import lax
from jax.sharding import Mesh
from jax.sharding import PartitionSpec as P

SPAN = 256
SHARD = ("shard_0", "shard_1")
REP = ("rep_hi", "core")
REP_SHARD = ("rep_hi", "core", "shard_0", "shard_1")
ALL = REP_SHARD


EPS = 1e-05
HIGH = lax.Precision.HIGHEST


def side_by_side(arrays, axis, dim, along):
    widths = [math.prod(a.shape[along:]) for a in arrays]
    both = jnp.concatenate(
        [a.reshape(*a.shape[:along], w) for a, w in zip(arrays, widths)], axis=along
    )
    result = lax.all_gather(both, axis, axis=dim, tiled=True)
    blocks = jnp.split(result, [sum(widths[:k]) for k in range(1, len(widths))], axis=along)
    return tuple(
        (b.reshape(*result.shape[:along], *a.shape[along:]) for a, b in zip(arrays, blocks))
    )


def sum_by_axis(total, axes):
    for axis in axes:
        total = lax.psum_scatter(total, axis, scatter_dimension=0, tiled=True)
    return total


def in_blocks(shard, dim, size):
    before, after = (shard.shape[:dim], shard.shape[dim + 1 :])
    return jnp.moveaxis(shard.reshape(*before, size, -1, *after), dim, 0)


def sum_at_owner(shard, axis, dim):
    size = lax.axis_size(axis)
    blocks = lax.all_to_all(in_blocks(shard, dim, size), axis, 0, 0, tiled=True)
    return jnp.sum(blocks, axis=0)


def sent_together(arrays, axis, dim, along):
    widths = [math.prod(a.shape[along:]) for a in arrays]
    both = jnp.concatenate(
        [a.reshape(*a.shape[:along], w) for a, w in zip(arrays, widths)], axis=along
    )
    result = sum_at_owner(both, axis, dim)
    blocks = jnp.split(result, [sum(widths[:k]) for k in range(1, len(widths))], axis=along)
    return tuple(
        (b.reshape(*result.shape[:along], *a.shape[along:]) for a, b in zip(arrays, blocks))
    )


def shifted(values, lag):
    zeros_top = jnp.zeros((lag,) + values.shape[1:], values.dtype)
    return jnp.concatenate([zeros_top, values[:-lag]], axis=0)


def segment_ids(lengths_row, count):
    offsets = jnp.cumsum(lengths_row, dtype=jnp.int32) - lengths_row
    places = jnp.arange(count, dtype=jnp.int32)
    return (
        jnp.sum((places[:, None] >= offsets[None, :]).astype(jnp.int32), axis=1, dtype=jnp.int32)
        - 1
    )


def row_product(left, right):
    return lax.dot_general(
        left, right, (((0,), (0,)), ((), ())), preferred_element_type=jnp.float32
    )


def back_product(left, right):
    return lax.dot_general(
        left, right, (((1,), (1,)), ((), ())), preferred_element_type=jnp.float32
    )


def norm_input(inputs, gain_one):
    scaling = lax.rsqrt(jnp.mean(inputs * inputs, axis=1, keepdims=True) + EPS)
    return inputs * scaling * gain_one[None, :]


def mixer(projected, segment, conv_weight, conv_bias, step_bias, decay_log, skip_gain, gate_gain):
    count = projected.shape[0]
    inner = gate_gain.shape[0]
    heads = step_bias.shape[0]
    head_dim = inner // heads
    channels = conv_weight.shape[0]
    state_dim = (channels - inner) // 2
    taps = conv_weight.shape[1]
    gate_part = projected[:, :inner]
    conv_in = projected[:, inner : inner + channels]
    step_raw = projected[:, inner + channels :]
    places = jnp.arange(count, dtype=jnp.int32)
    conv_out = conv_bias[None, :] + conv_weight[:, taps - 1][None, :] * conv_in
    for lag in range(1, taps):
        same = (shifted(segment, lag) == segment) & (places >= lag)
        conv_out = conv_out + jnp.where(
            same[:, None], conv_weight[:, taps - 1 - lag][None, :] * shifted(conv_in, lag), 0.0
        )
    activated = jax.nn.silu(conv_out)
    values = activated[:, :inner].reshape(count, heads, head_dim)
    b_matrix = activated[:, inner : inner + state_dim]
    c_matrix = activated[:, inner + state_dim :]
    step_size = jax.nn.softplus(step_raw + step_bias[None, :])
    decay = -jnp.exp(decay_log)[None, :] * step_size
    blocks = count // SPAN
    values_c = values.reshape(blocks, SPAN, heads, head_dim)
    b_spans = b_matrix.reshape(blocks, SPAN, state_dim)
    c_spans = c_matrix.reshape(blocks, SPAN, state_dim)
    step_c = step_size.reshape(blocks, SPAN, heads)
    cumul = jnp.cumsum(decay.reshape(blocks, SPAN, heads), axis=1)
    seg_c = segment.reshape(blocks, SPAN)
    rows_in = jnp.arange(SPAN, dtype=jnp.int32)
    lower = rows_in[:, None] >= rows_in[None, :]
    allowed = lower[None] & (seg_c[:, :, None] == seg_c[:, None, :])
    cumul_t = jnp.transpose(cumul, (0, 2, 1))
    differ = cumul_t[:, :, :, None] - cumul_t[:, :, None, :]
    weights_l = jnp.exp(jnp.where(allowed[:, None], differ, -10000.0))
    scores = jnp.einsum("cin,cjn->cij", c_spans, b_spans, precision=HIGH)
    mixing = weights_l * scores[:, None]
    scaled_in = values_c * step_c[..., None]
    y_intra = jnp.einsum("chij,cjhp->cihp", mixing, scaled_in, precision=HIGH)
    carried = jnp.zeros((heads, head_dim, state_dim), jnp.float32)
    before_seg = jnp.int32(-1)
    linked = (seg_c[0] == before_seg).astype(jnp.float32)
    reach = jnp.exp(cumul[0]) * linked[:, None]
    inter = jnp.einsum("in,hpn->ihp", c_spans[0], carried, precision=HIGH) * reach[:, :, None]
    pieces = [y_intra[0] + inter]
    y_all = jnp.concatenate(pieces, axis=0) + skip_gain[None, :, None] * values
    gated_pre = y_all.reshape(count, inner) * jax.nn.silu(gate_part)
    scaling = lax.rsqrt(jnp.mean(gated_pre * gated_pre, axis=1, keepdims=True) + EPS)
    return gated_pre * scaling * gate_gain[None, :]


def reduce_group(halves, small=None):
    ring = lax.axis_size("shard_0")
    y = lax.axis_index("shard_1")
    z = lax.axis_index("shard_0")
    up = [(i, (i + 1) % ring) for i in range(ring)]
    down = [(i, (i - 1) % ring) for i in range(ring)]
    items = [(halves, jnp.bfloat16)] + ([] if small is None else [(small, jnp.float32)])
    rels, halfs = [], []
    for values, _ in items:
        blocks = values.reshape((ring, 2) + values.shape[1:])
        doubled = jnp.concatenate([blocks, blocks], axis=0)
        rels.append(lax.dynamic_slice_in_dim(doubled, z, ring, axis=0))
        halfs.append(values.shape[1] // 2)

    def send(parts, pairs):
        return [lax.ppermute(p.astype(w), "shard_0", pairs) for p, (_, w) in zip(parts, items)]

    acc_up = send([r[3][:, :h] for r, h in zip(rels, halfs)], up)
    acc_dn = send([r[1][:, h:] for r, h in zip(rels, halfs)], down)
    acc_up = send([a + r[2][:, :h] for a, r, h in zip(acc_up, rels, halfs)], up)
    acc_dn = send([a + r[2][:, h:] for a, r, h in zip(acc_dn, rels, halfs)], down)
    acc_up = send([a + r[1][:, :h] for a, r, h in zip(acc_up, rels, halfs)], up)
    acc_dn = send([a + r[3][:, h:] for a, r, h in zip(acc_dn, rels, halfs)], down)
    results = []
    for au, ad, r, h, (_, w) in zip(acc_up, acc_dn, rels, halfs, items):
        zsum = jnp.concatenate(
            [au.astype(jnp.float32) + r[0][:, :h], ad.astype(jnp.float32) + r[0][:, h:]], axis=1
        )
        keep = lax.dynamic_index_in_dim(zsum, y, axis=0, keepdims=False)
        give = lax.dynamic_index_in_dim(zsum, 1 - y, axis=0, keepdims=False)
        got = lax.ppermute(give.astype(w), "shard_1", [(0, 1), (1, 0)])
        results.append(keep + got.astype(jnp.float32))
    return results[0] if small is None else results


def allreduce_rep(values):
    ring = 4
    size = lax.axis_size("rep_hi")
    index = lax.axis_index("rep_hi")
    x = index % ring
    up = [(i, (i // ring) * ring + (i % ring + 1) % ring) for i in range(size)]
    down = [(i, (i // ring) * ring + (i % ring - 1) % ring) for i in range(size)]
    rows = values.shape[0]
    chunks = values.reshape(ring, rows // ring, values.shape[1])
    doubled = jnp.concatenate([chunks, chunks], axis=0)
    rel = lax.dynamic_slice_in_dim(doubled, x, ring, axis=0)
    half = rows // ring // 2
    a = lax.ppermute(rel[2][:half], "rep_hi", up)
    b = lax.ppermute(rel[2][half:], "rep_hi", down)
    up_msg = jnp.concatenate([a + rel[1][:half], rel[1][half:]], axis=0)
    down_msg = jnp.concatenate([rel[3][:half], b + rel[3][half:]], axis=0)
    mine = rel[0] + lax.ppermute(up_msg, "rep_hi", up) + lax.ppermute(down_msg, "rep_hi", down)
    step = ring
    while step < size:
        mine = mine + lax.ppermute(mine, "rep_hi", [(i, i ^ step) for i in range(size)])
        step *= 2
    from_prev = lax.ppermute(mine, "rep_hi", up)
    from_next = lax.ppermute(mine, "rep_hi", down)
    far_a = lax.ppermute(from_prev[:half], "rep_hi", up)
    far_b = lax.ppermute(from_next[half:], "rep_hi", down)
    opposite = jnp.concatenate([far_a, far_b], axis=0)
    ordered = jnp.stack([mine, from_next, opposite, from_prev])
    doubled = jnp.concatenate([ordered, ordered], axis=0)
    placed = lax.dynamic_slice_in_dim(doubled, (ring - x) % ring, ring, axis=0)
    return placed.reshape(values.shape)


def core_join(owned):
    core = lax.axis_index("core")
    other = core_swap(owned)
    first = jnp.where(core == 0, owned, other)
    second = jnp.where(core == 0, other, owned)
    return jnp.concatenate([first, second], axis=0)


def core_swap(values):
    return lax.ppermute(values, "core", [(0, 1), (1, 0)])


def gather_group(block, sibling):
    ring = lax.axis_size("shard_0")
    y = lax.axis_index("shard_1")
    z = lax.axis_index("shard_0")
    up = [(i, (i + 1) % ring) for i in range(ring)]
    down = [(i, (i - 1) % ring) for i in range(ring)]
    half = block.shape[0] // 2

    def place(own, got):
        return jnp.where(y == 0, jnp.stack([own, got]), jnp.stack([got, own]))

    def arrange(pair, from_next, opposite, from_prev):
        ordered = jnp.stack([pair, from_next, opposite, from_prev])
        doubled = jnp.concatenate([ordered, ordered], axis=0)
        placed = lax.dynamic_slice_in_dim(doubled, (ring - z) % ring, ring, axis=0)
        return placed.reshape((ring * 2,) + block.shape)

    other_y = lax.ppermute(block, "shard_1", [(0, 1), (1, 0)])
    pair = place(block, other_y)
    from_prev = lax.ppermute(pair, "shard_0", up)
    from_next = lax.ppermute(pair, "shard_0", down)
    pair_s = place(sibling, core_swap(other_y))
    far_a = lax.ppermute(from_prev[:, :half], "shard_0", up)
    far_b = lax.ppermute(from_next[:, half:], "shard_0", down)
    from_prev_s = core_swap(from_prev)
    from_next_s = core_swap(from_next)
    opposite = jnp.concatenate([far_a, far_b], axis=1)
    opposite_s = core_swap(opposite)
    return (
        arrange(pair, from_next, opposite, from_prev),
        arrange(pair_s, from_next_s, opposite_s, from_prev_s),
    )


def core_swap(values):
    return lax.ppermute(values, "core", [(0, 1), (1, 0)])


def gather_rows(weight, by_permutes=False):
    rows = weight.shape[0]
    half = rows // 2
    core = lax.axis_index("core")
    mine = lax.dynamic_slice_in_dim(weight, core * half, half, axis=0)
    if by_permutes:
        sibling = lax.dynamic_slice_in_dim(weight, (1 - core) * half, half, axis=0)
        part, other = gather_group(mine, sibling)
    else:
        part = lax.all_gather(mine, SHARD, axis=0, tiled=False)
        other = core_swap(part)
    return part.reshape(-1, weight.shape[1]), other.reshape(-1, weight.shape[1])


def split_cols(values, groups):
    core = lax.axis_index("core")
    blocks = values.reshape(values.shape[0], groups, 2, -1)
    own = lax.dynamic_index_in_dim(blocks, core, axis=2, keepdims=False)
    other = lax.dynamic_index_in_dim(blocks, 1 - core, axis=2, keepdims=False)
    return own.reshape(values.shape[0], -1), other.reshape(values.shape[0], -1)


def join_cols(own, other, groups):
    core = lax.axis_index("core")
    count = own.shape[0]
    pair = jnp.stack([own.reshape(count, groups, -1), other.reshape(count, groups, -1)], axis=2)
    doubled = jnp.concatenate([pair, pair], axis=2)
    placed = lax.dynamic_slice_in_dim(doubled, core, 2, axis=2)
    return placed.reshape(count, -1)


def halves_product(left, halves, groups):
    own_l, other_l = split_cols(left, groups)
    own_w, other_w = halves
    return jnp.dot(own_l, own_w, preferred_element_type=jnp.float32) + jnp.dot(
        other_l, other_w, preferred_element_type=jnp.float32
    )


def halves_back(left, halves, groups):
    own_w, other_w = halves
    return join_cols(back_product(left, own_w), back_product(left, other_w), groups)


def reduce_core(partial):
    groups = lax.axis_size(SHARD)
    cols = partial.shape[1]
    core = lax.axis_index("core")
    blocks = partial.reshape(groups, 2, -1, cols)
    keep = lax.dynamic_index_in_dim(blocks, core, axis=1, keepdims=False)
    give = lax.dynamic_index_in_dim(blocks, 1 - core, axis=1, keepdims=False)
    return keep + core_swap(give.astype(jnp.bfloat16)).astype(jnp.float32)


def reduce_rest(halves, wait_for=None):
    core = lax.axis_index("core")
    owned = reduce_group(halves)
    if wait_for is not None:
        owned, wait_for = lax.optimization_barrier((owned, wait_for))
    owned = lax.psum(owned, "rep_hi")
    other = core_swap(owned)
    first = jnp.where(core == 0, owned, other)
    second = jnp.where(core == 0, other, owned)
    return jnp.concatenate([first, second], axis=0)


def reduce_rows(partial, wait_for=None):
    return reduce_rest(reduce_core(partial), wait_for)


def exchange_sum(values, axes):
    for axis in axes:
        size = lax.axis_size(axis)
        step = 1
        while step < size:
            pairs = [(i, i ^ step) for i in range(size)]
            values = values + lax.ppermute(values, axis, pairs)
            step *= 2
    return values


def on_device(
    layer_in,
    cotangent,
    seq_lengths,
    norm_gain,
    in_weight,
    conv_weight,
    conv_bias,
    step_bias,
    decay_log,
    skip_gain,
    gate_gain,
    out_weight,
):
    count = layer_in.shape[0]
    groups = lax.axis_size(SHARD)
    segment = segment_ids(seq_lengths[0], count)
    smalls = (norm_gain, conv_weight, conv_bias, step_bias, decay_log, skip_gain, gate_gain)
    flat = jnp.concatenate([a.reshape(-1) for a in smalls])
    flat_len = flat.shape[0]
    place = lax.axis_index(SHARD)
    spread = jnp.where(
        (jnp.arange(groups, dtype=jnp.int32) == place)[:, None], flat[None, :], 0.0
    )
    flat_all = exchange_sum(spread, ("shard_1", "shard_0"))
    pieces_full = []
    offset = 0
    for a in smalls:
        size = a.size
        block = flat_all[:, offset : offset + size]
        pieces_full.append(block.reshape((groups * a.shape[0],) + a.shape[1:]))
        offset += size
    norm_full, convw_full, convb_full, stepb_full, decay_full, skip_full, gategain_full = pieces_full
    normed_f, norm_back = jax.vjp(norm_input, layer_in, norm_full)
    normed = normed_f.astype(jnp.bfloat16)
    in_whole = gather_rows(in_weight, by_permutes=True)
    out_whole = gather_rows(out_weight)
    projected = halves_product(normed, in_whole, groups)

    def bound_mixer(proj_arg, cw_arg, cb_arg, sb_arg, dl_arg, sk_arg, gg_arg):
        return mixer(proj_arg, segment, cw_arg, cb_arg, sb_arg, dl_arg, sk_arg, gg_arg)

    gated_f, mixer_back = jax.vjp(
        bound_mixer,
        projected,
        convw_full,
        convb_full,
        stepb_full,
        decay_full,
        skip_full,
        gategain_full,
    )
    gated = gated_f.astype(jnp.bfloat16)
    branch_out = halves_product(gated, out_whole, groups)
    layer_out = layer_in + branch_out
    cot_low = cotangent.astype(jnp.bfloat16)
    out_halves = reduce_core(row_product(gated, cot_low))
    gated_grad = halves_back(cot_low, out_whole, groups)
    out_group = reduce_group(out_halves)
    proj_grad, g_convw, g_convb, g_stepb, g_decay, g_skip, g_gategain = mixer_back(gated_grad)
    proj_low = proj_grad.astype(jnp.bfloat16)
    normed_grad = halves_back(proj_low, in_whole, groups)
    back_in, g_norm = norm_back(normed_grad)
    input_grad = cotangent + back_in
    grads = (g_norm, g_convw, g_convb, g_stepb, g_decay, g_skip, g_gategain)
    small_blocks = jnp.concatenate([g.reshape(groups, -1) for g in grads], axis=1)
    small_len = small_blocks.shape[1]
    small_rows = -(-small_len // 2048) * 16
    small_blocks = jnp.pad(small_blocks, ((0, 0), (0, small_rows * 128 - small_len)))
    small_blocks = small_blocks.reshape(groups, small_rows, 128)
    small_blocks = small_blocks + core_swap(small_blocks)
    cols = proj_low.shape[1]
    wide = -(-cols // 128) * 128
    proj_wide = jnp.pad(proj_low, ((0, 0), (0, wide - cols)))
    in_group, small_group = reduce_group(
        reduce_core(row_product(normed, proj_wide)), small_blocks
    )
    in_shape, out_shape = in_group.shape, out_group.shape
    big_rows = (in_group.size + out_group.size) // 128
    tail_rows = -(-(big_rows + small_group.shape[0]) // 64) * 64 - big_rows
    small_group = jnp.pad(small_group, ((0, tail_rows - small_group.shape[0]), (0, 0)))
    joined = jnp.concatenate(
        [in_group.reshape(-1, 128), out_group.reshape(-1, 128), small_group], axis=0
    )
    joined = allreduce_rep(joined)
    split_at = in_group.size // 128
    split_out = split_at + out_group.size // 128
    in_owned = core_join(joined[:split_at].reshape(in_shape))[:, :cols]
    out_owned = core_join(joined[split_at:split_out].reshape(out_shape))
    mine = joined[split_out:].reshape(-1)[:small_len]
    small_final = []
    offset = 0
    for g in grads:
        size = g.size // groups
        small_final.append(mine[offset : offset + size].reshape((g.shape[0] // groups,) + g.shape[1:]))
        offset += size
    return (
        layer_out,
        input_grad,
        small_final[0],
        in_owned,
        small_final[1],
        small_final[2],
        small_final[3],
        small_final[4],
        small_final[5],
        small_final[6],
        out_owned,
    )


def solution(mesh):
    split = Mesh(
        mesh.devices.reshape(mesh.shape["rep"] // 2, 2, 4, 2),
        ("rep_hi", "core", "shard_0", "shard_1"),
    )
    in_specs = (
        P(REP_SHARD, None),
        P(REP_SHARD, None),
        P(REP_SHARD, None),
        P(SHARD),
        P(SHARD, None),
        P(SHARD, None),
        P(SHARD),
        P(SHARD),
        P(SHARD),
        P(SHARD),
        P(SHARD),
        P(SHARD, None),
    )
    out_specs = (
        P(REP_SHARD, None),
        P(REP_SHARD, None),
        P(SHARD),
        P(SHARD, None),
        P(SHARD, None),
        P(SHARD),
        P(SHARD),
        P(SHARD),
        P(SHARD),
        P(SHARD),
        P(SHARD, None),
    )
    return jax.shard_map(
        on_device, mesh=split, in_specs=in_specs, out_specs=out_specs, check_vma=False
    )
```

```python
import math

import jax
import jax.numpy as jnp
from jax import lax
from jax.sharding import Mesh
from jax.sharding import PartitionSpec as P

SPAN = 256
SHARD = ("shard_0", "shard_1")
REP = ("rep_hi", "core")
REP_SHARD = ("rep_hi", "core", "shard_0", "shard_1")
ALL = REP_SHARD


EPS = 1e-05
HIGH = lax.Precision.HIGHEST


def side_by_side(arrays, axis, dim, along):
    widths = [math.prod(a.shape[along:]) for a in arrays]
    both = jnp.concatenate(
        [a.reshape(*a.shape[:along], w) for a, w in zip(arrays, widths)], axis=along
    )
    result = lax.all_gather(both, axis, axis=dim, tiled=True)
    blocks = jnp.split(result, [sum(widths[:k]) for k in range(1, len(widths))], axis=along)
    return tuple(
        (b.reshape(*result.shape[:along], *a.shape[along:]) for a, b in zip(arrays, blocks))
    )


def sum_by_axis(total, axes):
    for axis in axes:
        total = lax.psum_scatter(total, axis, scatter_dimension=0, tiled=True)
    return total


def in_blocks(shard, dim, size):
    before, after = (shard.shape[:dim], shard.shape[dim + 1 :])
    return jnp.moveaxis(shard.reshape(*before, size, -1, *after), dim, 0)


def sum_at_owner(shard, axis, dim):
    size = lax.axis_size(axis)
    blocks = lax.all_to_all(in_blocks(shard, dim, size), axis, 0, 0, tiled=True)
    return jnp.sum(blocks, axis=0)


def sent_together(arrays, axis, dim, along):
    widths = [math.prod(a.shape[along:]) for a in arrays]
    both = jnp.concatenate(
        [a.reshape(*a.shape[:along], w) for a, w in zip(arrays, widths)], axis=along
    )
    result = sum_at_owner(both, axis, dim)
    blocks = jnp.split(result, [sum(widths[:k]) for k in range(1, len(widths))], axis=along)
    return tuple(
        (b.reshape(*result.shape[:along], *a.shape[along:]) for a, b in zip(arrays, blocks))
    )


def shifted(values, lag):
    zeros_top = jnp.zeros((lag,) + values.shape[1:], values.dtype)
    return jnp.concatenate([zeros_top, values[:-lag]], axis=0)


def segment_ids(lengths_row, count):
    offsets = jnp.cumsum(lengths_row, dtype=jnp.int32) - lengths_row
    places = jnp.arange(count, dtype=jnp.int32)
    return (
        jnp.sum((places[:, None] >= offsets[None, :]).astype(jnp.int32), axis=1, dtype=jnp.int32)
        - 1
    )


def row_product(left, right):
    return lax.dot_general(
        left, right, (((0,), (0,)), ((), ())), preferred_element_type=jnp.float32
    )


def back_product(left, right):
    return lax.dot_general(
        left, right, (((1,), (1,)), ((), ())), preferred_element_type=jnp.float32
    )


def norm_input(inputs, gain_one):
    scaling = lax.rsqrt(jnp.mean(inputs * inputs, axis=1, keepdims=True) + EPS)
    return inputs * scaling * gain_one[None, :]


def mixer(projected, segment, conv_weight, conv_bias, step_bias, decay_log, skip_gain, gate_gain):
    count = projected.shape[0]
    inner = gate_gain.shape[0]
    heads = step_bias.shape[0]
    head_dim = inner // heads
    channels = conv_weight.shape[0]
    state_dim = (channels - inner) // 2
    taps = conv_weight.shape[1]
    gate_part = projected[:, :inner]
    conv_in = projected[:, inner : inner + channels]
    step_raw = projected[:, inner + channels :]
    places = jnp.arange(count, dtype=jnp.int32)
    conv_out = conv_bias[None, :] + conv_weight[:, taps - 1][None, :] * conv_in
    for lag in range(1, taps):
        same = (shifted(segment, lag) == segment) & (places >= lag)
        conv_out = conv_out + jnp.where(
            same[:, None], conv_weight[:, taps - 1 - lag][None, :] * shifted(conv_in, lag), 0.0
        )
    activated = jax.nn.silu(conv_out)
    values = activated[:, :inner].reshape(count, heads, head_dim)
    b_matrix = activated[:, inner : inner + state_dim]
    c_matrix = activated[:, inner + state_dim :]
    step_size = jax.nn.softplus(step_raw + step_bias[None, :])
    decay = -jnp.exp(decay_log)[None, :] * step_size
    blocks = count // SPAN
    values_c = values.reshape(blocks, SPAN, heads, head_dim)
    b_spans = b_matrix.reshape(blocks, SPAN, state_dim)
    c_spans = c_matrix.reshape(blocks, SPAN, state_dim)
    step_c = step_size.reshape(blocks, SPAN, heads)
    cumul = jnp.cumsum(decay.reshape(blocks, SPAN, heads), axis=1)
    seg_c = segment.reshape(blocks, SPAN)
    rows_in = jnp.arange(SPAN, dtype=jnp.int32)
    lower = rows_in[:, None] >= rows_in[None, :]
    allowed = lower[None] & (seg_c[:, :, None] == seg_c[:, None, :])
    cumul_t = jnp.transpose(cumul, (0, 2, 1))
    differ = cumul_t[:, :, :, None] - cumul_t[:, :, None, :]
    weights_l = jnp.exp(jnp.where(allowed[:, None], differ, -10000.0))
    scores = jnp.einsum("cin,cjn->cij", c_spans, b_spans, precision=HIGH)
    mixing = weights_l * scores[:, None]
    scaled_in = values_c * step_c[..., None]
    y_intra = jnp.einsum("chij,cjhp->cihp", mixing, scaled_in, precision=HIGH)
    carried = jnp.zeros((heads, head_dim, state_dim), jnp.float32)
    before_seg = jnp.int32(-1)
    linked = (seg_c[0] == before_seg).astype(jnp.float32)
    reach = jnp.exp(cumul[0]) * linked[:, None]
    inter = jnp.einsum("in,hpn->ihp", c_spans[0], carried, precision=HIGH) * reach[:, :, None]
    pieces = [y_intra[0] + inter]
    y_all = jnp.concatenate(pieces, axis=0) + skip_gain[None, :, None] * values
    gated_pre = y_all.reshape(count, inner) * jax.nn.silu(gate_part)
    scaling = lax.rsqrt(jnp.mean(gated_pre * gated_pre, axis=1, keepdims=True) + EPS)
    return gated_pre * scaling * gate_gain[None, :]


def reduce_group(halves, small=None):
    ring = lax.axis_size("shard_0")
    y = lax.axis_index("shard_1")
    z = lax.axis_index("shard_0")
    up = [(i, (i + 1) % ring) for i in range(ring)]
    down = [(i, (i - 1) % ring) for i in range(ring)]
    items = [(halves, jnp.bfloat16)] + ([] if small is None else [(small, jnp.float32)])
    rels, halfs = [], []
    for values, _ in items:
        blocks = values.reshape((ring, 2) + values.shape[1:])
        doubled = jnp.concatenate([blocks, blocks], axis=0)
        rels.append(lax.dynamic_slice_in_dim(doubled, z, ring, axis=0))
        halfs.append(values.shape[1] // 2)

    def send(parts, pairs):
        return [lax.ppermute(p.astype(w), "shard_0", pairs) for p, (_, w) in zip(parts, items)]

    acc_up = send([r[3][:, :h] for r, h in zip(rels, halfs)], up)
    acc_dn = send([r[1][:, h:] for r, h in zip(rels, halfs)], down)
    acc_up = send([a + r[2][:, :h] for a, r, h in zip(acc_up, rels, halfs)], up)
    acc_dn = send([a + r[2][:, h:] for a, r, h in zip(acc_dn, rels, halfs)], down)
    acc_up = send([a + r[1][:, :h] for a, r, h in zip(acc_up, rels, halfs)], up)
    acc_dn = send([a + r[3][:, h:] for a, r, h in zip(acc_dn, rels, halfs)], down)
    results = []
    for au, ad, r, h, (_, w) in zip(acc_up, acc_dn, rels, halfs, items):
        zsum = jnp.concatenate(
            [au.astype(jnp.float32) + r[0][:, :h], ad.astype(jnp.float32) + r[0][:, h:]], axis=1
        )
        keep = lax.dynamic_index_in_dim(zsum, y, axis=0, keepdims=False)
        give = lax.dynamic_index_in_dim(zsum, 1 - y, axis=0, keepdims=False)
        got = lax.ppermute(give.astype(w), "shard_1", [(0, 1), (1, 0)])
        results.append(keep + got.astype(jnp.float32))
    return results[0] if small is None else results


def allreduce_rep(values):
    ring = 4
    size = lax.axis_size("rep_hi")
    index = lax.axis_index("rep_hi")
    x = index % ring
    up = [(i, (i // ring) * ring + (i % ring + 1) % ring) for i in range(size)]
    down = [(i, (i // ring) * ring + (i % ring - 1) % ring) for i in range(size)]
    rows = values.shape[0]
    chunks = values.reshape(ring, rows // ring, values.shape[1])
    doubled = jnp.concatenate([chunks, chunks], axis=0)
    rel = lax.dynamic_slice_in_dim(doubled, x, ring, axis=0)
    half = rows // ring // 2
    a = lax.ppermute(rel[2][:half], "rep_hi", up)
    b = lax.ppermute(rel[2][half:], "rep_hi", down)
    up_msg = jnp.concatenate([a + rel[1][:half], rel[1][half:]], axis=0)
    down_msg = jnp.concatenate([rel[3][:half], b + rel[3][half:]], axis=0)
    mine = rel[0] + lax.ppermute(up_msg, "rep_hi", up) + lax.ppermute(down_msg, "rep_hi", down)
    step = ring
    while step < size:
        mine = mine + lax.ppermute(mine, "rep_hi", [(i, i ^ step) for i in range(size)])
        step *= 2
    from_prev = lax.ppermute(mine, "rep_hi", up)
    from_next = lax.ppermute(mine, "rep_hi", down)
    far_a = lax.ppermute(from_prev[:half], "rep_hi", up)
    far_b = lax.ppermute(from_next[half:], "rep_hi", down)
    opposite = jnp.concatenate([far_a, far_b], axis=0)
    ordered = jnp.stack([mine, from_next, opposite, from_prev])
    doubled = jnp.concatenate([ordered, ordered], axis=0)
    placed = lax.dynamic_slice_in_dim(doubled, (ring - x) % ring, ring, axis=0)
    return placed.reshape(values.shape)


def core_join(owned):
    core = lax.axis_index("core")
    other = core_swap(owned)
    rows = owned.shape[0]
    trio = jnp.concatenate([owned, other, owned], axis=0)
    return lax.dynamic_slice_in_dim(trio, core * rows, 2 * rows, axis=0)


def core_swap(values):
    return lax.ppermute(values, "core", [(0, 1), (1, 0)])


def gather_group(block, sibling):
    ring = lax.axis_size("shard_0")
    y = lax.axis_index("shard_1")
    z = lax.axis_index("shard_0")
    up = [(i, (i + 1) % ring) for i in range(ring)]
    down = [(i, (i - 1) % ring) for i in range(ring)]
    half = block.shape[0] // 2

    def place(own, got):
        pair = jnp.stack([own, got, own])
        return lax.dynamic_slice_in_dim(pair, y, 2, axis=0)

    def arrange(pair, from_next, opposite, from_prev):
        ordered = jnp.stack([pair, from_next, opposite, from_prev])
        doubled = jnp.concatenate([ordered, ordered], axis=0)
        placed = lax.dynamic_slice_in_dim(doubled, (ring - z) % ring, ring, axis=0)
        return placed.reshape((ring * 2,) + block.shape)

    other_y = lax.ppermute(block, "shard_1", [(0, 1), (1, 0)])
    pair = place(block, other_y)
    from_prev = lax.ppermute(pair, "shard_0", up)
    from_next = lax.ppermute(pair, "shard_0", down)
    pair_s = place(sibling, core_swap(other_y))
    far_a = lax.ppermute(from_prev[:, :half], "shard_0", up)
    far_b = lax.ppermute(from_next[:, half:], "shard_0", down)
    from_prev_s = core_swap(from_prev)
    from_next_s = core_swap(from_next)
    opposite = jnp.concatenate([far_a, far_b], axis=1)
    opposite_s = core_swap(opposite)
    return (
        arrange(pair, from_next, opposite, from_prev),
        arrange(pair_s, from_next_s, opposite_s, from_prev_s),
    )


def core_swap(values):
    return lax.ppermute(values, "core", [(0, 1), (1, 0)])


def gather_rows(weight, by_permutes=False):
    rows = weight.shape[0]
    half = rows // 2
    core = lax.axis_index("core")
    mine = lax.dynamic_slice_in_dim(weight, core * half, half, axis=0)
    if by_permutes:
        sibling = lax.dynamic_slice_in_dim(weight, (1 - core) * half, half, axis=0)
        part, other = gather_group(mine, sibling)
    else:
        part = lax.all_gather(mine, SHARD, axis=0, tiled=False)
        other = core_swap(part)
    return part.reshape(-1, weight.shape[1]), other.reshape(-1, weight.shape[1])


def split_cols(values, groups):
    core = lax.axis_index("core")
    blocks = values.reshape(values.shape[0], groups, 2, -1)
    own = lax.dynamic_index_in_dim(blocks, core, axis=2, keepdims=False)
    other = lax.dynamic_index_in_dim(blocks, 1 - core, axis=2, keepdims=False)
    return own.reshape(values.shape[0], -1), other.reshape(values.shape[0], -1)


def join_cols(own, other, groups):
    core = lax.axis_index("core")
    count = own.shape[0]
    pair = jnp.stack([own.reshape(count, groups, -1), other.reshape(count, groups, -1)], axis=2)
    doubled = jnp.concatenate([pair, pair], axis=2)
    placed = lax.dynamic_slice_in_dim(doubled, core, 2, axis=2)
    return placed.reshape(count, -1)


def halves_product(left, halves, groups):
    own_l, other_l = split_cols(left, groups)
    own_w, other_w = halves
    return jnp.dot(own_l, own_w, preferred_element_type=jnp.float32) + jnp.dot(
        other_l, other_w, preferred_element_type=jnp.float32
    )


def halves_back(left, halves, groups):
    own_w, other_w = halves
    return join_cols(back_product(left, own_w), back_product(left, other_w), groups)


def reduce_core(partial):
    groups = lax.axis_size(SHARD)
    cols = partial.shape[1]
    core = lax.axis_index("core")
    blocks = partial.reshape(groups, 2, -1, cols)
    keep = lax.dynamic_index_in_dim(blocks, core, axis=1, keepdims=False)
    give = lax.dynamic_index_in_dim(blocks, 1 - core, axis=1, keepdims=False)
    return keep + core_swap(give.astype(jnp.bfloat16)).astype(jnp.float32)


def reduce_rest(halves, wait_for=None):
    core = lax.axis_index("core")
    owned = reduce_group(halves)
    if wait_for is not None:
        owned, wait_for = lax.optimization_barrier((owned, wait_for))
    owned = lax.psum(owned, "rep_hi")
    other = core_swap(owned)
    first = jnp.where(core == 0, owned, other)
    second = jnp.where(core == 0, other, owned)
    return jnp.concatenate([first, second], axis=0)


def reduce_rows(partial, wait_for=None):
    return reduce_rest(reduce_core(partial), wait_for)


def exchange_sum(values, axes):
    for axis in axes:
        size = lax.axis_size(axis)
        step = 1
        while step < size:
            pairs = [(i, i ^ step) for i in range(size)]
            values = values + lax.ppermute(values, axis, pairs)
            step *= 2
    return values


def on_device(
    layer_in,
    cotangent,
    seq_lengths,
    norm_gain,
    in_weight,
    conv_weight,
    conv_bias,
    step_bias,
    decay_log,
    skip_gain,
    gate_gain,
    out_weight,
):
    count = layer_in.shape[0]
    groups = lax.axis_size(SHARD)
    segment = segment_ids(seq_lengths[0], count)
    smalls = (norm_gain, conv_weight, conv_bias, step_bias, decay_log, skip_gain, gate_gain)
    flat = jnp.concatenate([a.reshape(-1) for a in smalls])
    flat_len = flat.shape[0]
    place = lax.axis_index(SHARD)
    spread = jnp.where(
        (jnp.arange(groups, dtype=jnp.int32) == place)[:, None], flat[None, :], 0.0
    )
    flat_all = exchange_sum(spread, ("shard_1", "shard_0"))
    pieces_full = []
    offset = 0
    for a in smalls:
        size = a.size
        block = flat_all[:, offset : offset + size]
        pieces_full.append(block.reshape((groups * a.shape[0],) + a.shape[1:]))
        offset += size
    norm_full, convw_full, convb_full, stepb_full, decay_full, skip_full, gategain_full = pieces_full
    normed_f, norm_back = jax.vjp(norm_input, layer_in, norm_full)
    normed = normed_f.astype(jnp.bfloat16)
    in_whole = gather_rows(in_weight, by_permutes=True)
    out_whole = gather_rows(out_weight)
    projected = halves_product(normed, in_whole, groups)

    def bound_mixer(proj_arg, cw_arg, cb_arg, sb_arg, dl_arg, sk_arg, gg_arg):
        return mixer(proj_arg, segment, cw_arg, cb_arg, sb_arg, dl_arg, sk_arg, gg_arg)

    gated_f, mixer_back = jax.vjp(
        bound_mixer,
        projected,
        convw_full,
        convb_full,
        stepb_full,
        decay_full,
        skip_full,
        gategain_full,
    )
    gated = gated_f.astype(jnp.bfloat16)
    branch_out = halves_product(gated, out_whole, groups)
    layer_out = layer_in + branch_out
    cot_low = cotangent.astype(jnp.bfloat16)
    out_halves = reduce_core(row_product(gated, cot_low))
    gated_grad = halves_back(cot_low, out_whole, groups)
    out_group = reduce_group(out_halves)
    proj_grad, g_convw, g_convb, g_stepb, g_decay, g_skip, g_gategain = mixer_back(gated_grad)
    proj_low = proj_grad.astype(jnp.bfloat16)
    normed_grad = halves_back(proj_low, in_whole, groups)
    back_in, g_norm = norm_back(normed_grad)
    input_grad = cotangent + back_in
    grads = (g_norm, g_convw, g_convb, g_stepb, g_decay, g_skip, g_gategain)
    small_blocks = jnp.concatenate([g.reshape(groups, -1) for g in grads], axis=1)
    small_len = small_blocks.shape[1]
    small_rows = -(-small_len // 2048) * 16
    small_blocks = jnp.pad(small_blocks, ((0, 0), (0, small_rows * 128 - small_len)))
    small_blocks = small_blocks.reshape(groups, small_rows, 128)
    small_blocks = small_blocks + core_swap(small_blocks)
    cols = proj_low.shape[1]
    wide = -(-cols // 128) * 128
    proj_wide = jnp.pad(proj_low, ((0, 0), (0, wide - cols)))
    in_group, small_group = reduce_group(
        reduce_core(row_product(normed, proj_wide)), small_blocks
    )
    in_shape, out_shape = in_group.shape, out_group.shape
    big_rows = (in_group.size + out_group.size) // 128
    tail_rows = -(-(big_rows + small_group.shape[0]) // 64) * 64 - big_rows
    small_group = jnp.pad(small_group, ((0, tail_rows - small_group.shape[0]), (0, 0)))
    joined = jnp.concatenate(
        [in_group.reshape(-1, 128), out_group.reshape(-1, 128), small_group], axis=0
    )
    joined = allreduce_rep(joined)
    split_at = in_group.size // 128
    split_out = split_at + out_group.size // 128
    in_owned = core_join(joined[:split_at].reshape(in_shape))[:, :cols]
    out_owned = core_join(joined[split_at:split_out].reshape(out_shape))
    mine = joined[split_out:].reshape(-1)[:small_len]
    small_final = []
    offset = 0
    for g in grads:
        size = g.size // groups
        small_final.append(mine[offset : offset + size].reshape((g.shape[0] // groups,) + g.shape[1:]))
        offset += size
    return (
        layer_out,
        input_grad,
        small_final[0],
        in_owned,
        small_final[1],
        small_final[2],
        small_final[3],
        small_final[4],
        small_final[5],
        small_final[6],
        out_owned,
    )


def solution(mesh):
    split = Mesh(
        mesh.devices.reshape(mesh.shape["rep"] // 2, 2, 4, 2),
        ("rep_hi", "core", "shard_0", "shard_1"),
    )
    in_specs = (
        P(REP_SHARD, None),
        P(REP_SHARD, None),
        P(REP_SHARD, None),
        P(SHARD),
        P(SHARD, None),
        P(SHARD, None),
        P(SHARD),
        P(SHARD),
        P(SHARD),
        P(SHARD),
        P(SHARD),
        P(SHARD, None),
    )
    out_specs = (
        P(REP_SHARD, None),
        P(REP_SHARD, None),
        P(SHARD),
        P(SHARD, None),
        P(SHARD, None),
        P(SHARD),
        P(SHARD),
        P(SHARD),
        P(SHARD),
        P(SHARD),
        P(SHARD, None),
    )
    return jax.shard_map(
        on_device, mesh=split, in_specs=in_specs, out_specs=out_specs, check_vma=False
    )
```
